512 devices in a mesh: group: 4 (over z_hi, core), shard: 128 (over x, z_lo, y).
Axes of the slice: x: 4, y: 8, z: 8 (z_hi: 2, z_lo: 4; z = z_hi * 4 + z_lo), core: 2. Of those that a mesh axis runs over, the one named last changes fastest.
Arguments:
- data: float32 [2, 524288], P(None, ('group', 'shard')), as said below
- inv_noise: bfloat16 [524288], P(('group', 'shard')), may hold values from 0.5 to 2
- mbh_amp: float32 [128, 6, 3, 512], P('shard', None, None, 'group'), may hold values from -0.15 to 0.15
- mbh_phase: float32 [128, 6, 3, 512], P('shard', None, None, 'group'), may hold values from -1024 to 1024
- bin_amp: float32 [512, 512], P(('group', 'shard')), may hold values from 0.15 to 0.4
- bin_phase: float32 [512, 512], P(('group', 'shard')), may hold values from -3.140625 to 3.140625
- bin_slope: float32 [512, 512], P(('group', 'shard')), may hold values from -3 to 3
- bin_curve: float32 [512, 512], P(('group', 'shard')), may hold values from -0.01 to 0.01
- bin_start: int32 [512, 512], P(('group', 'shard')), may hold values from 0 to 1023, as said below
- bin_count: int32 [512], P(('group', 'shard')), may hold values from 64 to 512, as said below
Outputs:
- accept_prob: float32 [64, 262144], P(None, ('group', 'shard'))
- residual_new: float32 [64, 2, 524288], P(None, None, ('group', 'shard'))
- noise_fit: float32 [512], P(('group', 'shard'))
The draws below stay inside these ranges and needn't reach their ends.
Inputs may be any that keep to these rules, and one draw needn't show every extreme that they name: data has a scale that varies from bin to bin and shrinks from the first band to the last. Slots p < bin_count[n] of band n are live, the others are empty; each band's count is 512, 256, 128 or 64, and some band holds 512. `bin_start`: in the last band every start is at most 896, so that no waveform passes the last bin; in every other band slot 0 starts from 960 to 992, so that its waveform passes into the next band.
All inputs are finite; a program needn't handle non-finite values.
Results may differ from the reference program's by a relative error of at most 0.0025.
The reference program's roundings to bfloat16 on the way count: a program that leaves them out, or rounds other values in their place, can miss the bound.
Values may be sent and summed in bfloat16 or wider, within the bound.
A program may use at most 64 MiB of HBM per device.

```python
import math
import jax
import jax.numpy as jnp
from jax import lax

BB = 1024
P_SIZE = 512
W = 64
H = 12
Q = 128
NCOEF = 8
NBANDS = 512
NBIN = 524288


def draw_data(key, part):
    key_scale, key_noise = jax.random.split(jax.random.fold_in(key, 11))
    band_of_bin = jnp.arange(NBIN, dtype=jnp.int32) // BB
    position = (2 * band_of_bin + 1).astype(jnp.float32) / NBANDS - 1.0
    trend = jnp.exp(-0.6 * position)
    scale = jnp.exp(jax.random.uniform(key_scale, (NBIN,), jnp.float32, jnp.log(0.3), jnp.log(3.0)))
    values = jax.random.normal(key_noise, (2, NBIN), jnp.float32)
    return values * (trend * scale)[None, :]


def draw_bin_start(key, part):
    key_main, key_top, key_band, key_slot, key_edge = jax.random.split(jax.random.fold_in(key, 23), 5)
    starts = jax.random.randint(key_main, (NBANDS, P_SIZE), 0, BB)
    edge_starts = jax.random.randint(key_edge, (NBANDS,), BB - Q // 2, BB - Q // 4 + 1)
    starts = starts.at[:, 0].set(edge_starts)
    last_row = jax.random.randint(key_top, (P_SIZE,), 0, BB - Q + 1)
    starts = starts.at[NBANDS - 1].set(last_row)
    chosen_band = jax.random.randint(key_band, (), 0, NBANDS - 1)
    chosen_slot = jax.random.randint(key_slot, (), 1, P_SIZE)
    return starts.at[chosen_band, chosen_slot].set(BB - 1).astype(jnp.int32)


def draw_bin_count(key, part):
    key_level, key_full = jax.random.split(jax.random.fold_in(key, 37))
    levels = jax.random.randint(key_level, (NBANDS,), 0, 4)
    counts = P_SIZE // jnp.left_shift(jnp.ones_like(levels), levels)
    chosen_band = jax.random.randint(key_full, (), 0, NBANDS)
    return counts.at[chosen_band].set(P_SIZE).astype(jnp.int32)


def shard_levels(rng, dims, shards, low, high):
    level, own = 1.0, jax.random.fold_in(rng, 6)
    for dim, parts in shards:
        draws = jnp.exp(jax.random.uniform(jax.random.fold_in(own, dim), (parts,), jnp.float32, low / len(shards), high / len(shards)))
        level = level * jnp.repeat(draws, dims[dim] // parts).reshape([-1 if axis == dim else 1 for axis in range(len(dims))])
    return level


def setup_inputs(seed: int = 0) -> dict:
    key_of = jax.random.split(jax.random.key(seed), 11)
    data = draw_data(jax.random.fold_in(key_of[10], 71), 0)
    inv_noise = jnp.clip(jnp.exp(math.log(2.0) - 1.3862944 * jax.random.uniform(key_of[1], (NBIN,), jnp.float32) ** shard_levels(key_of[1], (NBIN,), ((0, 512),), -0.2, 0.2)), 0.5, 2.0).astype(jnp.bfloat16)
    mbh_amp = jnp.clip(jax.random.uniform(key_of[2], (2 * W, H // 2, 3, NBANDS), jnp.float32, -0.15, 0.15) * shard_levels(key_of[2], (2 * W, H // 2, 3, NBANDS), ((0, 128), (3, 4)), -0.4, 0.0), -0.15, 0.15)
    mbh_phase = jnp.clip(jax.random.uniform(key_of[3], (2 * W, H // 2, 3, NBANDS), jnp.float32, -1024.0, 1024.0) * shard_levels(key_of[3], (2 * W, H // 2, 3, NBANDS), ((0, 128), (3, 4)), -0.4, 0.0), -1024.0, 1024.0)
    bin_amp = jnp.clip(jnp.exp(math.log(0.4) - 0.98082923 * jax.random.uniform(key_of[4], (NBANDS, P_SIZE), jnp.float32) ** shard_levels(key_of[4], (NBANDS, P_SIZE), ((0, 512),), -0.2, 0.2)), 0.15, 0.4)
    bin_phase = jnp.clip(jax.random.uniform(key_of[5], (NBANDS, P_SIZE), jnp.float32, -3.140625, 3.140625), -3.140625, 3.140625)
    bin_slope = jnp.clip(jax.random.uniform(key_of[6], (NBANDS, P_SIZE), jnp.float32, -3.0, 3.0) * shard_levels(key_of[6], (NBANDS, P_SIZE), ((0, 512),), -0.4, 0.0), -3.0, 3.0)
    bin_curve = jnp.clip(jax.random.uniform(key_of[7], (NBANDS, P_SIZE), jnp.float32, -0.01, 0.01) * shard_levels(key_of[7], (NBANDS, P_SIZE), ((0, 512),), -0.4, 0.0), -0.01, 0.01)
    bin_start = draw_bin_start(jax.random.fold_in(key_of[10], 71), 0)
    bin_count = draw_bin_count(jax.random.fold_in(key_of[10], 71), 0)
    return {"data": data, "inv_noise": inv_noise, "mbh_amp": mbh_amp, "mbh_phase": mbh_phase, "bin_amp": bin_amp, "bin_phase": bin_phase, "bin_slope": bin_slope, "bin_curve": bin_curve, "bin_start": bin_start, "bin_count": bin_count}


def half_templates(coef_amp, coef_phase, band_bins):
    fraction = jnp.arange(band_bins, dtype=jnp.float32) / band_bins
    amp_curve = coef_amp[:, :, 0, :, None] + coef_amp[:, :, 1, :, None] * fraction + coef_amp[:, :, 2, :, None] * fraction * fraction
    phase_curve = coef_phase[:, :, 0, :, None] + coef_phase[:, :, 1, :, None] * fraction + coef_phase[:, :, 2, :, None] * fraction * fraction
    real_part = jnp.sum(amp_curve * jnp.cos(phase_curve), axis=1)
    imag_part = jnp.sum(amp_curve * jnp.sin(phase_curve), axis=1)
    return jnp.stack([real_part, imag_part], axis=1).astype(jnp.bfloat16)

def make_wave(amplitude, phase_zero, slope, curvature, first_bin, slot_index, live_count, extent, window):
    offsets = jnp.arange(extent, dtype=jnp.int32)[None, :] - first_bin[:, None]
    inside = (offsets >= 0) & (offsets < window) & (slot_index < live_count)[:, None]
    shifted = offsets.astype(jnp.float32)
    envelope = jnp.sin(jnp.pi * (shifted + 0.5) / window) ** 2
    phase_angle = phase_zero[:, None] + slope[:, None] * shifted + curvature[:, None] * shifted * shifted
    real_part = jnp.where(inside, amplitude[:, None] * envelope * jnp.cos(phase_angle), 0.0)
    imag_part = jnp.where(inside, amplitude[:, None] * envelope * jnp.sin(phase_angle), 0.0)
    return jnp.stack([real_part, imag_part], axis=1).astype(jnp.bfloat16)

def chebyshev(position):
    terms = [jnp.ones_like(position), position]
    for degree in range(2, NCOEF):
        terms.append(2.0 * position * terms[-1] - terms[-2])
    return jnp.stack(terms[:NCOEF], axis=-1)

def cholesky_solve(gram, moment):
    lower = jnp.linalg.cholesky(gram)
    order_count = gram.shape[0]
    forward = []
    for row_index in range(order_count):
        partial_sum = moment[row_index]
        for col_index in range(row_index):
            partial_sum = partial_sum - lower[row_index, col_index] * forward[col_index]
        forward.append(partial_sum / lower[row_index, row_index])
    backward = [None] * order_count
    for row_index in reversed(range(order_count)):
        partial_sum = forward[row_index]
        for col_index in range(row_index + 1, order_count):
            partial_sum = partial_sum - lower[col_index, row_index] * backward[col_index]
        backward[row_index] = partial_sum / lower[row_index, row_index]
    return jnp.stack(backward)

def reference(data, inv_noise, mbh_amp, mbh_phase, bin_amp, bin_phase, bin_slope, bin_curve, bin_start, bin_count):

    def band_template(band_index):
        coef_amp = lax.dynamic_slice_in_dim(mbh_amp, band_index, 1, 3)
        coef_phase = lax.dynamic_slice_in_dim(mbh_phase, band_index, 1, 3)
        halves = half_templates(coef_amp, coef_phase, BB)[:, :, 0, :]
        return halves.reshape(W, 2, 2, BB).astype(jnp.float32).sum(axis=1)
    band_ids = jnp.arange(NBANDS, dtype=jnp.int32)
    template = lax.map(band_template, band_ids)
    template = template.transpose(1, 2, 0, 3).reshape(W, 2, NBIN)
    residual = data[None] - template
    weighted = (residual * inv_noise.astype(jnp.float32)[None, None, :]).astype(jnp.bfloat16)
    weighted_pad = jnp.concatenate([weighted, jnp.zeros((W, 2, Q), jnp.bfloat16)], axis=2)
    noise_pad = jnp.concatenate([inv_noise, jnp.zeros((Q,), jnp.bfloat16)], axis=0)
    slot_index = jnp.arange(P_SIZE, dtype=jnp.int32)

    def band_scores(band_index):
        offset = (band_index * BB).astype(jnp.int32)
        weighted_ext = lax.dynamic_slice_in_dim(weighted_pad, offset, BB + Q, 2)
        noise_ext = lax.dynamic_slice_in_dim(noise_pad, offset, BB + Q, 0).astype(jnp.float32)
        live_count = bin_count[band_index]
        wave = make_wave(bin_amp[band_index], bin_phase[band_index], bin_slope[band_index], bin_curve[band_index], bin_start[band_index], slot_index, live_count, BB + Q, Q)
        wave_flat = wave.reshape(P_SIZE, 2 * (BB + Q))
        correlation = jnp.dot(wave_flat.astype(jnp.float32), weighted_ext.reshape(W, 2 * (BB + Q)).T.astype(jnp.float32), preferred_element_type=jnp.float32)
        self_power = jnp.sum(wave.astype(jnp.float32) ** 2 * noise_ext[None, None, :], axis=(1, 2))
        live = slot_index < live_count
        accept = jnp.where(live[:, None], jax.nn.sigmoid(correlation - 0.5 * self_power[:, None]), 0.0)
        correction = jnp.dot(accept.astype(jnp.bfloat16).T.astype(jnp.float32), wave_flat.astype(jnp.float32), preferred_element_type=jnp.float32)
        return (accept.T, correction.reshape(W, 2, BB + Q))
    accept_all, correction_all = lax.map(band_scores, band_ids)
    accept_prob = accept_all.transpose(1, 0, 2).reshape(W, NBANDS * P_SIZE)
    own_part = correction_all[:, :, :, :BB].transpose(1, 2, 0, 3).reshape(W, 2, NBIN)
    rim_part = jnp.concatenate([correction_all[:, :, :, BB:], jnp.zeros((NBANDS, W, 2, BB - Q), jnp.float32)], axis=3)
    rim_part = jnp.concatenate([jnp.zeros((1, W, 2, BB), jnp.float32), rim_part[:-1]], axis=0)
    rim_part = rim_part.transpose(1, 2, 0, 3).reshape(W, 2, NBIN)
    residual_new = residual - own_part - rim_part
    squares = (residual_new * residual_new).reshape(W, 2, NBANDS, BB)
    log_power = jnp.log(jnp.mean(squares, axis=(0, 1, 3)) + 1e-06)
    position = (2 * band_ids + 1).astype(jnp.float32) / NBANDS - 1.0
    basis = chebyshev(position)
    gram = jnp.dot(basis.T, basis, precision=lax.Precision.HIGHEST)
    moment = jnp.dot(basis.T, log_power, precision=lax.Precision.HIGHEST)
    coef = cholesky_solve(gram, moment)
    noise_fit = jnp.dot(basis, coef, precision=lax.Precision.HIGHEST)
    return (accept_prob, residual_new, noise_fit)
```

```python
import jax
import jax.numpy as jnp
from jax import lax
from jax.experimental import pallas as pl
from jax.experimental.pallas import tpu as pltpu
from jax.sharding import Mesh
from jax.sharding import PartitionSpec as P

W = 64
HALF = 6
Q = 128
BINS = 1024
SLOTS = 512
NCOEF = 8
NX, NZ, NY = 4, 4, 8
NXZ = NX * NZ
NBANDS = 512
NBLK = BINS // Q
EXT = NBLK + 2
SHARD = ("shard_0", "shard_1", "shard_2")
GROUP_SHARD = ("group_0", "group_1", "shard_0", "shard_1", "shard_2")
GROUP = ("group_0", "group_1")
MESH = pl.DeviceIdType.MESH
F32 = jnp.float32
BF16 = jnp.bfloat16

INV_TURN = 0.15915494309189535
TURN_HI = 6.28125
TURN_LO = 0.0019353071795864769
MAGIC = 12582912.0
SIN_C = (4.44288283, -7.30824115, 3.60628896, -0.84576359, 0.10920575)
COS_C = (1.4142135, -6.97885099, 5.73946117, -1.88356298, 0.31069818)
COS6_C = (1.41421356, -6.97886411, 5.73988155, -1.888275, 0.33225188, -0.03450217)
SECTION = 40


def poly(coefs, square):
    total = coefs[-1] * square + coefs[-2]
    for c in coefs[-3::-1]:
        total = total * square + c
    return total


def nearest(t):
    return (t + MAGIC) - MAGIC


def sin_cos_halves(f):
    square = f * f
    return f * poly(SIN_C, square), poly(COS_C, square)


def chebyshev_rows(x, index):
    terms = [jnp.ones_like(x), x]
    for _ in range(2, NCOEF):
        terms.append(2.0 * x * terms[-1] - terms[-2])
    out = jnp.zeros_like(x)
    for k in range(NCOEF):
        out = jnp.where(index == k, terms[k], out)
    return out


def wave_tile(amp, phase, slope, curve, start, live):
    low = jnp.bitwise_and(start, Q - 1)
    row = lax.broadcasted_iota(jnp.int32, (Q, SLOTS), 0)
    j = jnp.bitwise_and(row - low, Q - 1)
    block = lax.shift_right_logical(start, 7) + (row < low).astype(jnp.int32)
    jf = j.astype(F32)
    angle = phase + slope * jf + curve * jf * jf
    turns = nearest(angle * INV_TURN)
    rest = (angle - turns * TURN_HI) - turns * TURN_LO
    s, c = sin_cos_halves(rest * INV_TURN)
    y = (jf + (0.5 - Q / 2)) * (1.0 / Q)
    half = poly(COS6_C, y * y)
    size = jnp.where(live, amp, 0.0) * (half * half * 0.5)
    re = size * (1.0 - s * s)
    im = size * (s * c)
    return re.astype(BF16).astype(F32), im.astype(BF16).astype(F32), block


def kernel(
    data_ref, noise_ref, amp_ref, phase_ref, bamp, bphase, bslope, bcurve, bstart, bcount,
    acc_out, res_out, fit_out,
    xm, m, s1, r1, a, ex, pk, fw, bk, bw, nz, wt, wp, res, ra, rb, zrow_ref,
    p1_send, p1_recv, p2_send, p2_recv, own_sem, ex_send, ex_recv, nb_send, nb_recv,
    ra_send, ra_recv, rb_send, rb_recv,
):
    zh, co = lax.axis_index("group_0"), lax.axis_index("group_1")
    x, z, y = lax.axis_index("shard_0"), lax.axis_index("shard_1"), lax.axis_index("shard_2")
    g = zh * 2 + co
    s = x * (NZ * NY) + z * NY + y
    n = g * (NBANDS // 4) + s
    xz = x * NZ + z
    ida = co * NY + y
    idb = (zh * NZ + z) * NX + x
    has_prev, has_next = n > 0, n < NBANDS - 1

    def device(group, xzi, yi):
        return {
            "group_0": group // 2, "group_1": group % 2,
            "shard_0": xzi // NZ, "shard_1": xzi % NZ, "shard_2": yi,
        }

    def band_device(band):
        r = band % (NBANDS // 4)
        return device(band // (NBANDS // 4), r // NY, r % NY)

    def peer_a(k):
        return {"group_1": k // NY, "shard_2": k % NY}

    def peer_b(k):
        return {"group_0": k // NXZ, "shard_1": (k // NX) % NZ, "shard_0": k % NX}

    barrier = pltpu.get_barrier_semaphore()

    def greet(where):
        pl.semaphore_signal(barrier, inc=1, device_id=where, device_id_type=MESH)

    for d in range(1, 32):
        greet(peer_b((idb + d) % 32))
    for d in range(1, 16):
        greet(peer_a((ida + d) % 16))

    @pl.when(has_prev)
    def _():
        greet(band_device(n - 1))

    @pl.when(has_next)
    def _():
        greet(band_device(n + 1))

    first, last = s == 0, s == NBANDS // 4 - 1

    @pl.when(first & (g > 0))
    def _():
        for k in range(NXZ):
            greet(device(g - 1, jnp.int32(k), jnp.int32(0)))

    @pl.when(last & (g < 3))
    def _():
        for k in range(NXZ):
            greet(device(g + 1, jnp.int32(k), jnp.int32(NY - 1)))

    up = (y == 0) & (g < 3)
    down = (y == NY - 1) & (g > 0)

    coef_rows = 3 * HALF
    amp_rows, phase_rows = amp_ref[...], phase_ref[...]
    xm[...] = jnp.zeros_like(xm)
    xm[0:coef_rows, :] = amp_rows
    xm[coef_rows:2 * coef_rows, :] = phase_rows
    own = xm[0:SECTION, :]
    xm[SECTION:2 * SECTION, :] = pltpu.roll(own, 1, 1)
    xm[2 * SECTION:3 * SECTION, :] = pltpu.roll(own, Q - 1, 1)
    m[...] = xm[...].T
    for k in range(NY):
        s1[k, :, 0, :] = m[pl.ds(k, NXZ, stride=NY), :]

    noise = noise_ref[...].astype(F32)
    pk[...] = jnp.zeros_like(pk)
    pk[0:1, :] = bamp[...]
    pk[1:2, :] = bphase[...]
    pk[2:3, :] = bslope[...]
    pk[3:4, :] = bcurve[...]
    pk[4:5, :] = bstart[...].astype(F32)
    pk[5:6, :] = jnp.full((1, SLOTS), bcount[0], jnp.int32).astype(F32)
    pk[6:7, 0:Q] = data_ref[0:1, BINS - Q:]
    pk[6:7, Q:2 * Q] = data_ref[1:2, BINS - Q:]
    pk[6:7, 2 * Q:3 * Q] = noise[:, BINS - Q:]
    bk[...] = jnp.zeros_like(bk)
    bk[0:2, :] = data_ref[:, 0:Q]
    bk[2:3, :] = noise[:, 0:Q]

    slot = lax.broadcasted_iota(jnp.int32, (1, SLOTS), 1)
    re_own, im_own, block_own = wave_tile(
        bamp[...], bphase[...], bslope[...], bcurve[...], bstart[...], slot < bcount[0]
    )
    for b in range(NBLK + 1):
        here = block_own == b
        wt[0, b * Q:(b + 1) * Q, :] = jnp.where(here, re_own, 0.0).astype(BF16)
        wt[1, b * Q:(b + 1) * Q, :] = jnp.where(here, im_own, 0.0).astype(BF16)

    waits = 15 + 31 + has_prev.astype(jnp.int32) + has_next.astype(jnp.int32)
    pl.semaphore_wait(barrier, waits + up.astype(jnp.int32) + down.astype(jnp.int32))

    def remote(src, dst, send, recv, where):
        return pltpu.make_async_remote_copy(
            src_ref=src, dst_ref=dst, send_sem=send, recv_sem=recv, device_id=where,
            device_id_type=MESH,
        )

    def p1(d):
        k = (y + d) % NY
        return remote(
            s1.at[k], r1.at[y % 2, y // 2], p1_send.at[d - 1], p1_recv.at[d - 1], {"shard_2": k}
        )

    for d in range(1, NY):
        p1(d).start()

    forward = remote(pk, fw, nb_send.at[0], nb_recv.at[0], band_device(n + 1))
    backward = remote(bk, bw, nb_send.at[1], nb_recv.at[1], band_device(n - 1))

    @pl.when(has_next)
    def _():
        forward.start()

    @pl.when(has_prev)
    def _():
        backward.start()

    r1[y % 2, y // 2] = s1[y]

    bands = lax.broadcasted_iota(jnp.int32, (NCOEF, NBANDS), 1)
    basis = chebyshev_rows(
        (2 * bands + 1).astype(F32) / NBANDS - 1.0,
        lax.broadcasted_iota(jnp.int32, (NCOEF, NBANDS), 0),
    )
    sub = lax.broadcasted_iota(jnp.int32, (NCOEF, Q), 0)
    lane8 = lax.broadcasted_iota(jnp.int32, (NCOEF, Q), 1)
    lane = lax.broadcasted_iota(jnp.int32, (1, Q), 1)
    position = (2 * jnp.full((NCOEF, Q), n, jnp.int32) + 1).astype(F32) / NBANDS - 1.0
    table = jnp.where(lane8 == NCOEF, chebyshev_rows(position, sub), 0.0)
    for k in range(NCOEF):
        column = jnp.sum(basis * basis[k:k + 1, :], axis=1, keepdims=True)
        table = jnp.where(lane8 == k, column, table)
    rows = []
    for k in range(NCOEF):
        root = jnp.sqrt(table[k:k + 1, k:k + 1])
        row = table[k:k + 1, :] / root
        column = table[:, k:k + 1] / root
        rows.append(row)
        table = jnp.where(sub > k, table - column * row, table)
    zrow = jnp.zeros((1, Q), F32)
    for k in reversed(range(NCOEF)):
        row = rows[k]
        known = jnp.sum(jnp.where((lane > k) & (lane < NCOEF), row * zrow, 0.0), axis=1, keepdims=True)
        value = (row[:, NCOEF:NCOEF + 1] - known) / row[:, k:k + 1]
        zrow = jnp.where(lane == k, value, zrow)
    zrow_ref[...] = zrow

    for d in range(1, NY):
        p1(d).wait_recv()

    def p2(d):
        k = (xz + d) % NXZ
        return remote(
            r1.at[:, :, k], a.at[:, pl.ds(xz * 4, 4)], p2_send.at[d - 1], p2_recv.at[d - 1],
            {"shard_0": k // NZ, "shard_1": k % NZ},
        )

    for d in range(1, NXZ):
        p2(d).start()
    own_copy = pltpu.make_async_copy(r1.at[:, :, xz], a.at[:, pl.ds(xz * 4, 4)], own_sem)
    own_copy.start()
    up_copy = remote(
        r1.at[:, :, 0], ex.at[:, pl.ds(xz * 4, 4)], ex_send.at[0], ex_recv.at[xz],
        device(g + 1, jnp.int32(0), jnp.int32(0)),
    )
    down_copy = remote(
        r1.at[:, :, NXZ - 1], ex.at[:, pl.ds(xz * 4, 4)], ex_send.at[1], ex_recv.at[xz],
        device(g - 1, jnp.int32(NXZ - 1), jnp.int32(NY - 1)),
    )

    @pl.when(up)
    def _():
        up_copy.start()

    @pl.when(down)
    def _():
        down_copy.start()

    @pl.when(has_prev)
    def _():
        forward.wait_recv()

    @pl.when(has_next)
    def _():
        backward.wait_recv()

    below = jnp.where(jnp.full((8, SLOTS), n, jnp.int32) > 0, fw[...], 0.0)
    above = jnp.where(jnp.full((8, Q), n, jnp.int32) < NBANDS - 1, bw[...], 0.0)
    re_prev, im_prev, block_prev = wave_tile(
        below[0:1], below[1:2], below[2:3], below[3:4], below[4:5].astype(jnp.int32),
        slot.astype(F32) < below[5:6],
    )
    for b in range(2):
        here = block_prev == NBLK - 1 + b
        wp[0, b * Q:(b + 1) * Q, :] = jnp.where(here, re_prev, 0.0).astype(BF16)
        wp[1, b * Q:(b + 1) * Q, :] = jnp.where(here, im_prev, 0.0).astype(BF16)

    nz[...] = jnp.zeros_like(nz)
    nz[0:1, :] = below[6:7, 2 * Q:3 * Q]
    for b in range(NBLK):
        nz[b + 1:b + 2, :] = noise[:, b * Q:(b + 1) * Q]
    nz[NBLK + 1:NBLK + 2, :] = above[2:3, :]
    noise_columns = nz[...].T
    power = re_own * re_own + im_own * im_own
    total = jnp.zeros((Q, SLOTS), F32)
    for b in range(NBLK + 1):
        total = jnp.where(block_own == b, noise_columns[:, b + 1:b + 2], total)
    self_power = jnp.sum(power * total, axis=0, keepdims=True)
    power_prev = re_prev * re_prev + im_prev * im_prev
    total_prev = jnp.where(
        block_prev == NBLK - 1, noise_columns[:, 0:1],
        jnp.where(block_prev == NBLK, noise_columns[:, 1:2], 0.0),
    )
    self_prev = jnp.sum(power_prev * total_prev, axis=0, keepdims=True)

    for d in range(1, NXZ):
        p2(d).wait_recv()
    own_copy.wait()

    edge = (first & (g > 0)) | (last & (g < 3))

    @pl.when(edge)
    def _():
        for k in range(NXZ):
            remote(
                r1.at[:, :, 0], ex.at[:, pl.ds(k * 4, 4)], ex_send.at[0], ex_recv.at[k],
                device(g, jnp.int32(0), jnp.int32(0)),
            ).wait_recv()

    lane_q = lax.broadcasted_iota(jnp.int32, (8, Q), 1)
    take_prev = jnp.full((8, Q), (first & (g > 0)).astype(jnp.int32), jnp.int32)
    take_next = jnp.full((8, Q), (last & (g < 3)).astype(jnp.int32), jnp.int32)
    take = ((take_prev > 0) & (lane_q >= SECTION) & (lane_q < 2 * SECTION)) | (
        (take_next > 0) & (lane_q >= 2 * SECTION)
    )
    below_data = (below[6:7, 0:Q], below[6:7, Q:2 * Q])

    def template_rows(step, carry):
        at = pl.multiple_of(step * 8, 8)
        sums = {}
        for half in range(2):
            tile = a[half, pl.ds(at, 8), 0, :]
            tile = jnp.where(take, ex[half, pl.ds(at, 8), 0, :], tile)
            turns_tile = tile * INV_TURN
            pieces = [(1, BINS - Q, 0)] + [(0, 256 * c, 1 + 2 * c) for c in range(4)]
            for section, offset, block in pieces + [(2, 0, NBLK + 1)]:
                width = 256 if section == 0 else Q
                u = (
                    lax.broadcasted_iota(jnp.int32, (1, width), 1).astype(F32) + offset
                ) * (1.0 / BINS)
                base = section * SECTION
                lost = amp_sum = im = None
                for h in range(HALF):
                    a0, a1, a2 = (tile[:, base + 3 * h + i:base + 3 * h + i + 1] for i in range(3))
                    q = base + coef_rows + 3 * h
                    p0, p1_, p2_ = (turns_tile[:, q + i:q + i + 1] for i in range(3))
                    t = p0 + u * (p1_ + u * p2_)
                    f = t - nearest(t)
                    sn, cs = sin_cos_halves(f)
                    amp = a0 + u * (a1 + u * a2)
                    asn = amp * sn
                    if h == 0:
                        amp_sum, lost, im = amp, asn * sn, asn * cs
                    else:
                        amp_sum, lost, im = amp_sum + amp, lost + asn * sn, im + asn * cs
                parts = (
                    (amp_sum - lost).astype(BF16).astype(F32),
                    im.astype(BF16).astype(F32),
                )
                if half == 0:
                    sums[block] = parts
                    continue
                for part in range(2):
                    template = sums[block][part] + parts[part]
                    if section == 0:
                        d = data_ref[part:part + 1, offset:offset + width]
                    elif section == 1:
                        d = below_data[part]
                    else:
                        d = above[part:part + 1, :]
                    res[part, pl.ds(at, 8), block * Q:block * Q + width] = d - template
        return carry

    lax.fori_loop(0, W // 8, template_rows, 0)

    noise_ext = jnp.concatenate([nz[0:1, :], noise, nz[NBLK + 1:NBLK + 2, :]], axis=1)
    corr = jnp.zeros((W, SLOTS), F32)
    corr_prev = jnp.zeros((W, SLOTS), F32)
    for part in range(2):
        weighted = (res[part] * noise_ext).astype(BF16)
        corr += jnp.dot(weighted[:, Q:], wt[part], preferred_element_type=F32)
        corr_prev += jnp.dot(weighted[:, 0:2 * Q], wp[part], preferred_element_type=F32)

    def sigmoid(v):
        return 1.0 / (1.0 + jnp.exp(-v))

    accept = jnp.where(slot < bcount[0], sigmoid(corr - 0.5 * self_power), 0.0)
    acc_out[...] = accept
    accept = accept.astype(BF16)
    accept_prev = sigmoid(corr_prev - 0.5 * self_prev).astype(BF16)
    square = jnp.zeros((1, BINS), F32)
    nt = (((1,), (1,)), ((), ()))
    for part in range(2):
        change = lax.dot_general(accept, wt[part, 0:BINS, :], nt, preferred_element_type=F32)
        rim = lax.dot_general(accept_prev, wp[part, Q:2 * Q, :], nt, preferred_element_type=F32)
        new = res[part, :, Q:Q + BINS] - change
        new = jnp.concatenate([new[:, 0:Q] - rim, new[:, Q:]], axis=1)
        res_out[part] = new
        square += jnp.sum(new * new, axis=0, keepdims=True)
    mean = jnp.sum(square, axis=1, keepdims=True) * (1.0 / (2 * W * BINS))
    log_power = jnp.log(mean + 1e-06)
    mine = chebyshev_rows((2 * jnp.full((1, Q), n, jnp.int32) + 1).astype(F32) / NBANDS - 1.0, lane)
    ra[ida] = mine * log_power

    def stage(buf, me, peers, send, recv, where):
        def copy(d):
            k = (me + d) % peers
            return remote(buf.at[me], buf.at[me], send.at[d - 1], recv.at[d - 1], where(k))

        for d in range(1, peers):
            copy(d).start()
        for d in range(1, peers):
            copy(d).wait_recv()
        return copy

    sent_a = stage(ra, ida, 16, ra_send, ra_recv, peer_a)
    rb[idb] = jnp.sum(ra[...], axis=0)
    sent_b = stage(rb, idb, 32, rb_send, rb_recv, peer_b)
    moment = jnp.sum(rb[...], axis=0)
    fit_out[0] = jnp.sum(zrow_ref[...] * moment)

    for d in range(1, NY):
        p1(d).wait_send()
    for d in range(1, NXZ):
        p2(d).wait_send()
    for d in range(1, 16):
        sent_a(d).wait_send()
    for d in range(1, 32):
        sent_b(d).wait_send()

    @pl.when(has_next)
    def _():
        forward.wait_send()

    @pl.when(has_prev)
    def _():
        backward.wait_send()

    @pl.when(up)
    def _():
        up_copy.wait_send()

    @pl.when(down)
    def _():
        down_copy.wait_send()


def local(data, inv_noise, mbh_amp, mbh_phase, bin_amp, bin_phase, bin_slope, bin_curve, bin_start, bin_count):
    vmem = pl.BlockSpec(memory_space=pltpu.VMEM)
    smem = pl.BlockSpec(memory_space=pltpu.SMEM)
    dma = pltpu.SemaphoreType.DMA
    rows = 3 * HALF
    accept, residual, fit = pl.pallas_call(
        kernel,
        out_shape=(
            jax.ShapeDtypeStruct((W, SLOTS), F32),
            jax.ShapeDtypeStruct((2, W, BINS), F32),
            jax.ShapeDtypeStruct((1,), F32),
        ),
        in_specs=[vmem] * 9 + [smem],
        out_specs=(vmem, vmem, smem),
        scratch_shapes=[
            pltpu.VMEM((Q, Q), F32),
            pltpu.VMEM((Q, Q), F32),
            pltpu.VMEM((NY, NXZ, 1, Q), F32),
            pltpu.VMEM((2, NY // 2, NXZ, 1, Q), F32),
            pltpu.VMEM((2, W, 1, Q), F32),
            pltpu.VMEM((2, W, 1, Q), F32),
            pltpu.VMEM((8, SLOTS), F32),
            pltpu.VMEM((8, SLOTS), F32),
            pltpu.VMEM((8, Q), F32),
            pltpu.VMEM((8, Q), F32),
            pltpu.VMEM((16, Q), F32),
            pltpu.VMEM((2, (NBLK + 1) * Q, SLOTS), BF16),
            pltpu.VMEM((2, 2 * Q, SLOTS), BF16),
            pltpu.VMEM((2, W, EXT * Q), F32),
            pltpu.VMEM((16, 1, Q), F32),
            pltpu.VMEM((32, 1, Q), F32),
            pltpu.VMEM((1, Q), F32),
            dma((NY - 1,)), dma((NY - 1,)),
            dma((NXZ - 1,)), dma((NXZ - 1,)),
            dma,
            dma((2,)), dma((NXZ,)),
            dma((2,)), dma((2,)),
            dma((15,)), dma((15,)),
            dma((31,)), dma((31,)),
        ],
        compiler_params=pltpu.CompilerParams(
            collective_id=0, has_side_effects=True, vmem_limit_bytes=48 * 1024 * 1024
        ),
        name="gibbs_round",
    )(
        data,
        inv_noise.reshape(1, BINS),
        mbh_amp.reshape(rows, Q),
        mbh_phase.reshape(rows, Q),
        bin_amp, bin_phase, bin_slope, bin_curve, bin_start, bin_count,
    )
    return accept, residual.transpose(1, 0, 2), fit


def solution(mesh):
    split = Mesh(mesh.devices.reshape(2, 2, NX, NZ, NY), GROUP_SHARD)
    return jax.shard_map(
        local,
        mesh=split,
        in_specs=(
            P(None, GROUP_SHARD),
            P(GROUP_SHARD),
            P(SHARD, None, None, GROUP),
            P(SHARD, None, None, GROUP),
            P(GROUP_SHARD, None),
            P(GROUP_SHARD, None),
            P(GROUP_SHARD, None),
            P(GROUP_SHARD, None),
            P(GROUP_SHARD, None),
            P(GROUP_SHARD),
        ),
        out_specs=(P(None, GROUP_SHARD), P(None, None, GROUP_SHARD), P(GROUP_SHARD)),
        check_vma=False,
    )
```

```python
import jax
import jax.numpy as jnp
from jax import lax
from jax.experimental import pallas as pl
from jax.experimental.pallas import tpu as pltpu
from jax.sharding import Mesh
from jax.sharding import PartitionSpec as P

W = 64
HALF = 6
Q = 128
BINS = 1024
SLOTS = 512
NCOEF = 8
NX, NZ, NY = 4, 4, 8
NXZ = NX * NZ
NBANDS = 512
NBLK = BINS // Q
EXT = NBLK + 2
SHARD = ("shard_0", "shard_1", "shard_2")
GROUP_SHARD = ("group_0", "group_1", "shard_0", "shard_1", "shard_2")
GROUP = ("group_0", "group_1")
MESH = pl.DeviceIdType.MESH
F32 = jnp.float32
BF16 = jnp.bfloat16

INV_TURN = 0.15915494309189535
TURN_HI = 6.28125
TURN_LO = 0.0019353071795864769
MAGIC = 12582912.0
SIN_C = (4.44288283, -7.30824115, 3.60628896, -0.84576359, 0.10920575)
COS_C = (1.4142135, -6.97885099, 5.73946117, -1.88356298, 0.31069818)
COS6_C = (1.41421356, -6.97886411, 5.73988155, -1.888275, 0.33225188, -0.03450217)
SECTION = 40
FAR = (4, 3, 5, 2, 6, 1, 7, 0)
PLANE = ((2, 2), (2, 1), (1, 2), (2, 3), (3, 2), (1, 1), (1, 3), (3, 1), (3, 3),
         (0, 2), (2, 0), (0, 1), (0, 3), (1, 0), (3, 0), (0, 0))


def poly(coefs, square):
    total = coefs[-1] * square + coefs[-2]
    for c in coefs[-3::-1]:
        total = total * square + c
    return total


def nearest(t):
    return (t + MAGIC) - MAGIC


def sin_cos_halves(f):
    square = f * f
    return f * poly(SIN_C, square), poly(COS_C, square)


def chebyshev_rows(x, index):
    terms = [jnp.ones_like(x), x]
    for _ in range(2, NCOEF):
        terms.append(2.0 * x * terms[-1] - terms[-2])
    out = jnp.zeros_like(x)
    for k in range(NCOEF):
        out = jnp.where(index == k, terms[k], out)
    return out


def wave_tile(amp, phase, slope, curve, start, live):
    low = jnp.bitwise_and(start, Q - 1)
    row = lax.broadcasted_iota(jnp.int32, (Q, SLOTS), 0)
    j = jnp.bitwise_and(row - low, Q - 1)
    block = lax.shift_right_logical(start, 7) + (row < low).astype(jnp.int32)
    jf = j.astype(F32)
    angle = phase + slope * jf + curve * jf * jf
    turns = nearest(angle * INV_TURN)
    rest = (angle - turns * TURN_HI) - turns * TURN_LO
    s, c = sin_cos_halves(rest * INV_TURN)
    y = (jf + (0.5 - Q / 2)) * (1.0 / Q)
    half = poly(COS6_C, y * y)
    size = jnp.where(live, amp, 0.0) * (half * half * 0.5)
    re = size * (1.0 - s * s)
    im = size * (s * c)
    return re.astype(BF16).astype(F32), im.astype(BF16).astype(F32), block


def wrapped(v, n):
    return jnp.where(v >= n, v - n, v)


def kernel(
    data_hbm, noise_hbm, amp_hbm, phase_hbm, bamp_hbm, bphase_hbm, bslope_hbm, bcurve_hbm,
    bstart_hbm, bcount,
    acc_out, res_out, fit_out,
    data_ref, noise_ref, bamp, bphase, bslope, bcurve, bstart,
    xm, m, s1, r1, a, ex, pk, fw, bk, bw, nz, wt, wp, res, ra, rb, zrow_ref,
    in_sem, p1_send, p1_recv, p2_send, p2_recv, own_sem, ex_send, ex_recv, nb_send, nb_recv,
    ra_send, ra_recv, rb_send, rb_recv,
):
    coef_rows = 3 * HALF
    inputs = [
        (amp_hbm, xm.at[0:coef_rows]), (phase_hbm, xm.at[coef_rows:2 * coef_rows]),
        (data_hbm, data_ref), (noise_hbm, noise_ref), (bamp_hbm, bamp), (bphase_hbm, bphase),
        (bslope_hbm, bslope), (bcurve_hbm, bcurve), (bstart_hbm, bstart),
    ]
    fetches = [
        pltpu.make_async_copy(src, dst, in_sem.at[i]) for i, (src, dst) in enumerate(inputs)
    ]
    for fetch in fetches:
        fetch.start()

    zh, co = lax.axis_index("group_0"), lax.axis_index("group_1")
    x, z, y = lax.axis_index("shard_0"), lax.axis_index("shard_1"), lax.axis_index("shard_2")
    g = zh * 2 + co
    s = x * (NZ * NY) + z * NY + y
    n = g * (NBANDS // 4) + s
    xz = x * NZ + z
    ida = co * NY + y
    idb = zh * NXZ + xz
    has_prev, has_next = n > 0, n < NBANDS - 1
    first, last = s == 0, s == NBANDS // 4 - 1
    up = (y == 0) & (g < 3)
    down = (y == NY - 1) & (g > 0)

    def at(group0, group1, xi, zi, yi):
        return {
            "group_0": group0, "group_1": group1, "shard_0": xi, "shard_1": zi, "shard_2": yi,
        }

    turn_y = y == NY - 1
    turn_z = turn_y & (z == NZ - 1)
    turn_x = turn_z & (x == NX - 1)
    turn_c = turn_x & (co == 1)
    above_id = at(
        jnp.where(turn_c, 1 - zh, zh), jnp.where(turn_x, 1 - co, co),
        jnp.where(turn_z, wrapped(x + 1, NX), x), jnp.where(turn_y, wrapped(z + 1, NZ), z),
        wrapped(y + 1, NY),
    )
    back_y = y == 0
    back_z = back_y & (z == 0)
    back_x = back_z & (x == 0)
    back_c = back_x & (co == 0)
    below_id = at(
        jnp.where(back_c, 1 - zh, zh), jnp.where(back_x, 1 - co, co),
        jnp.where(back_z, wrapped(x + NX - 1, NX), x),
        jnp.where(back_y, wrapped(z + NZ - 1, NZ), z),
        wrapped(y + NY - 1, NY),
    )
    next_zh, next_co = jnp.where(co == 1, 1 - zh, zh), 1 - co
    prev_zh, prev_co = jnp.where(co == 0, 1 - zh, zh), 1 - co

    barrier = pltpu.get_barrier_semaphore()

    def greet(where):
        pl.semaphore_signal(barrier, inc=1, device_id=where, device_id_type=MESH)

    def peer_y(dc, dy):
        return {"group_1": 1 - co if dc else co, "shard_2": wrapped(y + dy, NY)}

    def peer_plane(dh, dx, dz):
        return {
            "group_0": 1 - zh if dh else zh,
            "shard_0": wrapped(x + dx, NX), "shard_1": wrapped(z + dz, NZ),
        }

    members_a = [(dc, dy) for dy in FAR for dc in (1, 0) if (dc, dy) != (0, 0)]
    members_b = [(dh, dx, dz) for dx, dz in PLANE for dh in (1, 0) if (dh, dx, dz) != (0, 0, 0)]

    @pl.when(first & (g > 0))
    def _():
        for k in range(NXZ):
            greet(at(prev_zh, prev_co, k // NZ, k % NZ, 0))

    @pl.when(last & (g < 3))
    def _():
        for k in range(NXZ):
            greet(at(next_zh, next_co, k // NZ, k % NZ, NY - 1))

    for member in members_b:
        greet(peer_plane(*member))
    for member in members_a:
        greet(peer_y(*member))

    @pl.when(has_prev)
    def _():
        greet(below_id)

    @pl.when(has_next)
    def _():
        greet(above_id)

    xm[2 * coef_rows:SECTION] = jnp.zeros((SECTION - 2 * coef_rows, 1, Q), F32)
    for fetch in fetches:
        fetch.wait()
    own = xm[:, 0, :]
    m[...] = jnp.concatenate(
        [own, pltpu.roll(own, 1, 1), pltpu.roll(own, Q - 1, 1), jnp.zeros((8, Q), F32)], axis=0
    ).T
    for k in range(NY):
        s1[k, :, 0, :] = m[pl.ds(k, NXZ, stride=NY), :]

    noise8 = noise_ref[...].astype(F32)
    noise = jnp.concatenate([noise8[b:b + 1, :] for b in range(NBLK)], axis=1)
    pk[...] = jnp.zeros_like(pk)
    pk[0:1, :] = bamp[...]
    pk[1:2, :] = bphase[...]
    pk[2:3, :] = bslope[...]
    pk[3:4, :] = bcurve[...]
    pk[4:5, :] = bstart[...].astype(F32)
    pk[5:6, :] = jnp.full((1, SLOTS), bcount[0], jnp.int32).astype(F32)
    pk[6:7, 0:Q] = data_ref[0:1, BINS - Q:]
    pk[6:7, Q:2 * Q] = data_ref[1:2, BINS - Q:]
    pk[6:7, 2 * Q:3 * Q] = noise8[NBLK - 1:NBLK, :]
    bk[...] = jnp.zeros_like(bk)
    bk[0:2, :] = data_ref[:, 0:Q]
    bk[2:3, :] = noise8[0:1, :]

    slot = lax.broadcasted_iota(jnp.int32, (1, SLOTS), 1)
    re_own, im_own, block_own = wave_tile(
        bamp[...], bphase[...], bslope[...], bcurve[...], bstart[...], slot < bcount[0]
    )
    for b in range(NBLK + 1):
        here = block_own == b
        wt[0, b * Q:(b + 1) * Q, :] = jnp.where(here, re_own, 0.0).astype(BF16)
        wt[1, b * Q:(b + 1) * Q, :] = jnp.where(here, im_own, 0.0).astype(BF16)

    waits = 15 + 31 + has_prev.astype(jnp.int32) + has_next.astype(jnp.int32)
    pl.semaphore_wait(barrier, waits + up.astype(jnp.int32) + down.astype(jnp.int32))

    def remote(src, dst, send, recv, where):
        return pltpu.make_async_remote_copy(
            src_ref=src, dst_ref=dst, send_sem=send, recv_sem=recv, device_id=where,
            device_id_type=MESH,
        )

    slot_y = (y % 2) * (NY // 2) + y // 2

    def p1(dy):
        k = wrapped(y + dy, NY)
        return remote(
            s1.at[k], r1.at[slot_y], p1_send.at[dy - 1], p1_recv.at[dy - 1], {"shard_2": k}
        )

    for dy in FAR[:-1]:
        p1(dy).start()

    forward = remote(pk, fw, nb_send.at[0], nb_recv.at[0], above_id)
    backward = remote(bk, bw, nb_send.at[1], nb_recv.at[1], below_id)

    @pl.when(has_next)
    def _():
        forward.start()

    @pl.when(has_prev)
    def _():
        backward.start()

    r1[slot_y] = s1[y]

    bands = lax.broadcasted_iota(jnp.int32, (NCOEF, NBANDS), 1)
    basis = chebyshev_rows(
        (2 * bands + 1).astype(F32) / NBANDS - 1.0,
        lax.broadcasted_iota(jnp.int32, (NCOEF, NBANDS), 0),
    )
    sub = lax.broadcasted_iota(jnp.int32, (NCOEF, Q), 0)
    lane8 = lax.broadcasted_iota(jnp.int32, (NCOEF, Q), 1)
    lane = lax.broadcasted_iota(jnp.int32, (1, Q), 1)
    position = (2 * jnp.full((NCOEF, Q), n, jnp.int32) + 1).astype(F32) / NBANDS - 1.0
    table = jnp.where(lane8 == NCOEF, chebyshev_rows(position, sub), 0.0)
    for k in range(NCOEF):
        column = jnp.sum(basis * basis[k:k + 1, :], axis=1, keepdims=True)
        table = jnp.where(lane8 == k, column, table)
    rows = []
    for k in range(NCOEF):
        root = jnp.sqrt(table[k:k + 1, k:k + 1])
        row = table[k:k + 1, :] / root
        column = table[:, k:k + 1] / root
        rows.append(row)
        table = jnp.where(sub > k, table - column * row, table)
    zrow = jnp.zeros((1, Q), F32)
    for k in reversed(range(NCOEF)):
        row = rows[k]
        known = jnp.sum(jnp.where((lane > k) & (lane < NCOEF), row * zrow, 0.0), axis=1, keepdims=True)
        value = (row[:, NCOEF:NCOEF + 1] - known) / row[:, k:k + 1]
        zrow = jnp.where(lane == k, value, zrow)
    zrow_ref[...] = zrow

    for dy in FAR[:-1]:
        p1(dy).wait_recv()

    up_copy = remote(
        r1.at[:, 0], ex.at[xz], ex_send.at[0], ex_recv.at[xz], at(next_zh, next_co, 0, 0, 0)
    )
    down_copy = remote(
        r1.at[:, NXZ - 1], ex.at[xz], ex_send.at[1], ex_recv.at[xz],
        at(prev_zh, prev_co, NX - 1, NZ - 1, NY - 1),
    )

    @pl.when(up)
    def _():
        up_copy.start()

    @pl.when(down)
    def _():
        down_copy.start()

    def p2(dx, dz):
        xk, zk = wrapped(x + dx, NX), wrapped(z + dz, NZ)
        d = dx * NZ + dz
        return remote(
            r1.at[:, xk * NZ + zk], a.at[xz], p2_send.at[d], p2_recv.at[d],
            {"shard_0": xk, "shard_1": zk},
        )

    for dx, dz in PLANE[:-1]:
        p2(dx, dz).start()
    a[xz] = r1[:, xz]

    @pl.when(has_prev)
    def _():
        forward.wait_recv()

    @pl.when(has_next)
    def _():
        backward.wait_recv()

    below = jnp.where(jnp.full((8, SLOTS), n, jnp.int32) > 0, fw[...], 0.0)
    above = jnp.where(jnp.full((8, Q), n, jnp.int32) < NBANDS - 1, bw[...], 0.0)
    re_prev, im_prev, block_prev = wave_tile(
        below[0:1], below[1:2], below[2:3], below[3:4], below[4:5].astype(jnp.int32),
        slot.astype(F32) < below[5:6],
    )
    for b in range(2):
        here = block_prev == NBLK - 1 + b
        wp[0, b * Q:(b + 1) * Q, :] = jnp.where(here, re_prev, 0.0).astype(BF16)
        wp[1, b * Q:(b + 1) * Q, :] = jnp.where(here, im_prev, 0.0).astype(BF16)

    nz[...] = jnp.zeros_like(nz)
    nz[0:1, :] = below[6:7, 2 * Q:3 * Q]
    nz[1:NBLK + 1, :] = noise8
    nz[NBLK + 1:NBLK + 2, :] = above[2:3, :]
    noise_columns = nz[...].T
    power = re_own * re_own + im_own * im_own
    total = jnp.zeros((Q, SLOTS), F32)
    for b in range(NBLK + 1):
        total = jnp.where(block_own == b, noise_columns[:, b + 1:b + 2], total)
    self_power = jnp.sum(power * total, axis=0, keepdims=True)
    power_prev = re_prev * re_prev + im_prev * im_prev
    total_prev = jnp.where(
        block_prev == NBLK - 1, noise_columns[:, 0:1],
        jnp.where(block_prev == NBLK, noise_columns[:, 1:2], 0.0),
    )
    self_prev = jnp.sum(power_prev * total_prev, axis=0, keepdims=True)

    edge_first, edge_last = first & (g > 0), last & (g < 3)
    edge = edge_first | edge_last
    lane_q = lax.broadcasted_iota(jnp.int32, (8, Q), 1)
    take_prev = jnp.full((8, Q), edge_first.astype(jnp.int32), jnp.int32)
    take_next = jnp.full((8, Q), edge_last.astype(jnp.int32), jnp.int32)
    take = ((take_prev > 0) & (lane_q >= SECTION) & (lane_q < 2 * SECTION)) | (
        (take_next > 0) & (lane_q >= 2 * SECTION)
    )
    below_data = (below[6:7, 0:Q], below[6:7, Q:2 * Q])

    def template_rows(step, carry):
        quarter = step // NZ
        dx = jnp.where(quarter >= 2, 5 - quarter, quarter)
        dz = step % NZ
        xk, zk = wrapped(x + NX - dx, NX), wrapped(z + NZ - dz, NZ)
        k = xk * NZ + zk
        d = dx * NZ + dz

        @pl.when(step > 0)
        def _():
            remote(
                r1.at[:, 0], a.at[k], p2_send.at[d], p2_recv.at[d],
                {"shard_0": xk, "shard_1": zk},
            ).wait_recv()

        @pl.when(edge)
        def _():
            remote(
                r1.at[:, 0], ex.at[k], ex_send.at[0], ex_recv.at[k], at(zh, co, 0, 0, 0)
            ).wait_recv()

        tile = jnp.where(take, ex[k, :, 0, :], a[k, :, 0, :])
        turns_tile = tile * INV_TURN
        pieces = [(1, BINS - Q, 0)] + [(0, 512 * c, 1 + 4 * c) for c in range(2)]
        for section, offset, block in pieces + [(2, 0, NBLK + 1)]:
            width = 512 if section == 0 else Q
            u = (
                lax.broadcasted_iota(jnp.int32, (1, width), 1).astype(F32) + offset
            ) * (1.0 / BINS)
            base = section * SECTION
            lost = amp_sum = im = None
            for h in range(HALF):
                a0, a1, a2 = (tile[:, base + 3 * h + i:base + 3 * h + i + 1] for i in range(3))
                q = base + coef_rows + 3 * h
                p0, p1_, p2_ = (turns_tile[:, q + i:q + i + 1] for i in range(3))
                t = p0 + u * (p1_ + u * p2_)
                f = t - nearest(t)
                sn, cs = sin_cos_halves(f)
                amp = a0 + u * (a1 + u * a2)
                asn = amp * sn
                if h == 0:
                    amp_sum, lost, im = amp, asn * sn, asn * cs
                else:
                    amp_sum, lost, im = amp_sum + amp, lost + asn * sn, im + asn * cs
            for part, half in enumerate((amp_sum - lost, im)):
                half = half.astype(BF16).astype(F32)
                template = half + pltpu.roll(half, 4, 0)
                if section == 0:
                    values = data_ref[part:part + 1, offset:offset + width]
                elif section == 1:
                    values = below_data[part]
                else:
                    values = above[part:part + 1, :]
                res[part, k, :, block * Q:block * Q + width] = values - template
        return carry

    lax.fori_loop(0, NXZ, template_rows, 0)

    noise_ext = jnp.concatenate([nz[0:1, :], noise, nz[NBLK + 1:NBLK + 2, :]], axis=1)
    corr = jnp.zeros((W, SLOTS), F32)
    corr_prev = jnp.zeros((W, SLOTS), F32)
    upper = lax.broadcasted_iota(jnp.int32, (NXZ // 2, 8, EXT * Q), 1) < 4

    def residual(part):
        pairs = res[part].reshape(NXZ // 2, 2, 8, EXT * Q)
        return jnp.where(upper, pairs[:, 0], pairs[:, 1]).reshape(W, EXT * Q)

    residuals = [residual(part) for part in range(2)]
    for part in range(2):
        weighted = (residuals[part] * noise_ext).astype(BF16)
        corr += jnp.dot(weighted[:, Q:], wt[part], preferred_element_type=F32)
        corr_prev += jnp.dot(weighted[:, 0:2 * Q], wp[part], preferred_element_type=F32)

    def sigmoid(v):
        return 1.0 / (1.0 + jnp.exp(-v))

    accept = jnp.where(slot < bcount[0], sigmoid(corr - 0.5 * self_power), 0.0)
    acc_out[...] = accept
    accept = accept.astype(BF16)
    accept_prev = sigmoid(corr_prev - 0.5 * self_prev).astype(BF16)
    square = jnp.zeros((1, BINS), F32)
    nt = (((1,), (1,)), ((), ()))
    for part in range(2):
        change = lax.dot_general(accept, wt[part, 0:BINS, :], nt, preferred_element_type=F32)
        rim = lax.dot_general(accept_prev, wp[part, Q:2 * Q, :], nt, preferred_element_type=F32)
        new = residuals[part][:, Q:Q + BINS] - change
        new = jnp.concatenate([new[:, 0:Q] - rim, new[:, Q:]], axis=1)
        res_out[part] = new
        square += jnp.sum(new * new, axis=0, keepdims=True)
    mean = jnp.sum(square, axis=1, keepdims=True) * (1.0 / (2 * W * BINS))
    log_power = jnp.log(mean + 1e-06)
    mine = chebyshev_rows((2 * jnp.full((1, Q), n, jnp.int32) + 1).astype(F32) / NBANDS - 1.0, lane)
    ra[ida] = mine * log_power

    def sum_a(dc, dy):
        d = dc * NY + dy
        return remote(ra.at[ida], ra.at[ida], ra_send.at[d], ra_recv.at[d], peer_y(dc, dy))

    def sum_b(dh, dx, dz):
        d = (dh * NX + dx) * NZ + dz
        return remote(rb.at[idb], rb.at[idb], rb_send.at[d], rb_recv.at[d], peer_plane(dh, dx, dz))

    for member in members_a:
        sum_a(*member).start()
    for dy in FAR[:-1]:
        p1(dy).wait_send()
    for dx, dz in PLANE[:-1]:
        p2(dx, dz).wait_send()

    @pl.when(has_next)
    def _():
        forward.wait_send()

    @pl.when(has_prev)
    def _():
        backward.wait_send()

    @pl.when(up)
    def _():
        up_copy.wait_send()

    @pl.when(down)
    def _():
        down_copy.wait_send()

    for member in members_a:
        sum_a(*member).wait_recv()
    rb[idb] = jnp.sum(ra[...], axis=0)
    for member in members_b:
        sum_b(*member).start()
    for member in members_a:
        sum_a(*member).wait_send()
    for member in members_b:
        sum_b(*member).wait_recv()
    moment = jnp.sum(rb[...], axis=0)
    fit_out[0] = jnp.sum(zrow_ref[...] * moment)
    for member in members_b:
        sum_b(*member).wait_send()


def local(data, inv_noise, mbh_amp, mbh_phase, bin_amp, bin_phase, bin_slope, bin_curve, bin_start, bin_count):
    vmem = pl.BlockSpec(memory_space=pltpu.VMEM)
    smem = pl.BlockSpec(memory_space=pltpu.SMEM)
    dma = pltpu.SemaphoreType.DMA
    rows = 3 * HALF
    accept, residual, fit = pl.pallas_call(
        kernel,
        out_shape=(
            jax.ShapeDtypeStruct((W, SLOTS), F32),
            jax.ShapeDtypeStruct((2, W, BINS), F32),
            jax.ShapeDtypeStruct((1,), F32),
        ),
        in_specs=[pl.BlockSpec(memory_space=pltpu.HBM)] * 9 + [smem],
        out_specs=(vmem, vmem, smem),
        scratch_shapes=[
            pltpu.VMEM((2, BINS), F32),
            pltpu.VMEM((NBLK, Q), BF16),
            pltpu.VMEM((1, SLOTS), F32),
            pltpu.VMEM((1, SLOTS), F32),
            pltpu.VMEM((1, SLOTS), F32),
            pltpu.VMEM((1, SLOTS), F32),
            pltpu.VMEM((1, SLOTS), jnp.int32),
            pltpu.VMEM((SECTION, 1, Q), F32),
            pltpu.VMEM((Q, Q), F32),
            pltpu.VMEM((NY, NXZ, 1, Q), F32),
            pltpu.VMEM((NY, NXZ, 1, Q), F32),
            pltpu.VMEM((NXZ, NY, 1, Q), F32),
            pltpu.VMEM((NXZ, NY, 1, Q), F32),
            pltpu.VMEM((8, SLOTS), F32),
            pltpu.VMEM((8, SLOTS), F32),
            pltpu.VMEM((8, Q), F32),
            pltpu.VMEM((8, Q), F32),
            pltpu.VMEM((16, Q), F32),
            pltpu.VMEM((2, (NBLK + 1) * Q, SLOTS), BF16),
            pltpu.VMEM((2, 2 * Q, SLOTS), BF16),
            pltpu.VMEM((2, NXZ, 8, EXT * Q), F32),
            pltpu.VMEM((16, 1, Q), F32),
            pltpu.VMEM((32, 1, Q), F32),
            pltpu.VMEM((1, Q), F32),
            dma((9,)),
            dma((NY - 1,)), dma((NY - 1,)),
            dma((NXZ,)), dma((NXZ,)),
            dma,
            dma((2,)), dma((NXZ,)),
            dma((2,)), dma((2,)),
            dma((16,)), dma((16,)),
            dma((32,)), dma((32,)),
        ],
        compiler_params=pltpu.CompilerParams(
            collective_id=0, has_side_effects=True, vmem_limit_bytes=48 * 1024 * 1024
        ),
        name="gibbs_round",
    )(
        *(
            pltpu.with_memory_space_constraint(v, pltpu.HBM)
            for v in (
                data,
                inv_noise.reshape(NBLK, Q),
                mbh_amp.transpose(1, 2, 0, 3).reshape(rows, 1, Q),
                mbh_phase.transpose(1, 2, 0, 3).reshape(rows, 1, Q),
                bin_amp, bin_phase, bin_slope, bin_curve, bin_start,
            )
        ),
        bin_count,
    )
    return accept, residual.transpose(1, 0, 2), fit


def solution(mesh):
    split = Mesh(mesh.devices.reshape(2, 2, NX, NZ, NY), GROUP_SHARD)
    return jax.shard_map(
        local,
        mesh=split,
        in_specs=(
            P(None, GROUP_SHARD),
            P(GROUP_SHARD),
            P(SHARD, None, None, GROUP),
            P(SHARD, None, None, GROUP),
            P(GROUP_SHARD, None),
            P(GROUP_SHARD, None),
            P(GROUP_SHARD, None),
            P(GROUP_SHARD, None),
            P(GROUP_SHARD, None),
            P(GROUP_SHARD),
        ),
        out_specs=(P(None, GROUP_SHARD), P(None, None, GROUP_SHARD), P(GROUP_SHARD)),
        check_vma=False,
    )
```

```python
import jax
import jax.numpy as jnp
from jax import lax
from jax.experimental import pallas as pl
from jax.experimental.pallas import tpu as pltpu
from jax.sharding import Mesh
from jax.sharding import PartitionSpec as P

W = 64
HALF = 6
Q = 128
BINS = 1024
SLOTS = 512
NCOEF = 8
NX, NZ, NY = 4, 4, 8
NXZ = NX * NZ
NBANDS = 512
NBLK = BINS // Q
EXT = NBLK + 2
SHARD = ("shard_0", "shard_1", "shard_2")
GROUP_SHARD = ("group_0", "group_1", "shard_0", "shard_1", "shard_2")
GROUP = ("group_0", "group_1")
MESH = pl.DeviceIdType.MESH
F32 = jnp.float32
BF16 = jnp.bfloat16

INV_TURN = 0.15915494309189535
TURN_HI = 6.28125
TURN_LO = 0.0019353071795864769
SIN_C = (4.44288283, -7.30824115, 3.60628896, -0.84576359, 0.10920575)
COS_C = (1.4142135, -6.97885099, 5.73946117, -1.88356298, 0.31069818)
COS6_C = (1.41421356, -6.97886411, 5.73988155, -1.888275, 0.33225188, -0.03450217)
SECTION = 40
FAR = (4, 3, 5, 2, 6, 1, 7, 0)
PLANE = ((2, 2), (2, 1), (1, 2), (2, 3), (3, 2), (1, 1), (1, 3), (3, 1), (3, 3),
         (0, 2), (2, 0), (0, 1), (0, 3), (1, 0), (3, 0), (0, 0))


def poly(coefs, square):
    total = coefs[-1] * square + coefs[-2]
    for c in coefs[-3::-1]:
        total = total * square + c
    return total


def nearest(t):
    return jnp.round(t)


def sin_cos_halves(f):
    square = f * f
    return f * poly(SIN_C, square), poly(COS_C, square)


def chebyshev_rows(x, index):
    terms = [jnp.ones_like(x), x]
    for _ in range(2, NCOEF):
        terms.append(2.0 * x * terms[-1] - terms[-2])
    out = jnp.zeros_like(x)
    for k in range(NCOEF):
        out = jnp.where(index == k, terms[k], out)
    return out


def wave_tile(amp, phase, slope, curve, start, live):
    low = jnp.bitwise_and(start, Q - 1)
    row = lax.broadcasted_iota(jnp.int32, (Q, SLOTS), 0)
    j = jnp.bitwise_and(row - low, Q - 1)
    block = lax.shift_right_logical(start, 7) + (row < low).astype(jnp.int32)
    jf = j.astype(F32)
    angle = phase + slope * jf + curve * jf * jf
    turns = nearest(angle * INV_TURN)
    rest = (angle - turns * TURN_HI) - turns * TURN_LO
    s, c = sin_cos_halves(rest * INV_TURN)
    y = (jf + (0.5 - Q / 2)) * (1.0 / Q)
    half = poly(COS6_C, y * y)
    size = jnp.where(live, amp, 0.0) * (half * half * 0.5)
    re = size * (1.0 - s * s)
    im = size * (s * c)
    return re.astype(BF16).astype(F32), im.astype(BF16).astype(F32), block


def wrapped(v, n):
    return jnp.where(v >= n, v - n, v)


def kernel(
    data_hbm, noise_hbm, amp_hbm, phase_hbm, bamp_hbm, bphase_hbm, bslope_hbm, bcurve_hbm,
    bstart_hbm, bcount,
    acc_out, res_out, fit_out,
    data_ref, noise_ref, bamp, bphase, bslope, bcurve, bstart,
    xm, m, s1, r1, a, ex, pk, fw, bk, bw, wt, wp, rim_power, self_ref, res, new_ref, ra, rb,
    zrow_ref,
    in_sem, p1_send, p1_recv, p2_send, p2_recv, own_sem, ex_send, ex_recv, nb_send, nb_recv,
    ra_send, ra_recv, rb_send, rb_recv,
):
    coef_rows = 3 * HALF
    inputs = [
        (amp_hbm, xm.at[0:coef_rows]), (phase_hbm, xm.at[coef_rows:2 * coef_rows]),
        (data_hbm, data_ref), (noise_hbm, noise_ref), (bamp_hbm, bamp), (bphase_hbm, bphase),
        (bslope_hbm, bslope), (bcurve_hbm, bcurve), (bstart_hbm, bstart),
    ]
    fetches = [
        pltpu.make_async_copy(src, dst, in_sem.at[i]) for i, (src, dst) in enumerate(inputs)
    ]
    for fetch in fetches:
        fetch.start()

    zh, co = lax.axis_index("group_0"), lax.axis_index("group_1")
    x, z, y = lax.axis_index("shard_0"), lax.axis_index("shard_1"), lax.axis_index("shard_2")
    g = zh * 2 + co
    s = x * (NZ * NY) + z * NY + y
    n = g * (NBANDS // 4) + s
    xz = x * NZ + z
    ida = co * NY + y
    idb = zh * NXZ + xz
    has_prev, has_next = n > 0, n < NBANDS - 1
    first, last = s == 0, s == NBANDS // 4 - 1
    up = (y == 0) & (g < 3)
    down = (y == NY - 1) & (g > 0)

    def at(group0, group1, xi, zi, yi):
        return {
            "group_0": group0, "group_1": group1, "shard_0": xi, "shard_1": zi, "shard_2": yi,
        }

    turn_y = y == NY - 1
    turn_z = turn_y & (z == NZ - 1)
    turn_x = turn_z & (x == NX - 1)
    turn_c = turn_x & (co == 1)
    above_id = at(
        jnp.where(turn_c, 1 - zh, zh), jnp.where(turn_x, 1 - co, co),
        jnp.where(turn_z, wrapped(x + 1, NX), x), jnp.where(turn_y, wrapped(z + 1, NZ), z),
        wrapped(y + 1, NY),
    )
    back_y = y == 0
    back_z = back_y & (z == 0)
    back_x = back_z & (x == 0)
    back_c = back_x & (co == 0)
    below_id = at(
        jnp.where(back_c, 1 - zh, zh), jnp.where(back_x, 1 - co, co),
        jnp.where(back_z, wrapped(x + NX - 1, NX), x),
        jnp.where(back_y, wrapped(z + NZ - 1, NZ), z),
        wrapped(y + NY - 1, NY),
    )
    next_zh, next_co = jnp.where(co == 1, 1 - zh, zh), 1 - co
    prev_zh, prev_co = jnp.where(co == 0, 1 - zh, zh), 1 - co

    barrier = pltpu.get_barrier_semaphore()

    def greet(where):
        pl.semaphore_signal(barrier, inc=1, device_id=where, device_id_type=MESH)

    def peer_y(dc, dy):
        return {"group_1": 1 - co if dc else co, "shard_2": wrapped(y + dy, NY)}

    def peer_plane(dh, dx, dz):
        return {
            "group_0": 1 - zh if dh else zh,
            "shard_0": wrapped(x + dx, NX), "shard_1": wrapped(z + dz, NZ),
        }

    members_a = [(dc, dy) for dy in FAR for dc in (1, 0) if (dc, dy) != (0, 0)]
    members_b = [(dh, dx, dz) for dx, dz in PLANE for dh in (1, 0) if (dh, dx, dz) != (0, 0, 0)]

    @pl.when(first & (g > 0))
    def _():
        for k in range(NXZ):
            greet(at(prev_zh, prev_co, k // NZ, k % NZ, 0))

    @pl.when(last & (g < 3))
    def _():
        for k in range(NXZ):
            greet(at(next_zh, next_co, k // NZ, k % NZ, NY - 1))

    for member in members_b:
        greet(peer_plane(*member))
    for member in members_a:
        greet(peer_y(*member))

    @pl.when(has_prev)
    def _():
        greet(below_id)

    @pl.when(has_next)
    def _():
        greet(above_id)

    xm[2 * coef_rows:SECTION] = jnp.zeros((SECTION - 2 * coef_rows, 1, Q), F32)
    for fetch in fetches:
        fetch.wait()
    own = xm[:, 0, :]
    m[...] = jnp.concatenate(
        [own, pltpu.roll(own, 1, 1), pltpu.roll(own, Q - 1, 1), jnp.zeros((8, Q), F32)], axis=0
    ).T
    for k in range(NY):
        s1[k, :, 0, :] = m[pl.ds(k, NXZ, stride=NY), :]

    noise8 = noise_ref[...].astype(F32)
    noise = jnp.concatenate([noise8[b:b + 1, :] for b in range(NBLK)], axis=1)
    pk[...] = jnp.zeros_like(pk)
    pk[0:1, :] = bamp[...]
    pk[1:2, :] = bphase[...]
    pk[2:3, :] = bslope[...]
    pk[3:4, :] = bcurve[...]
    pk[4:5, :] = bstart[...].astype(F32)
    pk[5:6, :] = jnp.full((1, SLOTS), bcount[0], jnp.int32).astype(F32)
    pk[6:7, 0:Q] = data_ref[0:1, BINS - Q:]
    pk[6:7, Q:2 * Q] = data_ref[1:2, BINS - Q:]
    pk[6:7, 2 * Q:3 * Q] = noise8[NBLK - 1:NBLK, :]
    bk[...] = jnp.zeros_like(bk)
    bk[0:2, :] = data_ref[:, 0:Q]
    bk[2:3, :] = noise8[0:1, :]

    slot = lax.broadcasted_iota(jnp.int32, (1, SLOTS), 1)
    waits = 15 + 31 + has_prev.astype(jnp.int32) + has_next.astype(jnp.int32)
    pl.semaphore_wait(barrier, waits + up.astype(jnp.int32) + down.astype(jnp.int32))

    def remote(src, dst, send, recv, where):
        return pltpu.make_async_remote_copy(
            src_ref=src, dst_ref=dst, send_sem=send, recv_sem=recv, device_id=where,
            device_id_type=MESH,
        )

    slot_y = (y % 2) * (NY // 2) + y // 2

    def p1(dy):
        k = wrapped(y + dy, NY)
        return remote(
            s1.at[k], r1.at[slot_y], p1_send.at[dy - 1], p1_recv.at[dy - 1], {"shard_2": k}
        )

    for dy in FAR[:-1]:
        p1(dy).start()

    forward = remote(pk, fw, nb_send.at[0], nb_recv.at[0], above_id)
    backward = remote(bk, bw, nb_send.at[1], nb_recv.at[1], below_id)

    @pl.when(has_next)
    def _():
        forward.start()

    @pl.when(has_prev)
    def _():
        backward.start()

    r1[slot_y] = s1[y]

    @pl.when(n >= 0)
    def _():
        re_own, im_own, block_own = wave_tile(
            bamp[...], bphase[...], bslope[...], bcurve[...], bstart[...], slot < bcount[0]
        )
        noise_columns = jnp.concatenate([noise8, jnp.zeros((8, Q), F32)], axis=0).T
        total = jnp.zeros((Q, SLOTS), F32)
        for b in range(NBLK + 1):
            here = block_own == b
            wt[0, b * Q:(b + 1) * Q, :] = jnp.where(here, re_own, 0.0).astype(BF16)
            wt[1, b * Q:(b + 1) * Q, :] = jnp.where(here, im_own, 0.0).astype(BF16)
            if b < NBLK:
                total = jnp.where(here, noise_columns[:, b:b + 1], total)
        power = re_own * re_own + im_own * im_own
        rim_power[...] = jnp.where(block_own == NBLK, power, 0.0)
        self_ref[...] = jnp.sum(power * total, axis=0, keepdims=True)

    for dy in FAR[:-1]:
        p1(dy).wait_recv()

    up_copy = remote(
        r1.at[:, 0], ex.at[xz], ex_send.at[0], ex_recv.at[xz], at(next_zh, next_co, 0, 0, 0)
    )
    down_copy = remote(
        r1.at[:, NXZ - 1], ex.at[xz], ex_send.at[1], ex_recv.at[xz],
        at(prev_zh, prev_co, NX - 1, NZ - 1, NY - 1),
    )

    @pl.when(up)
    def _():
        up_copy.start()

    @pl.when(down)
    def _():
        down_copy.start()

    def p2(dx, dz):
        xk, zk = wrapped(x + dx, NX), wrapped(z + dz, NZ)
        d = dx * NZ + dz
        return remote(
            r1.at[:, xk * NZ + zk], a.at[xz], p2_send.at[d], p2_recv.at[d],
            {"shard_0": xk, "shard_1": zk},
        )

    for dx, dz in PLANE[:-1]:
        p2(dx, dz).start()
    a[xz] = r1[:, xz]

    @pl.when(has_prev)
    def _():
        forward.wait_recv()

    @pl.when(has_next)
    def _():
        backward.wait_recv()

    below = jnp.where(jnp.full((8, SLOTS), n, jnp.int32) > 0, fw[...], 0.0)
    above = jnp.where(jnp.full((8, Q), n, jnp.int32) < NBANDS - 1, bw[...], 0.0)
    re_prev, im_prev, block_prev = wave_tile(
        below[0:1], below[1:2], below[2:3], below[3:4], below[4:5].astype(jnp.int32),
        slot.astype(F32) < below[5:6],
    )
    for b in range(2):
        here = block_prev == NBLK - 1 + b
        wp[0, b * Q:(b + 1) * Q, :] = jnp.where(here, re_prev, 0.0).astype(BF16)
        wp[1, b * Q:(b + 1) * Q, :] = jnp.where(here, im_prev, 0.0).astype(BF16)

    rim_noise = jnp.concatenate(
        [below[6:7, 2 * Q:3 * Q], noise8[0:1, :], above[2:3, :], jnp.zeros((5, Q), F32)], axis=0
    ).T
    self_power = self_ref[...] + jnp.sum(rim_power[...] * rim_noise[:, 2:3], axis=0, keepdims=True)
    power_prev = re_prev * re_prev + im_prev * im_prev
    total_prev = jnp.where(
        block_prev == NBLK - 1, rim_noise[:, 0:1],
        jnp.where(block_prev == NBLK, rim_noise[:, 1:2], 0.0),
    )
    self_prev = jnp.sum(power_prev * total_prev, axis=0, keepdims=True)

    edge_first, edge_last = first & (g > 0), last & (g < 3)
    edge = edge_first | edge_last
    lane_q = lax.broadcasted_iota(jnp.int32, (8, Q), 1)
    take_prev = jnp.full((8, Q), edge_first.astype(jnp.int32), jnp.int32)
    take_next = jnp.full((8, Q), edge_last.astype(jnp.int32), jnp.int32)
    take = ((take_prev > 0) & (lane_q >= SECTION) & (lane_q < 2 * SECTION)) | (
        (take_next > 0) & (lane_q >= 2 * SECTION)
    )
    below_data = (below[6:7, 0:Q], below[6:7, Q:2 * Q])

    def template_rows(step, carry):
        quarter = step // NZ
        dx = jnp.where(quarter >= 2, 5 - quarter, quarter)
        dz = step % NZ
        xk, zk = wrapped(x + NX - dx, NX), wrapped(z + NZ - dz, NZ)
        k = xk * NZ + zk
        d = dx * NZ + dz

        @pl.when(step > 0)
        def _():
            remote(
                r1.at[:, 0], a.at[k], p2_send.at[d], p2_recv.at[d],
                {"shard_0": xk, "shard_1": zk},
            ).wait_recv()

        @pl.when(edge)
        def _():
            remote(
                r1.at[:, 0], ex.at[k], ex_send.at[0], ex_recv.at[k], at(zh, co, 0, 0, 0)
            ).wait_recv()

        tile = jnp.where(take, ex[k, :, 0, :], a[k, :, 0, :])
        turns_tile = tile * INV_TURN
        pieces = [(1, BINS - Q, 0)] + [(0, 512 * c, 1 + 4 * c) for c in range(2)]
        for section, offset, block in pieces + [(2, 0, NBLK + 1)]:
            width = 512 if section == 0 else Q
            u = (
                lax.broadcasted_iota(jnp.int32, (1, width), 1).astype(F32) + offset
            ) * (1.0 / BINS)
            base = section * SECTION
            lost = amp_sum = im = None
            for h in range(HALF):
                a0, a1, a2 = (tile[:, base + 3 * h + i:base + 3 * h + i + 1] for i in range(3))
                q = base + coef_rows + 3 * h
                p0, p1_, p2_ = (turns_tile[:, q + i:q + i + 1] for i in range(3))
                t = p0 + u * (p1_ + u * p2_)
                f = t - nearest(t)
                sn, cs = sin_cos_halves(f)
                amp = a0 + u * (a1 + u * a2)
                asn = amp * sn
                if h == 0:
                    amp_sum, lost, im = amp, asn * sn, asn * cs
                else:
                    amp_sum, lost, im = amp_sum + amp, lost + asn * sn, im + asn * cs
            for part, half in enumerate((amp_sum - lost, im)):
                half = half.astype(BF16).astype(F32)
                template = half + pltpu.roll(half, 4, 0)
                if section == 0:
                    values = data_ref[part:part + 1, offset:offset + width]
                elif section == 1:
                    values = below_data[part]
                else:
                    values = above[part:part + 1, :]
                res[part, k, :, block * Q:block * Q + width] = values - template
        return carry

    lax.fori_loop(0, NXZ, template_rows, 0)

    noise_ext = jnp.concatenate([below[6:7, 2 * Q:3 * Q], noise, above[2:3, :]], axis=1)
    corr = jnp.zeros((W, SLOTS), F32)
    corr_prev = jnp.zeros((W, SLOTS), F32)
    upper = lax.broadcasted_iota(jnp.int32, (NXZ // 2, 8, EXT * Q), 1) < 4

    def residual(part):
        pairs = res[part].reshape(NXZ // 2, 2, 8, EXT * Q)
        return jnp.where(upper, pairs[:, 0], pairs[:, 1]).reshape(W, EXT * Q)

    residuals = [residual(part) for part in range(2)]
    for part in range(2):
        weighted = (residuals[part] * noise_ext).astype(BF16)
        corr += jnp.dot(weighted[:, Q:], wt[part], preferred_element_type=F32)
        corr_prev += jnp.dot(weighted[:, 0:2 * Q], wp[part], preferred_element_type=F32)

    def sigmoid(v):
        return 1.0 / (1.0 + jnp.exp(-v))

    accept = jnp.where(slot < bcount[0], sigmoid(corr - 0.5 * self_power), 0.0)
    acc_out[...] = accept
    accept = accept.astype(BF16)
    accept_prev = sigmoid(corr_prev - 0.5 * self_prev).astype(BF16)
    square = jnp.zeros((1, BINS), F32)
    nt = (((1,), (1,)), ((), ()))
    for part in range(2):
        change = lax.dot_general(accept, wt[part, 0:BINS, :], nt, preferred_element_type=F32)
        rim = lax.dot_general(accept_prev, wp[part, Q:2 * Q, :], nt, preferred_element_type=F32)
        new = residuals[part][:, Q:Q + BINS] - change
        new = jnp.concatenate([new[:, 0:Q] - rim, new[:, Q:]], axis=1)
        new_ref[part] = new
        square += jnp.sum(new * new, axis=0, keepdims=True)
    mean = jnp.sum(square, axis=1, keepdims=True) * (1.0 / (2 * W * BINS))
    log_power = jnp.log(mean + 1e-06)
    lane = lax.broadcasted_iota(jnp.int32, (1, Q), 1)
    mine = chebyshev_rows((2 * jnp.full((1, Q), n, jnp.int32) + 1).astype(F32) / NBANDS - 1.0, lane)
    ra[ida] = mine * log_power

    def sum_a(dc, dy):
        d = dc * NY + dy
        return remote(ra.at[ida], ra.at[ida], ra_send.at[d], ra_recv.at[d], peer_y(dc, dy))

    def sum_b(dh, dx, dz):
        d = (dh * NX + dx) * NZ + dz
        return remote(rb.at[idb], rb.at[idb], rb_send.at[d], rb_recv.at[d], peer_plane(dh, dx, dz))

    for member in members_a:
        sum_a(*member).start()

    @pl.when(n >= 0)
    def _():
        bands = lax.broadcasted_iota(jnp.int32, (NCOEF, NBANDS), 1)
        basis = chebyshev_rows(
            (2 * bands + 1).astype(F32) / NBANDS - 1.0,
            lax.broadcasted_iota(jnp.int32, (NCOEF, NBANDS), 0),
        )
        sub = lax.broadcasted_iota(jnp.int32, (NCOEF, Q), 0)
        lane8 = lax.broadcasted_iota(jnp.int32, (NCOEF, Q), 1)
        position = (2 * jnp.full((NCOEF, Q), n, jnp.int32) + 1).astype(F32) / NBANDS - 1.0
        table = jnp.where(lane8 == NCOEF, chebyshev_rows(position, sub), 0.0)
        for k in range(NCOEF):
            column = jnp.sum(basis * basis[k:k + 1, :], axis=1, keepdims=True)
            table = jnp.where(lane8 == k, column, table)
        rows = []
        for k in range(NCOEF):
            root = jnp.sqrt(table[k:k + 1, k:k + 1])
            row = table[k:k + 1, :] / root
            column = table[:, k:k + 1] / root
            rows.append(row)
            table = jnp.where(sub > k, table - column * row, table)
        zrow = jnp.zeros((1, Q), F32)
        for k in reversed(range(NCOEF)):
            row = rows[k]
            known = jnp.sum(jnp.where((lane > k) & (lane < NCOEF), row * zrow, 0.0), axis=1, keepdims=True)
            value = (row[:, NCOEF:NCOEF + 1] - known) / row[:, k:k + 1]
            zrow = jnp.where(lane == k, value, zrow)
        zrow_ref[...] = zrow
        for part in range(2):
            res_out[:, part, :] = new_ref[part]

    for dy in FAR[:-1]:
        p1(dy).wait_send()
    for dx, dz in PLANE[:-1]:
        p2(dx, dz).wait_send()

    @pl.when(has_next)
    def _():
        forward.wait_send()

    @pl.when(has_prev)
    def _():
        backward.wait_send()

    @pl.when(up)
    def _():
        up_copy.wait_send()

    @pl.when(down)
    def _():
        down_copy.wait_send()

    for member in members_a:
        sum_a(*member).wait_recv()
    rb[idb] = jnp.sum(ra[...], axis=0)
    for member in members_b:
        sum_b(*member).start()
    for member in members_a:
        sum_a(*member).wait_send()
    for member in members_b:
        sum_b(*member).wait_recv()
    moment = jnp.sum(rb[...], axis=0)
    fit_out[0] = jnp.sum(zrow_ref[...] * moment)
    for member in members_b:
        sum_b(*member).wait_send()


def write_out(acc_ref, res_ref, acc_out, res_out, sems):
    copies = [
        pltpu.make_async_copy(res_ref, res_out, sems.at[0]),
        pltpu.make_async_copy(acc_ref, acc_out, sems.at[1]),
    ]
    for copy in copies:
        copy.start()
    for copy in copies:
        copy.wait()


def local(data, inv_noise, mbh_amp, mbh_phase, bin_amp, bin_phase, bin_slope, bin_curve, bin_start, bin_count):
    vmem = pl.BlockSpec(memory_space=pltpu.VMEM)
    smem = pl.BlockSpec(memory_space=pltpu.SMEM)
    dma = pltpu.SemaphoreType.DMA
    rows = 3 * HALF
    accept, residual, fit = pl.pallas_call(
        kernel,
        out_shape=(
            jax.ShapeDtypeStruct((W, SLOTS), F32),
            jax.ShapeDtypeStruct((W, 2, BINS), F32),
            jax.ShapeDtypeStruct((1,), F32),
        ),
        in_specs=[pl.BlockSpec(memory_space=pltpu.HBM)] * 9 + [smem],
        out_specs=(vmem, vmem, smem),
        scratch_shapes=[
            pltpu.VMEM((2, BINS), F32),
            pltpu.VMEM((NBLK, Q), BF16),
            pltpu.VMEM((1, SLOTS), F32),
            pltpu.VMEM((1, SLOTS), F32),
            pltpu.VMEM((1, SLOTS), F32),
            pltpu.VMEM((1, SLOTS), F32),
            pltpu.VMEM((1, SLOTS), jnp.int32),
            pltpu.VMEM((SECTION, 1, Q), F32),
            pltpu.VMEM((Q, Q), F32),
            pltpu.VMEM((NY, NXZ, 1, Q), F32),
            pltpu.VMEM((NY, NXZ, 1, Q), F32),
            pltpu.VMEM((NXZ, NY, 1, Q), F32),
            pltpu.VMEM((NXZ, NY, 1, Q), F32),
            pltpu.VMEM((8, SLOTS), F32),
            pltpu.VMEM((8, SLOTS), F32),
            pltpu.VMEM((8, Q), F32),
            pltpu.VMEM((8, Q), F32),
            pltpu.VMEM((2, (NBLK + 1) * Q, SLOTS), BF16),
            pltpu.VMEM((2, 2 * Q, SLOTS), BF16),
            pltpu.VMEM((Q, SLOTS), F32),
            pltpu.VMEM((1, SLOTS), F32),
            pltpu.VMEM((2, NXZ, 8, EXT * Q), F32),
            pltpu.VMEM((2, W, BINS), F32),
            pltpu.VMEM((16, 1, Q), F32),
            pltpu.VMEM((32, 1, Q), F32),
            pltpu.VMEM((1, Q), F32),
            dma((9,)),
            dma((NY - 1,)), dma((NY - 1,)),
            dma((NXZ,)), dma((NXZ,)),
            dma,
            dma((2,)), dma((NXZ,)),
            dma((2,)), dma((2,)),
            dma((16,)), dma((16,)),
            dma((32,)), dma((32,)),
        ],
        compiler_params=pltpu.CompilerParams(
            collective_id=0, has_side_effects=True, vmem_limit_bytes=48 * 1024 * 1024
        ),
        name="gibbs_round",
    )(
        *(
            pltpu.with_memory_space_constraint(v, pltpu.HBM)
            for v in (
                data,
                inv_noise.reshape(NBLK, Q),
                mbh_amp.transpose(1, 2, 0, 3).reshape(rows, 1, Q),
                mbh_phase.transpose(1, 2, 0, 3).reshape(rows, 1, Q),
                bin_amp, bin_phase, bin_slope, bin_curve, bin_start,
            )
        ),
        bin_count,
    )
    accept, residual = pl.pallas_call(
        write_out,
        out_shape=(
            jax.ShapeDtypeStruct((W, SLOTS), F32),
            jax.ShapeDtypeStruct((W, 2, BINS), F32),
        ),
        in_specs=[vmem] * 2,
        out_specs=(pl.BlockSpec(memory_space=pltpu.HBM),) * 2,
        scratch_shapes=[dma((2,))],
        name="write_out",
    )(
        pltpu.with_memory_space_constraint(accept, pltpu.VMEM),
        pltpu.with_memory_space_constraint(residual, pltpu.VMEM),
    )
    return accept, residual, fit


def solution(mesh):
    split = Mesh(mesh.devices.reshape(2, 2, NX, NZ, NY), GROUP_SHARD)
    return jax.shard_map(
        local,
        mesh=split,
        in_specs=(
            P(None, GROUP_SHARD),
            P(GROUP_SHARD),
            P(SHARD, None, None, GROUP),
            P(SHARD, None, None, GROUP),
            P(GROUP_SHARD, None),
            P(GROUP_SHARD, None),
            P(GROUP_SHARD, None),
            P(GROUP_SHARD, None),
            P(GROUP_SHARD, None),
            P(GROUP_SHARD),
        ),
        out_specs=(P(None, GROUP_SHARD), P(None, None, GROUP_SHARD), P(GROUP_SHARD)),
        check_vma=False,
    )
```

```python
import jax
import jax.numpy as jnp
from jax import lax
from jax.experimental import pallas as pl
from jax.experimental.pallas import tpu as pltpu
from jax.sharding import Mesh
from jax.sharding import PartitionSpec as P

W = 64
HALF = 6
Q = 128
BINS = 1024
SLOTS = 512
NCOEF = 8
NX, NZ, NY = 4, 4, 8
NXZ = NX * NZ
NBANDS = 512
NBLK = BINS // Q
EXT = NBLK + 2
SHARD = ("shard_0", "shard_1", "shard_2")
GROUP_SHARD = ("group_0", "group_1", "shard_0", "shard_1", "shard_2")
GROUP = ("group_0", "group_1")
MESH = pl.DeviceIdType.MESH
F32 = jnp.float32
BF16 = jnp.bfloat16

INV_TURN = 0.15915494309189535
TURN_HI = 6.28125
TURN_LO = 0.0019353071795864769
SIN_C = (4.44288283, -7.30824115, 3.60628896, -0.84576359, 0.10920575)
COS_C = (1.4142135, -6.97885099, 5.73946117, -1.88356298, 0.31069818)
COS6_C = (1.41421356, -6.97886411, 5.73988155, -1.888275, 0.33225188, -0.03450217)
SIN1_C = (3.14159258, -5.16770688, 2.55003138, -0.59804517, 0.0772201264)
COS1_C = (0.999999956, -4.93479286, 4.05841191, -1.33188016, 0.21969679)
SECTION = 36
ROT = 108
TILES = 2
FAR = (4, 3, 5, 2, 6, 1, 7, 0)
PLANE = ((2, 2), (2, 1), (1, 2), (2, 3), (3, 2), (1, 1), (1, 3), (3, 1), (3, 3),
         (0, 2), (2, 0), (0, 1), (0, 3), (1, 0), (3, 0), (0, 0))


def poly(coefs, square):
    total = coefs[-1] * square + coefs[-2]
    for c in coefs[-3::-1]:
        total = total * square + c
    return total


def nearest(t):
    return jnp.round(t)


def sin_cos_halves(f):
    square = f * f
    return f * poly(SIN_C, square), poly(COS_C, square)


def chebyshev_rows(x, index):
    terms = [jnp.ones_like(x), x]
    for _ in range(2, NCOEF):
        terms.append(2.0 * x * terms[-1] - terms[-2])
    out = jnp.zeros_like(x)
    for k in range(NCOEF):
        out = jnp.where(index == k, terms[k], out)
    return out


def wave_tile(amp, phase, slope, curve, start, live):
    low = jnp.bitwise_and(start, Q - 1)
    row = lax.broadcasted_iota(jnp.int32, (Q, SLOTS), 0)
    j = jnp.bitwise_and(row - low, Q - 1)
    block = lax.shift_right_logical(start, 7) + (row < low).astype(jnp.int32)
    jf = j.astype(F32)
    angle = phase + slope * jf + curve * jf * jf
    turns = nearest(angle * INV_TURN)
    rest = (angle - turns * TURN_HI) - turns * TURN_LO
    s, c = sin_cos_halves(rest * INV_TURN)
    y = (jf + (0.5 - Q / 2)) * (1.0 / Q)
    half = poly(COS6_C, y * y)
    size = jnp.where(live, amp, 0.0) * (half * half * 0.5)
    re = size * (1.0 - s * s)
    im = size * (s * c)
    return re.astype(BF16).astype(F32), im.astype(BF16).astype(F32), block


def own_template(tile, base, coef_rows):
    v = (lax.broadcasted_iota(jnp.int32, (8, Q), 1).astype(F32) + (NBLK - 1) * Q / 2) * (1.0 / BINS)
    re, im = [None] * NBLK, [None] * NBLK
    for h in range(HALF):
        ca = base + 3 * h
        cp = ca + coef_rows
        a0, a1, a2, p0, p1, p2, g2r, g2i = (
            jnp.broadcast_to(tile[:, k:k + 1], (8, Q))
            for k in (ca, ca + 1, ca + 2, cp, cp + 1, cp + 2, ROT + h, ROT + 8 + h)
        )
        g4r, g4i = 1.0 - 2.0 * (g2i * g2i), 2.0 * (g2i * g2r)
        g6r, g6i = g4r * g2r - g4i * g2i, g4i * g2r + g4r * g2i
        theta = p1 * 0.125 + v * (p2 * 0.25)
        whole = nearest(theta)
        f = theta - whole
        square = f * f
        yi, yr = f * poly(SIN1_C, square), poly(COS1_C, square)
        twice = 2.0 - 4.0 * (yi * yi)
        y_last = None
        center = (p0 + v * (p1 + v * p2)) + (p2 * (1.0 / 256) + 0.5 * whole)
        s, c = sin_cos_halves(center - nearest(center))
        xr, xi = 1.0 - s * s, s * c
        alpha = a0 + v * (a1 + v * a2)
        beta = a1 * 0.125 + v * (a2 * 0.25)
        curve = a2 * (1.0 / 64)
        for i in range(NBLK // 2):
            m = i + 0.5
            if i == 1:
                y_next = ((twice - 1.0) * yr, (twice + 1.0) * yi)
            elif i > 1:
                y_next = (twice * yr - y_last[0], twice * yi - y_last[1])
            if i > 0:
                y_last, (yr, yi) = (yr, yi), y_next
                rr, ri = ((g2r, g2i), (g4r, g4i), (g6r, g6i))[i - 1]
                xr, xi = xr * rr - xi * ri, xi * rr + xr * ri
            size, tilt = alpha + curve * (m * m), beta * m
            rr_, ii_, ri_, ir_ = xr * yr, xi * yi, xr * yi, xi * yr
            for block, amp, x_re, x_im in (
                (NBLK // 2 + i, size + tilt, rr_ - ii_, ir_ + ri_),
                (NBLK // 2 - 1 - i, size - tilt, rr_ + ii_, ir_ - ri_),
            ):
                if h == 0:
                    re[block], im[block] = amp * x_re, amp * x_im
                else:
                    re[block], im[block] = re[block] + amp * x_re, im[block] + amp * x_im
    return re, im


def wrapped(v, n):
    return jnp.where(v >= n, v - n, v)


def kernel(
    data_hbm, noise_hbm, amp_hbm, phase_hbm, bamp_hbm, bphase_hbm, bslope_hbm, bcurve_hbm,
    bstart_hbm, bcount,
    acc_out, res_out, fit_out,
    data_ref, noise_ref, bamp, bphase, bslope, bcurve, bstart,
    xm, m, s1, r1, a, ex, pk, fw, bk, bw, wt, wp, rim_power, self_ref, res, new_ref, ra, rb,
    zrow_ref,
    in_sem, p1_send, p1_recv, p2_send, p2_recv, own_sem, ex_send, ex_recv, nb_send, nb_recv,
    ra_send, ra_recv, rb_send, rb_recv,
):
    coef_rows = 3 * HALF
    inputs = [
        (amp_hbm, xm.at[0:coef_rows]), (phase_hbm, xm.at[coef_rows:2 * coef_rows]),
        (data_hbm, data_ref), (noise_hbm, noise_ref), (bamp_hbm, bamp), (bphase_hbm, bphase),
        (bslope_hbm, bslope), (bcurve_hbm, bcurve), (bstart_hbm, bstart),
    ]
    fetches = [
        pltpu.make_async_copy(src, dst, in_sem.at[i]) for i, (src, dst) in enumerate(inputs)
    ]
    for fetch in fetches:
        fetch.start()

    zh, co = lax.axis_index("group_0"), lax.axis_index("group_1")
    x, z, y = lax.axis_index("shard_0"), lax.axis_index("shard_1"), lax.axis_index("shard_2")
    g = zh * 2 + co
    s = x * (NZ * NY) + z * NY + y
    n = g * (NBANDS // 4) + s
    xz = x * NZ + z
    ida = co * NY + y
    idb = zh * NXZ + xz
    has_prev, has_next = n > 0, n < NBANDS - 1
    first, last = s == 0, s == NBANDS // 4 - 1
    up = (y == 0) & (g < 3)
    down = (y == NY - 1) & (g > 0)

    def at(group0, group1, xi, zi, yi):
        return {
            "group_0": group0, "group_1": group1, "shard_0": xi, "shard_1": zi, "shard_2": yi,
        }

    turn_y = y == NY - 1
    turn_z = turn_y & (z == NZ - 1)
    turn_x = turn_z & (x == NX - 1)
    turn_c = turn_x & (co == 1)
    above_id = at(
        jnp.where(turn_c, 1 - zh, zh), jnp.where(turn_x, 1 - co, co),
        jnp.where(turn_z, wrapped(x + 1, NX), x), jnp.where(turn_y, wrapped(z + 1, NZ), z),
        wrapped(y + 1, NY),
    )
    back_y = y == 0
    back_z = back_y & (z == 0)
    back_x = back_z & (x == 0)
    back_c = back_x & (co == 0)
    below_id = at(
        jnp.where(back_c, 1 - zh, zh), jnp.where(back_x, 1 - co, co),
        jnp.where(back_z, wrapped(x + NX - 1, NX), x),
        jnp.where(back_y, wrapped(z + NZ - 1, NZ), z),
        wrapped(y + NY - 1, NY),
    )
    next_zh, next_co = jnp.where(co == 1, 1 - zh, zh), 1 - co
    prev_zh, prev_co = jnp.where(co == 0, 1 - zh, zh), 1 - co

    barrier = pltpu.get_barrier_semaphore()

    def greet(where):
        pl.semaphore_signal(barrier, inc=1, device_id=where, device_id_type=MESH)

    def peer_y(dc, dy):
        return {"group_1": 1 - co if dc else co, "shard_2": wrapped(y + dy, NY)}

    def peer_plane(dh, dx, dz):
        return {
            "group_0": 1 - zh if dh else zh,
            "shard_0": wrapped(x + dx, NX), "shard_1": wrapped(z + dz, NZ),
        }

    members_a = [(dc, dy) for dy in FAR for dc in (1, 0) if (dc, dy) != (0, 0)]
    members_b = [(dh, dx, dz) for dx, dz in PLANE for dh in (1, 0) if (dh, dx, dz) != (0, 0, 0)]

    @pl.when(first & (g > 0))
    def _():
        for k in range(NXZ):
            greet(at(prev_zh, prev_co, k // NZ, k % NZ, 0))

    @pl.when(last & (g < 3))
    def _():
        for k in range(NXZ):
            greet(at(next_zh, next_co, k // NZ, k % NZ, NY - 1))

    for member in members_b:
        greet(peer_plane(*member))
    for member in members_a:
        greet(peer_y(*member))

    @pl.when(has_prev)
    def _():
        greet(below_id)

    @pl.when(has_next)
    def _():
        greet(above_id)

    for fetch in fetches:
        fetch.wait()
    amps, turns = xm[0:coef_rows, 0, :], xm[coef_rows:2 * coef_rows, 0, :] * INV_TURN
    bend = jnp.concatenate([turns[3 * h + 2:3 * h + 3, :] for h in range(HALF)], axis=0)
    bend = bend * (1.0 / 32)
    sn, cs = sin_cos_halves(bend - nearest(bend))
    xm[coef_rows:2 * coef_rows, 0, :] = turns
    own = xm[:, 0, :]
    message = [own, pltpu.roll(own, 1, 1), pltpu.roll(own, Q - 1, 1)]
    xm[0:HALF, 0, :] = 1.0 - sn * sn
    xm[8:8 + HALF, 0, :] = sn * cs
    xm[16:24, 0, :] = jnp.zeros((8, Q), F32)
    m[...] = jnp.concatenate([part[0:2 * coef_rows] for part in message] + [xm[0:Q - 6 * coef_rows, 0, :]], axis=0).T
    for k in range(NY):
        s1[k, :, 0, :] = m[pl.ds(k, NXZ, stride=NY), :]

    noise8 = noise_ref[...].astype(F32)
    noise = jnp.concatenate([noise8[b:b + 1, :] for b in range(NBLK)], axis=1)
    pk[...] = jnp.zeros_like(pk)
    pk[0:1, :] = bamp[...]
    pk[1:2, :] = bphase[...]
    pk[2:3, :] = bslope[...]
    pk[3:4, :] = bcurve[...]
    pk[4:5, :] = bstart[...].astype(F32)
    pk[5:6, :] = jnp.full((1, SLOTS), bcount[0], jnp.int32).astype(F32)
    pk[6:7, 0:Q] = data_ref[0:1, BINS - Q:]
    pk[6:7, Q:2 * Q] = data_ref[1:2, BINS - Q:]
    pk[6:7, 2 * Q:3 * Q] = noise8[NBLK - 1:NBLK, :]
    bk[...] = jnp.zeros_like(bk)
    bk[0:2, :] = data_ref[:, 0:Q]
    bk[2:3, :] = noise8[0:1, :]

    slot = lax.broadcasted_iota(jnp.int32, (1, SLOTS), 1)
    waits = 15 + 31 + has_prev.astype(jnp.int32) + has_next.astype(jnp.int32)
    pl.semaphore_wait(barrier, waits + up.astype(jnp.int32) + down.astype(jnp.int32))

    def remote(src, dst, send, recv, where):
        return pltpu.make_async_remote_copy(
            src_ref=src, dst_ref=dst, send_sem=send, recv_sem=recv, device_id=where,
            device_id_type=MESH,
        )

    slot_y = (y % 2) * (NY // 2) + y // 2

    def p1(dy):
        k = wrapped(y + dy, NY)
        return remote(
            s1.at[k], r1.at[slot_y], p1_send.at[dy - 1], p1_recv.at[dy - 1], {"shard_2": k}
        )

    for dy in FAR[:-1]:
        p1(dy).start()

    forward = remote(pk, fw, nb_send.at[0], nb_recv.at[0], above_id)
    backward = remote(bk, bw, nb_send.at[1], nb_recv.at[1], below_id)

    @pl.when(has_next)
    def _():
        forward.start()

    @pl.when(has_prev)
    def _():
        backward.start()

    r1[slot_y] = s1[y]

    @pl.when(n >= 0)
    def _():
        re_own, im_own, block_own = wave_tile(
            bamp[...], bphase[...], bslope[...], bcurve[...], bstart[...], slot < bcount[0]
        )
        noise_columns = jnp.concatenate([noise8, jnp.zeros((8, Q), F32)], axis=0).T
        total = jnp.zeros((Q, SLOTS), F32)
        for b in range(NBLK + 1):
            here = block_own == b
            wt[0, b * Q:(b + 1) * Q, :] = jnp.where(here, re_own, 0.0).astype(BF16)
            wt[1, b * Q:(b + 1) * Q, :] = jnp.where(here, im_own, 0.0).astype(BF16)
            if b < NBLK:
                total = jnp.where(here, noise_columns[:, b:b + 1], total)
        power = re_own * re_own + im_own * im_own
        rim_power[...] = jnp.where(block_own == NBLK, power, 0.0)
        self_ref[...] = jnp.sum(power * total, axis=0, keepdims=True)

    for dy in FAR[:-1]:
        p1(dy).wait_recv()

    up_copy = remote(
        r1.at[:, 0], ex.at[xz], ex_send.at[0], ex_recv.at[xz], at(next_zh, next_co, 0, 0, 0)
    )
    down_copy = remote(
        r1.at[:, NXZ - 1], ex.at[xz], ex_send.at[1], ex_recv.at[xz],
        at(prev_zh, prev_co, NX - 1, NZ - 1, NY - 1),
    )

    @pl.when(up)
    def _():
        up_copy.start()

    @pl.when(down)
    def _():
        down_copy.start()

    def p2(dx, dz):
        xk, zk = wrapped(x + dx, NX), wrapped(z + dz, NZ)
        d = dx * NZ + dz
        return remote(
            r1.at[:, xk * NZ + zk], a.at[xz], p2_send.at[d], p2_recv.at[d],
            {"shard_0": xk, "shard_1": zk},
        )

    for dx, dz in PLANE[:-1]:
        p2(dx, dz).start()
    a[xz] = r1[:, xz]

    @pl.when(has_prev)
    def _():
        forward.wait_recv()

    @pl.when(has_next)
    def _():
        backward.wait_recv()

    below = jnp.where(jnp.full((8, SLOTS), n, jnp.int32) > 0, fw[...], 0.0)
    above = jnp.where(jnp.full((8, Q), n, jnp.int32) < NBANDS - 1, bw[...], 0.0)
    re_prev, im_prev, block_prev = wave_tile(
        below[0:1], below[1:2], below[2:3], below[3:4], below[4:5].astype(jnp.int32),
        slot.astype(F32) < below[5:6],
    )
    for b in range(2):
        here = block_prev == NBLK - 1 + b
        wp[0, b * Q:(b + 1) * Q, :] = jnp.where(here, re_prev, 0.0).astype(BF16)
        wp[1, b * Q:(b + 1) * Q, :] = jnp.where(here, im_prev, 0.0).astype(BF16)

    rim_noise = jnp.concatenate(
        [below[6:7, 2 * Q:3 * Q], noise8[0:1, :], above[2:3, :], jnp.zeros((5, Q), F32)], axis=0
    ).T
    self_power = self_ref[...] + jnp.sum(rim_power[...] * rim_noise[:, 2:3], axis=0, keepdims=True)
    power_prev = re_prev * re_prev + im_prev * im_prev
    total_prev = jnp.where(
        block_prev == NBLK - 1, rim_noise[:, 0:1],
        jnp.where(block_prev == NBLK, rim_noise[:, 1:2], 0.0),
    )
    self_prev = jnp.sum(power_prev * total_prev, axis=0, keepdims=True)

    edge_first, edge_last = first & (g > 0), last & (g < 3)
    edge = edge_first | edge_last
    lane_q = lax.broadcasted_iota(jnp.int32, (8, Q), 1)
    take_prev = jnp.full((8, Q), edge_first.astype(jnp.int32), jnp.int32)
    take_next = jnp.full((8, Q), edge_last.astype(jnp.int32), jnp.int32)
    take = ((take_prev > 0) & (lane_q >= SECTION) & (lane_q < 2 * SECTION)) | (
        (take_next > 0) & (lane_q >= 2 * SECTION) & (lane_q < 3 * SECTION)
    )
    below_data = (below[6:7, 0:Q], below[6:7, Q:2 * Q])

    def arrived(quarter, dz):
        dx = jnp.where(quarter >= 2, 5 - quarter, quarter)
        xk, zk = wrapped(x + NX - dx, NX), wrapped(z + NZ - dz, NZ)
        k = xk * NZ + zk
        d = dx * NZ + dz

        @pl.when(d > 0)
        def _():
            remote(
                r1.at[:, 0], a.at[k], p2_send.at[d], p2_recv.at[d],
                {"shard_0": xk, "shard_1": zk},
            ).wait_recv()

        @pl.when(edge)
        def _():
            remote(
                r1.at[:, 0], ex.at[k], ex_send.at[0], ex_recv.at[k], at(zh, co, 0, 0, 0)
            ).wait_recv()

        return k

    def edge_template(tile, section, offset):
        u = (lax.broadcasted_iota(jnp.int32, (8, Q), 1).astype(F32) + offset) * (1.0 / BINS)
        base = section * SECTION
        lost = amp_sum = im = None
        for h in range(HALF):
            ca = base + 3 * h
            cp = ca + coef_rows
            a0, a1, a2, p0, p1_, p2_ = (
                jnp.broadcast_to(tile[:, k:k + 1], (8, Q))
                for k in (ca, ca + 1, ca + 2, cp, cp + 1, cp + 2)
            )
            t = p0 + u * (p1_ + u * p2_)
            sn, cs = sin_cos_halves(t - nearest(t))
            amp = a0 + u * (a1 + u * a2)
            asn = amp * sn
            if h == 0:
                amp_sum, lost, im = amp, asn * sn, asn * cs
            else:
                amp_sum, lost, im = amp_sum + amp, lost + asn * sn, im + asn * cs
        return amp_sum - lost, im

    def template_rows(quarter, step):
        for k in [arrived(quarter, step * TILES + i) for i in range(TILES)]:
            tile = jnp.where(take, ex[k, :, 0, :], a[k, :, 0, :])
            own_re, own_im = own_template(tile, 0, coef_rows)
            halves = {block + 1: (own_re[block], own_im[block]) for block in range(NBLK)}
            halves[0] = edge_template(tile, 1, BINS - Q)
            halves[NBLK + 1] = edge_template(tile, 2, 0)
            for block, parts in halves.items():
                for part, half in enumerate(parts):
                    half = half.astype(BF16).astype(F32)
                    template = half + pltpu.roll(half, 4, 0)
                    if block == 0:
                        values = below_data[part]
                    elif block == NBLK + 1:
                        values = above[part:part + 1, :]
                    else:
                        values = data_ref[part:part + 1, (block - 1) * Q:block * Q]
                    res[part, k, :, block * Q:(block + 1) * Q] = values - template

    @pl.loop(0, NX)
    def _(quarter):
        @pl.loop(0, NZ // TILES)
        def _(step):
            template_rows(quarter, step)


    noise_ext = jnp.concatenate([below[6:7, 2 * Q:3 * Q], noise, above[2:3, :]], axis=1)
    corr = jnp.zeros((W, SLOTS), F32)
    corr_prev = jnp.zeros((W, SLOTS), F32)
    upper = lax.broadcasted_iota(jnp.int32, (NXZ // 2, 8, EXT * Q), 1) < 4

    def residual(part):
        pairs = res[part].reshape(NXZ // 2, 2, 8, EXT * Q)
        return jnp.where(upper, pairs[:, 0], pairs[:, 1]).reshape(W, EXT * Q)

    residuals = [residual(part) for part in range(2)]
    for part in range(2):
        weighted = (residuals[part] * noise_ext).astype(BF16)
        corr += jnp.dot(weighted[:, Q:], wt[part], preferred_element_type=F32)
        corr_prev += jnp.dot(weighted[:, 0:2 * Q], wp[part], preferred_element_type=F32)

    def sigmoid(v):
        return 1.0 / (1.0 + jnp.exp(-v))

    accept = jnp.where(slot < bcount[0], sigmoid(corr - 0.5 * self_power), 0.0)
    acc_out[...] = accept
    accept = accept.astype(BF16)
    accept_prev = sigmoid(corr_prev - 0.5 * self_prev).astype(BF16)
    square = jnp.zeros((1, BINS), F32)
    nt = (((1,), (1,)), ((), ()))
    for part in range(2):
        change = lax.dot_general(accept, wt[part, 0:BINS, :], nt, preferred_element_type=F32)
        rim = lax.dot_general(accept_prev, wp[part, Q:2 * Q, :], nt, preferred_element_type=F32)
        new = residuals[part][:, Q:Q + BINS] - change
        new = jnp.concatenate([new[:, 0:Q] - rim, new[:, Q:]], axis=1)
        new_ref[part] = new
        square += jnp.sum(new * new, axis=0, keepdims=True)
    mean = jnp.sum(square, axis=1, keepdims=True) * (1.0 / (2 * W * BINS))
    log_power = jnp.log(mean + 1e-06)
    lane = lax.broadcasted_iota(jnp.int32, (1, Q), 1)
    mine = chebyshev_rows((2 * jnp.full((1, Q), n, jnp.int32) + 1).astype(F32) / NBANDS - 1.0, lane)
    ra[ida] = mine * log_power

    def sum_a(dc, dy):
        d = dc * NY + dy
        return remote(ra.at[ida], ra.at[ida], ra_send.at[d], ra_recv.at[d], peer_y(dc, dy))

    def sum_b(dh, dx, dz):
        d = (dh * NX + dx) * NZ + dz
        return remote(rb.at[idb], rb.at[idb], rb_send.at[d], rb_recv.at[d], peer_plane(dh, dx, dz))

    for member in members_a:
        sum_a(*member).start()

    @pl.when(n >= 0)
    def _():
        bands = lax.broadcasted_iota(jnp.int32, (NCOEF, NBANDS), 1)
        basis = chebyshev_rows(
            (2 * bands + 1).astype(F32) / NBANDS - 1.0,
            lax.broadcasted_iota(jnp.int32, (NCOEF, NBANDS), 0),
        )
        sub = lax.broadcasted_iota(jnp.int32, (NCOEF, Q), 0)
        lane8 = lax.broadcasted_iota(jnp.int32, (NCOEF, Q), 1)
        position = (2 * jnp.full((NCOEF, Q), n, jnp.int32) + 1).astype(F32) / NBANDS - 1.0
        table = jnp.where(lane8 == NCOEF, chebyshev_rows(position, sub), 0.0)
        for k in range(NCOEF):
            column = jnp.sum(basis * basis[k:k + 1, :], axis=1, keepdims=True)
            table = jnp.where(lane8 == k, column, table)
        rows = []
        for k in range(NCOEF):
            root = jnp.sqrt(table[k:k + 1, k:k + 1])
            row = table[k:k + 1, :] / root
            column = table[:, k:k + 1] / root
            rows.append(row)
            table = jnp.where(sub > k, table - column * row, table)
        zrow = jnp.zeros((1, Q), F32)
        for k in reversed(range(NCOEF)):
            row = rows[k]
            known = jnp.sum(jnp.where((lane > k) & (lane < NCOEF), row * zrow, 0.0), axis=1, keepdims=True)
            value = (row[:, NCOEF:NCOEF + 1] - known) / row[:, k:k + 1]
            zrow = jnp.where(lane == k, value, zrow)
        zrow_ref[...] = zrow
        for part in range(2):
            res_out[:, part, :] = new_ref[part]

    for dy in FAR[:-1]:
        p1(dy).wait_send()
    for dx, dz in PLANE[:-1]:
        p2(dx, dz).wait_send()

    @pl.when(has_next)
    def _():
        forward.wait_send()

    @pl.when(has_prev)
    def _():
        backward.wait_send()

    @pl.when(up)
    def _():
        up_copy.wait_send()

    @pl.when(down)
    def _():
        down_copy.wait_send()

    for member in members_a:
        sum_a(*member).wait_recv()
    rb[idb] = jnp.sum(ra[...], axis=0)
    for member in members_b:
        sum_b(*member).start()
    for member in members_a:
        sum_a(*member).wait_send()
    for member in members_b:
        sum_b(*member).wait_recv()
    moment = jnp.sum(rb[...], axis=0)
    fit_out[0] = jnp.sum(zrow_ref[...] * moment)
    for member in members_b:
        sum_b(*member).wait_send()


def write_out(acc_ref, res_ref, acc_out, res_out, sems):
    copies = [
        pltpu.make_async_copy(res_ref, res_out, sems.at[0]),
        pltpu.make_async_copy(acc_ref, acc_out, sems.at[1]),
    ]
    for copy in copies:
        copy.start()
    for copy in copies:
        copy.wait()


def local(data, inv_noise, mbh_amp, mbh_phase, bin_amp, bin_phase, bin_slope, bin_curve, bin_start, bin_count):
    vmem = pl.BlockSpec(memory_space=pltpu.VMEM)
    smem = pl.BlockSpec(memory_space=pltpu.SMEM)
    dma = pltpu.SemaphoreType.DMA
    rows = 3 * HALF
    accept, residual, fit = pl.pallas_call(
        kernel,
        out_shape=(
            jax.ShapeDtypeStruct((W, SLOTS), F32),
            jax.ShapeDtypeStruct((W, 2, BINS), F32),
            jax.ShapeDtypeStruct((1,), F32),
        ),
        in_specs=[pl.BlockSpec(memory_space=pltpu.HBM)] * 9 + [smem],
        out_specs=(vmem, vmem, smem),
        scratch_shapes=[
            pltpu.VMEM((2, BINS), F32),
            pltpu.VMEM((NBLK, Q), BF16),
            pltpu.VMEM((1, SLOTS), F32),
            pltpu.VMEM((1, SLOTS), F32),
            pltpu.VMEM((1, SLOTS), F32),
            pltpu.VMEM((1, SLOTS), F32),
            pltpu.VMEM((1, SLOTS), jnp.int32),
            pltpu.VMEM((40, 1, Q), F32),
            pltpu.VMEM((Q, Q), F32),
            pltpu.VMEM((NY, NXZ, 1, Q), F32),
            pltpu.VMEM((NY, NXZ, 1, Q), F32),
            pltpu.VMEM((NXZ, NY, 1, Q), F32),
            pltpu.VMEM((NXZ, NY, 1, Q), F32),
            pltpu.VMEM((8, SLOTS), F32),
            pltpu.VMEM((8, SLOTS), F32),
            pltpu.VMEM((8, Q), F32),
            pltpu.VMEM((8, Q), F32),
            pltpu.VMEM((2, (NBLK + 1) * Q, SLOTS), BF16),
            pltpu.VMEM((2, 2 * Q, SLOTS), BF16),
            pltpu.VMEM((Q, SLOTS), F32),
            pltpu.VMEM((1, SLOTS), F32),
            pltpu.VMEM((2, NXZ, 8, EXT * Q), F32),
            pltpu.VMEM((2, W, BINS), F32),
            pltpu.VMEM((16, 1, Q), F32),
            pltpu.VMEM((32, 1, Q), F32),
            pltpu.VMEM((1, Q), F32),
            dma((9,)),
            dma((NY - 1,)), dma((NY - 1,)),
            dma((NXZ,)), dma((NXZ,)),
            dma,
            dma((2,)), dma((NXZ,)),
            dma((2,)), dma((2,)),
            dma((16,)), dma((16,)),
            dma((32,)), dma((32,)),
        ],
        compiler_params=pltpu.CompilerParams(
            collective_id=0, has_side_effects=True, vmem_limit_bytes=48 * 1024 * 1024
        ),
        name="gibbs_round",
    )(
        *(
            pltpu.with_memory_space_constraint(v, pltpu.HBM)
            for v in (
                data,
                inv_noise.reshape(NBLK, Q),
                mbh_amp.transpose(1, 2, 0, 3).reshape(rows, 1, Q),
                mbh_phase.transpose(1, 2, 0, 3).reshape(rows, 1, Q),
                bin_amp, bin_phase, bin_slope, bin_curve, bin_start,
            )
        ),
        bin_count,
    )
    accept, residual = pl.pallas_call(
        write_out,
        out_shape=(
            jax.ShapeDtypeStruct((W, SLOTS), F32),
            jax.ShapeDtypeStruct((W, 2, BINS), F32),
        ),
        in_specs=[vmem] * 2,
        out_specs=(pl.BlockSpec(memory_space=pltpu.HBM),) * 2,
        scratch_shapes=[dma((2,))],
        name="write_out",
    )(
        pltpu.with_memory_space_constraint(accept, pltpu.VMEM),
        pltpu.with_memory_space_constraint(residual, pltpu.VMEM),
    )
    return accept, residual, fit


def solution(mesh):
    split = Mesh(mesh.devices.reshape(2, 2, NX, NZ, NY), GROUP_SHARD)
    return jax.shard_map(
        local,
        mesh=split,
        in_specs=(
            P(None, GROUP_SHARD),
            P(GROUP_SHARD),
            P(SHARD, None, None, GROUP),
            P(SHARD, None, None, GROUP),
            P(GROUP_SHARD, None),
            P(GROUP_SHARD, None),
            P(GROUP_SHARD, None),
            P(GROUP_SHARD, None),
            P(GROUP_SHARD, None),
            P(GROUP_SHARD),
        ),
        out_specs=(P(None, GROUP_SHARD), P(None, None, GROUP_SHARD), P(GROUP_SHARD)),
        check_vma=False,
    )
```

```python
import jax
import jax.numpy as jnp
from jax import lax
from jax.experimental import pallas as pl
from jax.experimental.pallas import tpu as pltpu
from jax.sharding import Mesh
from jax.sharding import PartitionSpec as P

W = 64
HALF = 6
Q = 128
BINS = 1024
SLOTS = 512
NCOEF = 8
NX, NZ, NY = 4, 4, 8
NXZ = NX * NZ
NBANDS = 512
NBLK = BINS // Q
EXT = NBLK + 2
SHARD = ("shard_0", "shard_1", "shard_2")
GROUP_SHARD = ("group_0", "group_1", "shard_0", "shard_1", "shard_2")
GROUP = ("group_0", "group_1")
MESH = pl.DeviceIdType.MESH
F32 = jnp.float32
BF16 = jnp.bfloat16

INV_TURN = 0.15915494309189535
TURN_HI = 6.28125
TURN_LO = 0.0019353071795864769
SIN_C = (4.44288283, -7.30824115, 3.60628896, -0.84576359, 0.10920575)
COS_C = (1.4142135, -6.97885099, 5.73946117, -1.88356298, 0.31069818)
COS6_C = (1.41421356, -6.97886411, 5.73988155, -1.888275, 0.33225188, -0.03450217)
SIN1_C = (3.14159258, -5.16770688, 2.55003138, -0.59804517, 0.0772201264)
COS1_C = (0.999999956, -4.93479286, 4.05841191, -1.33188016, 0.21969679)
SECTION = 36
ROT = 108
TILES = 2
FAR = (4, 3, 5, 2, 6, 1, 7, 0)
PLANE = ((2, 2), (2, 1), (1, 2), (2, 3), (3, 2), (1, 1), (1, 3), (3, 1), (3, 3),
         (0, 2), (2, 0), (0, 1), (0, 3), (1, 0), (3, 0), (0, 0))


def poly(coefs, square):
    total = coefs[-1] * square + coefs[-2]
    for c in coefs[-3::-1]:
        total = total * square + c
    return total


def nearest(t):
    return jnp.round(t)


def sin_cos_halves(f):
    square = f * f
    return f * poly(SIN_C, square), poly(COS_C, square)


def chebyshev_rows(x, index):
    terms = [jnp.ones_like(x), x]
    for _ in range(2, NCOEF):
        terms.append(2.0 * x * terms[-1] - terms[-2])
    out = jnp.zeros_like(x)
    for k in range(NCOEF):
        out = jnp.where(index == k, terms[k], out)
    return out


def wave_tile(amp, phase, slope, curve, start, live):
    low = jnp.bitwise_and(start, Q - 1)
    row = lax.broadcasted_iota(jnp.int32, (Q, SLOTS), 0)
    j = jnp.bitwise_and(row - low, Q - 1)
    block = lax.shift_right_logical(start, 7) + (row < low).astype(jnp.int32)
    jf = j.astype(F32)
    angle = phase + slope * jf + curve * jf * jf
    turns = nearest(angle * INV_TURN)
    rest = (angle - turns * TURN_HI) - turns * TURN_LO
    s, c = sin_cos_halves(rest * INV_TURN)
    y = (jf + (0.5 - Q / 2)) * (1.0 / Q)
    half = poly(COS6_C, y * y)
    size = jnp.where(live, amp, 0.0) * (half * half * 0.5)
    re = size * (1.0 - s * s)
    im = size * (s * c)
    return re.astype(BF16).astype(F32), im.astype(BF16).astype(F32), block


def own_template(tile, base, coef_rows):
    v = (lax.broadcasted_iota(jnp.int32, (8, Q), 1).astype(F32) + (NBLK - 1) * Q / 2) * (1.0 / BINS)
    re, im = [None] * NBLK, [None] * NBLK
    for h in range(HALF):
        ca = base + 3 * h
        cp = ca + coef_rows
        a0, a1, a2, p0, p1, p2, g2r, g2i = (
            jnp.broadcast_to(tile[:, k:k + 1], (8, Q))
            for k in (ca, ca + 1, ca + 2, cp, cp + 1, cp + 2, ROT + h, ROT + 8 + h)
        )
        g4r, g4i = 1.0 - 2.0 * (g2i * g2i), 2.0 * (g2i * g2r)
        g6r, g6i = g4r * g2r - g4i * g2i, g4i * g2r + g4r * g2i
        theta = p1 * 0.125 + v * (p2 * 0.25)
        whole = nearest(theta)
        f = theta - whole
        square = f * f
        yi, yr = f * poly(SIN1_C, square), poly(COS1_C, square)
        twice = 2.0 - 4.0 * (yi * yi)
        y_last = None
        center = (p0 + v * (p1 + v * p2)) + (p2 * (1.0 / 256) + 0.5 * whole)
        s, c = sin_cos_halves(center - nearest(center))
        xr, xi = 1.0 - s * s, s * c
        alpha = a0 + v * (a1 + v * a2)
        beta = a1 * 0.125 + v * (a2 * 0.25)
        curve = a2 * (1.0 / 64)
        for i in range(NBLK // 2):
            m = i + 0.5
            if i == 1:
                y_next = ((twice - 1.0) * yr, (twice + 1.0) * yi)
            elif i > 1:
                y_next = (twice * yr - y_last[0], twice * yi - y_last[1])
            if i > 0:
                y_last, (yr, yi) = (yr, yi), y_next
                rr, ri = ((g2r, g2i), (g4r, g4i), (g6r, g6i))[i - 1]
                xr, xi = xr * rr - xi * ri, xi * rr + xr * ri
            size, tilt = alpha + curve * (m * m), beta * m
            rr_, ii_, ri_, ir_ = xr * yr, xi * yi, xr * yi, xi * yr
            for block, amp, x_re, x_im in (
                (NBLK // 2 + i, size + tilt, rr_ - ii_, ir_ + ri_),
                (NBLK // 2 - 1 - i, size - tilt, rr_ + ii_, ir_ - ri_),
            ):
                if h == 0:
                    re[block], im[block] = amp * x_re, amp * x_im
                else:
                    re[block], im[block] = re[block] + amp * x_re, im[block] + amp * x_im
    return re, im


def wrapped(v, n):
    return jnp.where(v >= n, v - n, v)


def kernel(
    data_hbm, noise_hbm, amp_hbm, phase_hbm, bamp_hbm, bphase_hbm, bslope_hbm, bcurve_hbm,
    bstart_hbm, bcount,
    acc_out, res_out, fit_out,
    data_ref, noise_ref, bamp, bphase, bslope, bcurve, bstart,
    xm, m, s1, r1, a, pk, fw, bk, bw, wt, wp, rim_power, self_ref, res, new_ref, ra, rb,
    zrow_ref,
    in_sem, p1_send, p1_recv, p2_send, p2_recv, ex_send, nb_send, nb_recv,
    ra_send, ra_recv, rb_send, rb_recv,
):
    coef_rows = 3 * HALF
    inputs = [
        (amp_hbm, xm.at[0:coef_rows]), (phase_hbm, xm.at[coef_rows:2 * coef_rows]),
        (data_hbm, data_ref), (noise_hbm, noise_ref), (bamp_hbm, bamp), (bphase_hbm, bphase),
        (bslope_hbm, bslope), (bcurve_hbm, bcurve), (bstart_hbm, bstart),
    ]
    fetches = [
        pltpu.make_async_copy(src, dst, in_sem.at[i]) for i, (src, dst) in enumerate(inputs)
    ]
    for fetch in fetches:
        fetch.start()

    zh, co = lax.axis_index("group_0"), lax.axis_index("group_1")
    x, z, y = lax.axis_index("shard_0"), lax.axis_index("shard_1"), lax.axis_index("shard_2")
    g = zh * 2 + co
    s = x * (NZ * NY) + z * NY + y
    n = g * (NBANDS // 4) + s
    xz = x * NZ + z
    ida = co * NY + y
    idb = zh * NXZ + xz
    has_prev, has_next = n > 0, n < NBANDS - 1
    first, last = s == 0, s == NBANDS // 4 - 1
    up = (y == 0) & (g < 3)
    down = (y == NY - 1) & (g > 0)

    def at(group0, group1, xi, zi, yi):
        return {
            "group_0": group0, "group_1": group1, "shard_0": xi, "shard_1": zi, "shard_2": yi,
        }

    turn_y = y == NY - 1
    turn_z = turn_y & (z == NZ - 1)
    turn_x = turn_z & (x == NX - 1)
    turn_c = turn_x & (co == 1)
    above_id = at(
        jnp.where(turn_c, 1 - zh, zh), jnp.where(turn_x, 1 - co, co),
        jnp.where(turn_z, wrapped(x + 1, NX), x), jnp.where(turn_y, wrapped(z + 1, NZ), z),
        wrapped(y + 1, NY),
    )
    back_y = y == 0
    back_z = back_y & (z == 0)
    back_x = back_z & (x == 0)
    back_c = back_x & (co == 0)
    below_id = at(
        jnp.where(back_c, 1 - zh, zh), jnp.where(back_x, 1 - co, co),
        jnp.where(back_z, wrapped(x + NX - 1, NX), x),
        jnp.where(back_y, wrapped(z + NZ - 1, NZ), z),
        wrapped(y + NY - 1, NY),
    )
    next_zh, next_co = jnp.where(co == 1, 1 - zh, zh), 1 - co
    prev_zh, prev_co = jnp.where(co == 0, 1 - zh, zh), 1 - co

    barrier = pltpu.get_barrier_semaphore()

    def greet(where):
        pl.semaphore_signal(barrier, inc=1, device_id=where, device_id_type=MESH)

    def peer_y(dc, dy):
        return {"group_1": 1 - co if dc else co, "shard_2": wrapped(y + dy, NY)}

    def peer_plane(dh, dx, dz):
        return {
            "group_0": 1 - zh if dh else zh,
            "shard_0": wrapped(x + dx, NX), "shard_1": wrapped(z + dz, NZ),
        }

    members_a = [(dc, dy) for dy in FAR for dc in (1, 0) if (dc, dy) != (0, 0)]
    members_b = [(dh, dx, dz) for dx, dz in PLANE for dh in (1, 0) if (dh, dx, dz) != (0, 0, 0)]

    @pl.when(first & (g > 0))
    def _():
        for k in range(NXZ):
            greet(at(prev_zh, prev_co, k // NZ, k % NZ, 0))

    @pl.when(last & (g < 3))
    def _():
        for k in range(NXZ):
            greet(at(next_zh, next_co, k // NZ, k % NZ, NY - 1))

    for member in members_b:
        greet(peer_plane(*member))
    for member in members_a:
        greet(peer_y(*member))

    @pl.when(has_prev)
    def _():
        greet(below_id)

    @pl.when(has_next)
    def _():
        greet(above_id)

    for fetch in fetches:
        fetch.wait()
    amps, turns = xm[0:coef_rows, 0, :], xm[coef_rows:2 * coef_rows, 0, :] * INV_TURN
    bend = jnp.concatenate([turns[3 * h + 2:3 * h + 3, :] for h in range(HALF)], axis=0)
    bend = bend * (1.0 / 32)
    sn, cs = sin_cos_halves(bend - nearest(bend))
    xm[coef_rows:2 * coef_rows, 0, :] = turns
    own = xm[:, 0, :]
    message = [own, pltpu.roll(own, 1, 1), pltpu.roll(own, Q - 1, 1)]
    xm[0:HALF, 0, :] = 1.0 - sn * sn
    xm[8:8 + HALF, 0, :] = sn * cs
    xm[16:24, 0, :] = jnp.zeros((8, Q), F32)
    m[...] = jnp.concatenate([part[0:2 * coef_rows] for part in message] + [xm[0:Q - 6 * coef_rows, 0, :]], axis=0).T
    for k in range(NY):
        s1[k, :, 0, :] = m[pl.ds(k, NXZ, stride=NY), :]

    noise8 = noise_ref[...].astype(F32)
    noise = jnp.concatenate([noise8[b:b + 1, :] for b in range(NBLK)], axis=1)
    pk[...] = jnp.zeros_like(pk)
    pk[0:1, :] = bamp[...]
    pk[1:2, :] = bphase[...]
    pk[2:3, :] = bslope[...]
    pk[3:4, :] = bcurve[...]
    pk[4:5, :] = bstart[...].astype(F32)
    pk[5:6, :] = jnp.full((1, SLOTS), bcount[0], jnp.int32).astype(F32)
    pk[6:7, 0:Q] = data_ref[0:1, BINS - Q:]
    pk[6:7, Q:2 * Q] = data_ref[1:2, BINS - Q:]
    pk[6:7, 2 * Q:3 * Q] = noise8[NBLK - 1:NBLK, :]
    bk[...] = jnp.zeros_like(bk)
    bk[0:2, :] = data_ref[:, 0:Q]
    bk[2:3, :] = noise8[0:1, :]

    slot = lax.broadcasted_iota(jnp.int32, (1, SLOTS), 1)
    waits = 15 + 31 + has_prev.astype(jnp.int32) + has_next.astype(jnp.int32)
    pl.semaphore_wait(barrier, waits + up.astype(jnp.int32) + down.astype(jnp.int32))

    def remote(src, dst, send, recv, where):
        return pltpu.make_async_remote_copy(
            src_ref=src, dst_ref=dst, send_sem=send, recv_sem=recv, device_id=where,
            device_id_type=MESH,
        )

    slot_y = (y % 2) * (NY // 2) + y // 2

    def p1(dy):
        k = wrapped(y + dy, NY)
        return remote(
            s1.at[k], r1.at[slot_y], p1_send, p1_recv, {"shard_2": k}
        )

    for dy in FAR[:-1]:
        p1(dy).start()

    forward = remote(pk, fw, nb_send.at[0], nb_recv.at[0], above_id)
    backward = remote(bk, bw, nb_send.at[1], nb_recv.at[1], below_id)

    @pl.when(has_next)
    def _():
        forward.start()

    @pl.when(has_prev)
    def _():
        backward.start()

    r1[slot_y] = s1[y]

    @pl.when(n >= 0)
    def _():
        re_own, im_own, block_own = wave_tile(
            bamp[...], bphase[...], bslope[...], bcurve[...], bstart[...], slot < bcount[0]
        )
        noise_columns = jnp.concatenate([noise8, jnp.zeros((8, Q), F32)], axis=0).T
        total = jnp.zeros((Q, SLOTS), F32)
        for b in range(NBLK + 1):
            here = block_own == b
            wt[0, b * Q:(b + 1) * Q, :] = jnp.where(here, re_own, 0.0).astype(BF16)
            wt[1, b * Q:(b + 1) * Q, :] = jnp.where(here, im_own, 0.0).astype(BF16)
            if b < NBLK:
                total = jnp.where(here, noise_columns[:, b:b + 1], total)
        power = re_own * re_own + im_own * im_own
        rim_power[...] = jnp.where(block_own == NBLK, power, 0.0)
        self_ref[...] = jnp.sum(power * total, axis=0, keepdims=True)

    p1_all = remote(r1.at[0:NY - 1], r1.at[0:NY - 1], p1_send, p1_recv, {"shard_2": y})
    p1_all.wait_recv()

    up_copy = remote(
        r1.at[:, 0], a.at[xz, 1], ex_send.at[0], p2_recv.at[xz], at(next_zh, next_co, 0, 0, 0)
    )
    down_copy = remote(
        r1.at[:, NXZ - 1], a.at[xz, 1], ex_send.at[1], p2_recv.at[xz],
        at(prev_zh, prev_co, NX - 1, NZ - 1, NY - 1),
    )

    @pl.when(up)
    def _():
        up_copy.start()

    @pl.when(down)
    def _():
        down_copy.start()

    def p2(dx, dz):
        xk, zk = wrapped(x + dx, NX), wrapped(z + dz, NZ)
        return remote(
            r1.at[:, xk * NZ + zk], a.at[xz, 0], p2_send, p2_recv.at[xz],
            {"shard_0": xk, "shard_1": zk},
        )

    for dx, dz in PLANE[:-1]:
        p2(dx, dz).start()
    a[xz, 0] = r1[:, xz]

    @pl.when(has_prev)
    def _():
        forward.wait_recv()

    @pl.when(has_next)
    def _():
        backward.wait_recv()

    below = jnp.where(jnp.full((8, SLOTS), n, jnp.int32) > 0, fw[...], 0.0)
    above = jnp.where(jnp.full((8, Q), n, jnp.int32) < NBANDS - 1, bw[...], 0.0)
    re_prev, im_prev, block_prev = wave_tile(
        below[0:1], below[1:2], below[2:3], below[3:4], below[4:5].astype(jnp.int32),
        slot.astype(F32) < below[5:6],
    )
    for b in range(2):
        here = block_prev == NBLK - 1 + b
        wp[0, b * Q:(b + 1) * Q, :] = jnp.where(here, re_prev, 0.0).astype(BF16)
        wp[1, b * Q:(b + 1) * Q, :] = jnp.where(here, im_prev, 0.0).astype(BF16)

    rim_noise = jnp.concatenate(
        [below[6:7, 2 * Q:3 * Q], noise8[0:1, :], above[2:3, :], jnp.zeros((5, Q), F32)], axis=0
    ).T
    self_power = self_ref[...] + jnp.sum(rim_power[...] * rim_noise[:, 2:3], axis=0, keepdims=True)
    power_prev = re_prev * re_prev + im_prev * im_prev
    total_prev = jnp.where(
        block_prev == NBLK - 1, rim_noise[:, 0:1],
        jnp.where(block_prev == NBLK, rim_noise[:, 1:2], 0.0),
    )
    self_prev = jnp.sum(power_prev * total_prev, axis=0, keepdims=True)

    edge_first, edge_last = first & (g > 0), last & (g < 3)
    edge = edge_first | edge_last
    lane_q = lax.broadcasted_iota(jnp.int32, (8, Q), 1)
    take_prev = jnp.full((8, Q), edge_first.astype(jnp.int32), jnp.int32)
    take_next = jnp.full((8, Q), edge_last.astype(jnp.int32), jnp.int32)
    take = ((take_prev > 0) & (lane_q >= SECTION) & (lane_q < 2 * SECTION)) | (
        (take_next > 0) & (lane_q >= 2 * SECTION) & (lane_q < 3 * SECTION)
    )
    below_data = (below[6:7, 0:Q], below[6:7, Q:2 * Q])

    def arrived(quarter, dz):
        dx = jnp.where(quarter >= 2, 5 - quarter, quarter)
        xk, zk = wrapped(x + NX - dx, NX), wrapped(z + NZ - dz, NZ)
        k = xk * NZ + zk
        d = dx * NZ + dz

        def wait(part):
            remote(part, part, p2_send, p2_recv.at[k], {"shard_2": y}).wait_recv()

        @pl.when((d > 0) & edge)
        def _():
            wait(a.at[k])

        @pl.when((d > 0) & jnp.logical_not(edge))
        def _():
            wait(a.at[k, 0])

        @pl.when((d == 0) & edge)
        def _():
            wait(a.at[k, 1])

        return k

    def edge_template(tile, section, offset):
        u = (lax.broadcasted_iota(jnp.int32, (8, Q), 1).astype(F32) + offset) * (1.0 / BINS)
        base = section * SECTION
        lost = amp_sum = im = None
        for h in range(HALF):
            ca = base + 3 * h
            cp = ca + coef_rows
            a0, a1, a2, p0, p1_, p2_ = (
                jnp.broadcast_to(tile[:, k:k + 1], (8, Q))
                for k in (ca, ca + 1, ca + 2, cp, cp + 1, cp + 2)
            )
            t = p0 + u * (p1_ + u * p2_)
            sn, cs = sin_cos_halves(t - nearest(t))
            amp = a0 + u * (a1 + u * a2)
            asn = amp * sn
            if h == 0:
                amp_sum, lost, im = amp, asn * sn, asn * cs
            else:
                amp_sum, lost, im = amp_sum + amp, lost + asn * sn, im + asn * cs
        return amp_sum - lost, im

    def template_rows(quarter, step):
        for k in [arrived(quarter, step * TILES + i) for i in range(TILES)]:
            tile = jnp.where(take, a[k, 1, :, 0, :], a[k, 0, :, 0, :])
            own_re, own_im = own_template(tile, 0, coef_rows)
            halves = {block + 1: (own_re[block], own_im[block]) for block in range(NBLK)}
            halves[0] = edge_template(tile, 1, BINS - Q)
            halves[NBLK + 1] = edge_template(tile, 2, 0)
            for block, parts in halves.items():
                for part, half in enumerate(parts):
                    half = half.astype(BF16).astype(F32)
                    template = half + pltpu.roll(half, 4, 0)
                    if block == 0:
                        values = below_data[part]
                    elif block == NBLK + 1:
                        values = above[part:part + 1, :]
                    else:
                        values = data_ref[part:part + 1, (block - 1) * Q:block * Q]
                    res[part, k, :, block * Q:(block + 1) * Q] = values - template

    @pl.loop(0, NX)
    def _(quarter):
        @pl.loop(0, NZ // TILES)
        def _(step):
            template_rows(quarter, step)


    noise_ext = jnp.concatenate([below[6:7, 2 * Q:3 * Q], noise, above[2:3, :]], axis=1)
    corr = jnp.zeros((W, SLOTS), F32)
    corr_prev = jnp.zeros((W, SLOTS), F32)
    upper = lax.broadcasted_iota(jnp.int32, (NXZ // 2, 8, EXT * Q), 1) < 4

    def residual(part):
        pairs = res[part].reshape(NXZ // 2, 2, 8, EXT * Q)
        return jnp.where(upper, pairs[:, 0], pairs[:, 1]).reshape(W, EXT * Q)

    residuals = [residual(part) for part in range(2)]
    for part in range(2):
        weighted = (residuals[part] * noise_ext).astype(BF16)
        corr += jnp.dot(weighted[:, Q:], wt[part], preferred_element_type=F32)
        corr_prev += jnp.dot(weighted[:, 0:2 * Q], wp[part], preferred_element_type=F32)

    def sigmoid(v):
        return 1.0 / (1.0 + jnp.exp(-v))

    accept = jnp.where(slot < bcount[0], sigmoid(corr - 0.5 * self_power), 0.0)
    acc_out[...] = accept
    accept = accept.astype(BF16)
    accept_prev = sigmoid(corr_prev - 0.5 * self_prev).astype(BF16)
    square = jnp.zeros((1, BINS), F32)
    nt = (((1,), (1,)), ((), ()))
    for part in range(2):
        change = lax.dot_general(accept, wt[part, 0:BINS, :], nt, preferred_element_type=F32)
        rim = lax.dot_general(accept_prev, wp[part, Q:2 * Q, :], nt, preferred_element_type=F32)
        new = residuals[part][:, Q:Q + BINS] - change
        new = jnp.concatenate([new[:, 0:Q] - rim, new[:, Q:]], axis=1)
        new_ref[part] = new
        square += jnp.sum(new * new, axis=0, keepdims=True)
    mean = jnp.sum(square, axis=1, keepdims=True) * (1.0 / (2 * W * BINS))
    log_power = jnp.log(mean + 1e-06)
    lane = lax.broadcasted_iota(jnp.int32, (1, Q), 1)
    mine = chebyshev_rows((2 * jnp.full((1, Q), n, jnp.int32) + 1).astype(F32) / NBANDS - 1.0, lane)
    ra[ida] = mine * log_power

    def sum_a(dc, dy):
        return remote(ra.at[ida], ra.at[ida], ra_send, ra_recv, peer_y(dc, dy))

    def sum_b(dh, dx, dz):
        return remote(rb.at[idb], rb.at[idb], rb_send, rb_recv, peer_plane(dh, dx, dz))

    sum_a_all = remote(ra.at[0:15], ra.at[0:15], ra_send, ra_recv, {"shard_2": y})
    sum_b_all = remote(rb.at[0:31], rb.at[0:31], rb_send, rb_recv, {"shard_2": y})

    for member in members_a:
        sum_a(*member).start()

    @pl.when(n >= 0)
    def _():
        bands = lax.broadcasted_iota(jnp.int32, (NCOEF, NBANDS), 1)
        basis = chebyshev_rows(
            (2 * bands + 1).astype(F32) / NBANDS - 1.0,
            lax.broadcasted_iota(jnp.int32, (NCOEF, NBANDS), 0),
        )
        sub = lax.broadcasted_iota(jnp.int32, (NCOEF, Q), 0)
        lane8 = lax.broadcasted_iota(jnp.int32, (NCOEF, Q), 1)
        position = (2 * jnp.full((NCOEF, Q), n, jnp.int32) + 1).astype(F32) / NBANDS - 1.0
        table = jnp.where(lane8 == NCOEF, chebyshev_rows(position, sub), 0.0)
        for k in range(NCOEF):
            column = jnp.sum(basis * basis[k:k + 1, :], axis=1, keepdims=True)
            table = jnp.where(lane8 == k, column, table)
        rows = []
        for k in range(NCOEF):
            root = jnp.sqrt(table[k:k + 1, k:k + 1])
            row = table[k:k + 1, :] / root
            column = table[:, k:k + 1] / root
            rows.append(row)
            table = jnp.where(sub > k, table - column * row, table)
        zrow = jnp.zeros((1, Q), F32)
        for k in reversed(range(NCOEF)):
            row = rows[k]
            known = jnp.sum(jnp.where((lane > k) & (lane < NCOEF), row * zrow, 0.0), axis=1, keepdims=True)
            value = (row[:, NCOEF:NCOEF + 1] - known) / row[:, k:k + 1]
            zrow = jnp.where(lane == k, value, zrow)
        zrow_ref[...] = zrow
        for part in range(2):
            res_out[:, part, :] = new_ref[part]

    p1_all.wait_send()
    remote(
        a.at[0:NXZ - 1, 0], a.at[0:NXZ - 1, 0], p2_send, p2_recv.at[xz], {"shard_2": y}
    ).wait_send()

    @pl.when(has_next)
    def _():
        forward.wait_send()

    @pl.when(has_prev)
    def _():
        backward.wait_send()

    @pl.when(up)
    def _():
        up_copy.wait_send()

    @pl.when(down)
    def _():
        down_copy.wait_send()

    sum_a_all.wait_recv()
    rb[idb] = jnp.sum(ra[...], axis=0)
    for member in members_b:
        sum_b(*member).start()
    sum_a_all.wait_send()
    sum_b_all.wait_recv()
    moment = jnp.sum(rb[...], axis=0)
    fit = jnp.sum(zrow_ref[...] * moment, axis=1, keepdims=True)
    fit_out[...] = jnp.broadcast_to(fit, (1, Q))
    sum_b_all.wait_send()


def write_out(acc_ref, res_ref, fit_ref, acc_out, res_out, fit_out, sems):
    copies = [pltpu.make_async_copy(acc_ref, acc_out, sems.at[4])]
    for i in range(4):
        rows = pl.ds(i * (W // 4), W // 4)
        copies.append(pltpu.make_async_copy(res_ref.at[rows], res_out.at[rows], sems.at[i]))
    for copy in copies:
        copy.start()
    fit_out[0] = fit_ref[0, 0]
    for copy in copies:
        copy.wait()


def local(data, inv_noise, mbh_amp, mbh_phase, bin_amp, bin_phase, bin_slope, bin_curve, bin_start, bin_count):
    vmem = pl.BlockSpec(memory_space=pltpu.VMEM)
    smem = pl.BlockSpec(memory_space=pltpu.SMEM)
    dma = pltpu.SemaphoreType.DMA
    rows = 3 * HALF
    accept, residual, fit = pl.pallas_call(
        kernel,
        out_shape=(
            jax.ShapeDtypeStruct((W, SLOTS), F32),
            jax.ShapeDtypeStruct((W, 2, BINS), F32),
            jax.ShapeDtypeStruct((1, Q), F32),
        ),
        in_specs=[pl.BlockSpec(memory_space=pltpu.HBM)] * 9 + [smem],
        out_specs=(vmem, vmem, vmem),
        scratch_shapes=[
            pltpu.VMEM((2, BINS), F32),
            pltpu.VMEM((NBLK, Q), BF16),
            pltpu.VMEM((1, SLOTS), F32),
            pltpu.VMEM((1, SLOTS), F32),
            pltpu.VMEM((1, SLOTS), F32),
            pltpu.VMEM((1, SLOTS), F32),
            pltpu.VMEM((1, SLOTS), jnp.int32),
            pltpu.VMEM((40, 1, Q), F32),
            pltpu.VMEM((Q, Q), F32),
            pltpu.VMEM((NY, NXZ, 1, Q), F32),
            pltpu.VMEM((NY, NXZ, 1, Q), F32),
            pltpu.VMEM((NXZ, 2, NY, 1, Q), F32),
            pltpu.VMEM((8, SLOTS), F32),
            pltpu.VMEM((8, SLOTS), F32),
            pltpu.VMEM((8, Q), F32),
            pltpu.VMEM((8, Q), F32),
            pltpu.VMEM((2, (NBLK + 1) * Q, SLOTS), BF16),
            pltpu.VMEM((2, 2 * Q, SLOTS), BF16),
            pltpu.VMEM((Q, SLOTS), F32),
            pltpu.VMEM((1, SLOTS), F32),
            pltpu.VMEM((2, NXZ, 8, EXT * Q), F32),
            pltpu.VMEM((2, W, BINS), F32),
            pltpu.VMEM((16, 1, Q), F32),
            pltpu.VMEM((32, 1, Q), F32),
            pltpu.VMEM((1, Q), F32),
            dma((9,)), dma, dma, dma, dma((NXZ,)), dma((2,)), dma((2,)), dma((2,)),
            dma, dma, dma, dma,
        ],
        compiler_params=pltpu.CompilerParams(
            collective_id=0, has_side_effects=True, vmem_limit_bytes=48 * 1024 * 1024
        ),
        name="gibbs_round",
    )(
        *(
            pltpu.with_memory_space_constraint(v, pltpu.HBM)
            for v in (
                data,
                inv_noise.reshape(NBLK, Q),
                mbh_amp.transpose(1, 2, 0, 3).reshape(rows, 1, Q),
                mbh_phase.transpose(1, 2, 0, 3).reshape(rows, 1, Q),
                bin_amp, bin_phase, bin_slope, bin_curve, bin_start,
            )
        ),
        bin_count,
    )
    accept, residual, fit = pl.pallas_call(
        write_out,
        out_shape=(
            jax.ShapeDtypeStruct((W, SLOTS), F32),
            jax.ShapeDtypeStruct((W, 2, BINS), F32),
            jax.ShapeDtypeStruct((1,), F32),
        ),
        in_specs=[vmem] * 3,
        out_specs=(pl.BlockSpec(memory_space=pltpu.HBM),) * 2 + (smem,),
        scratch_shapes=[dma((5,))],
        name="write_out",
    )(
        pltpu.with_memory_space_constraint(accept, pltpu.VMEM),
        pltpu.with_memory_space_constraint(residual, pltpu.VMEM),
        pltpu.with_memory_space_constraint(fit, pltpu.VMEM),
    )
    return accept, residual, fit


def solution(mesh):
    split = Mesh(mesh.devices.reshape(2, 2, NX, NZ, NY), GROUP_SHARD)
    return jax.shard_map(
        local,
        mesh=split,
        in_specs=(
            P(None, GROUP_SHARD),
            P(GROUP_SHARD),
            P(SHARD, None, None, GROUP),
            P(SHARD, None, None, GROUP),
            P(GROUP_SHARD, None),
            P(GROUP_SHARD, None),
            P(GROUP_SHARD, None),
            P(GROUP_SHARD, None),
            P(GROUP_SHARD, None),
            P(GROUP_SHARD),
        ),
        out_specs=(P(None, GROUP_SHARD), P(None, None, GROUP_SHARD), P(GROUP_SHARD)),
        check_vma=False,
    )
```

```python
import jax
import jax.numpy as jnp
from jax import lax
from jax.experimental import pallas as pl
from jax.experimental.pallas import tpu as pltpu
from jax.sharding import Mesh
from jax.sharding import PartitionSpec as P

W = 64
HALF = 6
Q = 128
BINS = 1024
SLOTS = 512
NCOEF = 8
NX, NZ, NY = 4, 4, 8
NXZ = NX * NZ
NBANDS = 512
NBLK = BINS // Q
EXT = NBLK + 2
SHARD = ("shard_0", "shard_1", "shard_2")
GROUP_SHARD = ("group_0", "group_1", "shard_0", "shard_1", "shard_2")
GROUP = ("group_0", "group_1")
MESH = pl.DeviceIdType.MESH
F32 = jnp.float32
BF16 = jnp.bfloat16

INV_TURN = 0.15915494309189535
TURN_HI = 6.28125
TURN_LO = 0.0019353071795864769
SIN_C = (4.44288283, -7.30824115, 3.60628896, -0.84576359, 0.10920575)
COS_C = (1.4142135, -6.97885099, 5.73946117, -1.88356298, 0.31069818)
COS6_C = (1.41421356, -6.97886411, 5.73988155, -1.888275, 0.33225188, -0.03450217)
SIN1_C = (3.14159258, -5.16770688, 2.55003138, -0.59804517, 0.0772201264)
COS1_C = (0.999999956, -4.93479286, 4.05841191, -1.33188016, 0.21969679)
SECTION = 36
ROT = 108
TILES = 2
FAR = (4, 3, 5, 2, 6, 1, 7, 0)
PLANE = ((2, 2), (2, 1), (1, 2), (2, 3), (3, 2), (1, 1), (1, 3), (3, 1), (3, 3),
         (0, 2), (2, 0), (0, 1), (0, 3), (1, 0), (3, 0), (0, 0))


def poly(coefs, square):
    total = coefs[-1] * square + coefs[-2]
    for c in coefs[-3::-1]:
        total = total * square + c
    return total


def nearest(t):
    return jnp.round(t)


def sin_cos_halves(f):
    square = f * f
    return f * poly(SIN_C, square), poly(COS_C, square)


def chebyshev_rows(x, index):
    terms = [jnp.ones_like(x), x]
    for _ in range(2, NCOEF):
        terms.append(2.0 * x * terms[-1] - terms[-2])
    out = jnp.zeros_like(x)
    for k in range(NCOEF):
        out = jnp.where(index == k, terms[k], out)
    return out


def wave_tile(amp, phase, slope, curve, start, live):
    low = jnp.bitwise_and(start, Q - 1)
    row = lax.broadcasted_iota(jnp.int32, (Q, SLOTS), 0)
    j = jnp.bitwise_and(row - low, Q - 1)
    block = lax.shift_right_logical(start, 7) + (row < low).astype(jnp.int32)
    jf = j.astype(F32)
    angle = phase + slope * jf + curve * jf * jf
    turns = nearest(angle * INV_TURN)
    rest = (angle - turns * TURN_HI) - turns * TURN_LO
    s, c = sin_cos_halves(rest * INV_TURN)
    y = (jf + (0.5 - Q / 2)) * (1.0 / Q)
    half = poly(COS6_C, y * y)
    size = jnp.where(live, amp, 0.0) * (half * half * 0.5)
    re = size * (1.0 - s * s)
    im = size * (s * c)
    return re.astype(BF16).astype(F32), im.astype(BF16).astype(F32), block


def own_template(tile, base, coef_rows):
    v = (lax.broadcasted_iota(jnp.int32, (8, Q), 1).astype(F32) + (NBLK - 1) * Q / 2) * (1.0 / BINS)
    re, im = [None] * NBLK, [None] * NBLK
    for h in range(HALF):
        ca = base + 3 * h
        cp = ca + coef_rows
        a0, a1, a2, p0, p1, p2, g2r, g2i = (
            jnp.broadcast_to(tile[:, k:k + 1], (8, Q))
            for k in (ca, ca + 1, ca + 2, cp, cp + 1, cp + 2, ROT + h, ROT + 8 + h)
        )
        g4r, g4i = 1.0 - 2.0 * (g2i * g2i), 2.0 * (g2i * g2r)
        g6r, g6i = g4r * g2r - g4i * g2i, g4i * g2r + g4r * g2i
        theta = p1 * 0.125 + v * (p2 * 0.25)
        whole = nearest(theta)
        f = theta - whole
        square = f * f
        yi, yr = f * poly(SIN1_C, square), poly(COS1_C, square)
        twice = 2.0 - 4.0 * (yi * yi)
        y_last = None
        center = (p0 + v * (p1 + v * p2)) + (p2 * (1.0 / 256) + 0.5 * whole)
        s, c = sin_cos_halves(center - nearest(center))
        xr, xi = 1.0 - s * s, s * c
        alpha = a0 + v * (a1 + v * a2)
        beta = a1 * 0.125 + v * (a2 * 0.25)
        curve = a2 * (1.0 / 64)
        for i in range(NBLK // 2):
            m = i + 0.5
            if i == 1:
                y_next = ((twice - 1.0) * yr, (twice + 1.0) * yi)
            elif i > 1:
                y_next = (twice * yr - y_last[0], twice * yi - y_last[1])
            if i > 0:
                y_last, (yr, yi) = (yr, yi), y_next
                rr, ri = ((g2r, g2i), (g4r, g4i), (g6r, g6i))[i - 1]
                xr, xi = xr * rr - xi * ri, xi * rr + xr * ri
            size, tilt = alpha + curve * (m * m), beta * m
            rr_, ii_, ri_, ir_ = xr * yr, xi * yi, xr * yi, xi * yr
            for block, amp, x_re, x_im in (
                (NBLK // 2 + i, size + tilt, rr_ - ii_, ir_ + ri_),
                (NBLK // 2 - 1 - i, size - tilt, rr_ + ii_, ir_ - ri_),
            ):
                if h == 0:
                    re[block], im[block] = amp * x_re, amp * x_im
                else:
                    re[block], im[block] = re[block] + amp * x_re, im[block] + amp * x_im
    return re, im


def wrapped(v, n):
    return jnp.where(v >= n, v - n, v)


def kernel(
    data_hbm, noise_hbm, amp_hbm, phase_hbm, bamp_hbm, bphase_hbm, bslope_hbm, bcurve_hbm,
    bstart_hbm, bcount,
    acc_out, res_out, fit_out,
    data_ref, noise_ref, bamp, bphase, bslope, bcurve, bstart,
    xm, m, s1, r1, a, pk, fw, bk, bw, wt, wp, rim_power, self_ref, res, new_ref, ra, rb,
    zrow_ref,
    in_sem, p1_send, p1_recv, p2_send, p2_recv, ex_send, nb_send, nb_recv,
    ra_send, ra_recv, rb_send, rb_recv,
):
    coef_rows = 3 * HALF
    inputs = [
        (amp_hbm, xm.at[0:coef_rows]), (phase_hbm, xm.at[coef_rows:2 * coef_rows]),
        (data_hbm, data_ref), (noise_hbm, noise_ref), (bamp_hbm, bamp), (bphase_hbm, bphase),
        (bslope_hbm, bslope), (bcurve_hbm, bcurve), (bstart_hbm, bstart),
    ]
    fetches = [
        pltpu.make_async_copy(src, dst, in_sem.at[i]) for i, (src, dst) in enumerate(inputs)
    ]
    for fetch in fetches:
        fetch.start()

    zh, co = lax.axis_index("group_0"), lax.axis_index("group_1")
    x, z, y = lax.axis_index("shard_0"), lax.axis_index("shard_1"), lax.axis_index("shard_2")
    g = zh * 2 + co
    s = x * (NZ * NY) + z * NY + y
    n = g * (NBANDS // 4) + s
    xz = x * NZ + z
    ida = co * NY + y
    idb = zh * NXZ + xz
    has_prev, has_next = n > 0, n < NBANDS - 1
    first, last = s == 0, s == NBANDS // 4 - 1
    up = (y == 0) & (g < 3)
    down = (y == NY - 1) & (g > 0)

    def at(group0, group1, xi, zi, yi):
        return {
            "group_0": group0, "group_1": group1, "shard_0": xi, "shard_1": zi, "shard_2": yi,
        }

    turn_y = y == NY - 1
    turn_z = turn_y & (z == NZ - 1)
    turn_x = turn_z & (x == NX - 1)
    turn_c = turn_x & (co == 1)
    above_id = at(
        jnp.where(turn_c, 1 - zh, zh), jnp.where(turn_x, 1 - co, co),
        jnp.where(turn_z, wrapped(x + 1, NX), x), jnp.where(turn_y, wrapped(z + 1, NZ), z),
        wrapped(y + 1, NY),
    )
    back_y = y == 0
    back_z = back_y & (z == 0)
    back_x = back_z & (x == 0)
    back_c = back_x & (co == 0)
    below_id = at(
        jnp.where(back_c, 1 - zh, zh), jnp.where(back_x, 1 - co, co),
        jnp.where(back_z, wrapped(x + NX - 1, NX), x),
        jnp.where(back_y, wrapped(z + NZ - 1, NZ), z),
        wrapped(y + NY - 1, NY),
    )
    next_zh, next_co = jnp.where(co == 1, 1 - zh, zh), 1 - co
    prev_zh, prev_co = jnp.where(co == 0, 1 - zh, zh), 1 - co

    barrier = pltpu.get_barrier_semaphore()

    def greet(where):
        pl.semaphore_signal(barrier, inc=1, device_id=where, device_id_type=MESH)

    def peer_y(dc, dy):
        return {"group_1": 1 - co if dc else co, "shard_2": wrapped(y + dy, NY)}

    def peer_plane(dh, dx, dz):
        return {
            "group_0": 1 - zh if dh else zh,
            "shard_0": wrapped(x + dx, NX), "shard_1": wrapped(z + dz, NZ),
        }

    members_a = [(dc, dy) for dy in FAR for dc in (1, 0) if (dc, dy) != (0, 0)]
    members_b = [(dh, dx, dz) for dx, dz in PLANE for dh in (1, 0) if (dh, dx, dz) != (0, 0, 0)]

    @pl.when(first & (g > 0))
    def _():
        for k in range(NXZ):
            greet(at(prev_zh, prev_co, k // NZ, k % NZ, 0))

    @pl.when(last & (g < 3))
    def _():
        for k in range(NXZ):
            greet(at(next_zh, next_co, k // NZ, k % NZ, NY - 1))

    for dx, dz in PLANE[:-1]:
        greet(peer_plane(0, dx, dz))
    greet(peer_plane(1, 0, 0))
    for dy in FAR[:-1]:
        greet(peer_y(0, dy))
    greet(peer_y(1, 0))

    @pl.when(has_prev)
    def _():
        greet(below_id)

    @pl.when(has_next)
    def _():
        greet(above_id)

    for fetch in fetches:
        fetch.wait()
    amps, turns = xm[0:coef_rows, 0, :], xm[coef_rows:2 * coef_rows, 0, :] * INV_TURN
    bend = jnp.concatenate([turns[3 * h + 2:3 * h + 3, :] for h in range(HALF)], axis=0)
    bend = bend * (1.0 / 32)
    sn, cs = sin_cos_halves(bend - nearest(bend))
    xm[coef_rows:2 * coef_rows, 0, :] = turns
    own = xm[:, 0, :]
    message = [own, pltpu.roll(own, 1, 1), pltpu.roll(own, Q - 1, 1)]
    xm[0:HALF, 0, :] = 1.0 - sn * sn
    xm[8:8 + HALF, 0, :] = sn * cs
    xm[16:24, 0, :] = jnp.zeros((8, Q), F32)
    m[...] = jnp.concatenate([part[0:2 * coef_rows] for part in message] + [xm[0:Q - 6 * coef_rows, 0, :]], axis=0).T
    for k in range(NY):
        s1[k, :, 0, :] = m[pl.ds(k, NXZ, stride=NY), :]

    noise8 = noise_ref[...].astype(F32)
    noise = jnp.concatenate([noise8[b:b + 1, :] for b in range(NBLK)], axis=1)
    pk[...] = jnp.zeros_like(pk)
    pk[0:1, :] = bamp[...]
    pk[1:2, :] = bphase[...]
    pk[2:3, :] = bslope[...]
    pk[3:4, :] = bcurve[...]
    pk[4:5, :] = bstart[...].astype(F32)
    pk[5:6, :] = jnp.full((1, SLOTS), bcount[0], jnp.int32).astype(F32)
    pk[6:7, 0:Q] = data_ref[0:1, BINS - Q:]
    pk[6:7, Q:2 * Q] = data_ref[1:2, BINS - Q:]
    pk[6:7, 2 * Q:3 * Q] = noise8[NBLK - 1:NBLK, :]
    bk[...] = jnp.zeros_like(bk)
    bk[0:2, :] = data_ref[:, 0:Q]
    bk[2:3, :] = noise8[0:1, :]

    slot = lax.broadcasted_iota(jnp.int32, (1, SLOTS), 1)
    waits = NXZ + NY + has_prev.astype(jnp.int32) + has_next.astype(jnp.int32)
    pl.semaphore_wait(barrier, waits + up.astype(jnp.int32) + down.astype(jnp.int32))

    def remote(src, dst, send, recv, where):
        return pltpu.make_async_remote_copy(
            src_ref=src, dst_ref=dst, send_sem=send, recv_sem=recv, device_id=where,
            device_id_type=MESH,
        )

    slot_y = (y % 2) * (NY // 2) + y // 2

    def p1(dy):
        k = wrapped(y + dy, NY)
        return remote(
            s1.at[k], r1.at[slot_y], p1_send, p1_recv, {"shard_2": k}
        )

    for dy in FAR[:-1]:
        p1(dy).start()

    forward = remote(pk, fw, nb_send.at[0], nb_recv.at[0], above_id)
    backward = remote(bk, bw, nb_send.at[1], nb_recv.at[1], below_id)

    @pl.when(has_next)
    def _():
        forward.start()

    @pl.when(has_prev)
    def _():
        backward.start()

    r1[slot_y] = s1[y]

    @pl.when(n >= 0)
    def _():
        re_own, im_own, block_own = wave_tile(
            bamp[...], bphase[...], bslope[...], bcurve[...], bstart[...], slot < bcount[0]
        )
        noise_columns = jnp.concatenate([noise8, jnp.zeros((8, Q), F32)], axis=0).T
        total = jnp.zeros((Q, SLOTS), F32)
        for b in range(NBLK + 1):
            here = block_own == b
            wt[0, b * Q:(b + 1) * Q, :] = jnp.where(here, re_own, 0.0).astype(BF16)
            wt[1, b * Q:(b + 1) * Q, :] = jnp.where(here, im_own, 0.0).astype(BF16)
            if b < NBLK:
                total = jnp.where(here, noise_columns[:, b:b + 1], total)
        power = re_own * re_own + im_own * im_own
        rim_power[...] = jnp.where(block_own == NBLK, power, 0.0)
        self_ref[...] = jnp.sum(power * total, axis=0, keepdims=True)

    p1_all = remote(r1.at[0:NY - 1], r1.at[0:NY - 1], p1_send, p1_recv, {"shard_2": y})
    p1_all.wait_recv()

    up_copy = remote(
        r1.at[:, 0], a.at[xz, 1], ex_send.at[0], p2_recv.at[xz], at(next_zh, next_co, 0, 0, 0)
    )
    down_copy = remote(
        r1.at[:, NXZ - 1], a.at[xz, 1], ex_send.at[1], p2_recv.at[xz],
        at(prev_zh, prev_co, NX - 1, NZ - 1, NY - 1),
    )

    @pl.when(up)
    def _():
        up_copy.start()

    @pl.when(down)
    def _():
        down_copy.start()

    def p2(dx, dz):
        xk, zk = wrapped(x + dx, NX), wrapped(z + dz, NZ)
        return remote(
            r1.at[:, xk * NZ + zk], a.at[xz, 0], p2_send, p2_recv.at[xz],
            {"shard_0": xk, "shard_1": zk},
        )

    for dx, dz in PLANE[:-1]:
        p2(dx, dz).start()
    a[xz, 0] = r1[:, xz]

    @pl.when(has_prev)
    def _():
        forward.wait_recv()

    @pl.when(has_next)
    def _():
        backward.wait_recv()

    below = jnp.where(jnp.full((8, SLOTS), n, jnp.int32) > 0, fw[...], 0.0)
    above = jnp.where(jnp.full((8, Q), n, jnp.int32) < NBANDS - 1, bw[...], 0.0)
    re_prev, im_prev, block_prev = wave_tile(
        below[0:1], below[1:2], below[2:3], below[3:4], below[4:5].astype(jnp.int32),
        slot.astype(F32) < below[5:6],
    )
    for b in range(2):
        here = block_prev == NBLK - 1 + b
        wp[0, b * Q:(b + 1) * Q, :] = jnp.where(here, re_prev, 0.0).astype(BF16)
        wp[1, b * Q:(b + 1) * Q, :] = jnp.where(here, im_prev, 0.0).astype(BF16)

    rim_noise = jnp.concatenate(
        [below[6:7, 2 * Q:3 * Q], noise8[0:1, :], above[2:3, :], jnp.zeros((5, Q), F32)], axis=0
    ).T
    self_power = self_ref[...] + jnp.sum(rim_power[...] * rim_noise[:, 2:3], axis=0, keepdims=True)
    power_prev = re_prev * re_prev + im_prev * im_prev
    total_prev = jnp.where(
        block_prev == NBLK - 1, rim_noise[:, 0:1],
        jnp.where(block_prev == NBLK, rim_noise[:, 1:2], 0.0),
    )
    self_prev = jnp.sum(power_prev * total_prev, axis=0, keepdims=True)

    edge_first, edge_last = first & (g > 0), last & (g < 3)
    edge = edge_first | edge_last
    lane_q = lax.broadcasted_iota(jnp.int32, (8, Q), 1)
    take_prev = jnp.full((8, Q), edge_first.astype(jnp.int32), jnp.int32)
    take_next = jnp.full((8, Q), edge_last.astype(jnp.int32), jnp.int32)
    take = ((take_prev > 0) & (lane_q >= SECTION) & (lane_q < 2 * SECTION)) | (
        (take_next > 0) & (lane_q >= 2 * SECTION) & (lane_q < 3 * SECTION)
    )
    below_data = (below[6:7, 0:Q], below[6:7, Q:2 * Q])

    def arrived(quarter, dz):
        dx = jnp.where(quarter >= 2, 5 - quarter, quarter)
        xk, zk = wrapped(x + NX - dx, NX), wrapped(z + NZ - dz, NZ)
        k = xk * NZ + zk
        d = dx * NZ + dz

        def wait(part):
            remote(part, part, p2_send, p2_recv.at[k], {"shard_2": y}).wait_recv()

        @pl.when((d > 0) & edge)
        def _():
            wait(a.at[k])

        @pl.when((d > 0) & jnp.logical_not(edge))
        def _():
            wait(a.at[k, 0])

        @pl.when((d == 0) & edge)
        def _():
            wait(a.at[k, 1])

        return k

    def edge_template(tile, section, offset):
        u = (lax.broadcasted_iota(jnp.int32, (8, Q), 1).astype(F32) + offset) * (1.0 / BINS)
        base = section * SECTION
        lost = amp_sum = im = None
        for h in range(HALF):
            ca = base + 3 * h
            cp = ca + coef_rows
            a0, a1, a2, p0, p1_, p2_ = (
                jnp.broadcast_to(tile[:, k:k + 1], (8, Q))
                for k in (ca, ca + 1, ca + 2, cp, cp + 1, cp + 2)
            )
            t = p0 + u * (p1_ + u * p2_)
            sn, cs = sin_cos_halves(t - nearest(t))
            amp = a0 + u * (a1 + u * a2)
            asn = amp * sn
            if h == 0:
                amp_sum, lost, im = amp, asn * sn, asn * cs
            else:
                amp_sum, lost, im = amp_sum + amp, lost + asn * sn, im + asn * cs
        return amp_sum - lost, im

    def template_rows(quarter, step):
        for k in [arrived(quarter, step * TILES + i) for i in range(TILES)]:
            tile = jnp.where(take, a[k, 1, :, 0, :], a[k, 0, :, 0, :])
            own_re, own_im = own_template(tile, 0, coef_rows)
            halves = {block + 1: (own_re[block], own_im[block]) for block in range(NBLK)}
            halves[0] = edge_template(tile, 1, BINS - Q)
            halves[NBLK + 1] = edge_template(tile, 2, 0)
            for block, parts in halves.items():
                for part, half in enumerate(parts):
                    half = half.astype(BF16).astype(F32)
                    template = half + pltpu.roll(half, 4, 0)
                    if block == 0:
                        values = below_data[part]
                    elif block == NBLK + 1:
                        values = above[part:part + 1, :]
                    else:
                        values = data_ref[part:part + 1, (block - 1) * Q:block * Q]
                    res[part, k, :, block * Q:(block + 1) * Q] = values - template

    @pl.loop(0, NX)
    def _(quarter):
        @pl.loop(0, NZ // TILES)
        def _(step):
            template_rows(quarter, step)


    noise_ext = jnp.concatenate([below[6:7, 2 * Q:3 * Q], noise, above[2:3, :]], axis=1)
    corr = jnp.zeros((W, SLOTS), F32)
    corr_prev = jnp.zeros((W, SLOTS), F32)
    upper = lax.broadcasted_iota(jnp.int32, (NXZ // 2, 8, EXT * Q), 1) < 4

    def residual(part):
        pairs = res[part].reshape(NXZ // 2, 2, 8, EXT * Q)
        return jnp.where(upper, pairs[:, 0], pairs[:, 1]).reshape(W, EXT * Q)

    residuals = [residual(part) for part in range(2)]
    for part in range(2):
        weighted = (residuals[part] * noise_ext).astype(BF16)
        corr += jnp.dot(weighted[:, Q:], wt[part], preferred_element_type=F32)
        corr_prev += jnp.dot(weighted[:, 0:2 * Q], wp[part], preferred_element_type=F32)

    def sigmoid(v):
        return 1.0 / (1.0 + jnp.exp(-v))

    accept = jnp.where(slot < bcount[0], sigmoid(corr - 0.5 * self_power), 0.0)
    acc_out[...] = accept
    accept = accept.astype(BF16)
    accept_prev = sigmoid(corr_prev - 0.5 * self_prev).astype(BF16)
    square = jnp.zeros((1, BINS), F32)
    nt = (((1,), (1,)), ((), ()))
    for part in range(2):
        change = lax.dot_general(accept, wt[part, 0:BINS, :], nt, preferred_element_type=F32)
        rim = lax.dot_general(accept_prev, wp[part, Q:2 * Q, :], nt, preferred_element_type=F32)
        new = residuals[part][:, Q:Q + BINS] - change
        new = jnp.concatenate([new[:, 0:Q] - rim, new[:, Q:]], axis=1)
        new_ref[part] = new
        square += jnp.sum(new * new, axis=0, keepdims=True)
    mean = jnp.sum(square, axis=1, keepdims=True) * (1.0 / (2 * W * BINS))
    log_power = jnp.log(mean + 1e-06)
    lane = lax.broadcasted_iota(jnp.int32, (1, Q), 1)
    mine = chebyshev_rows((2 * jnp.full((1, Q), n, jnp.int32) + 1).astype(F32) / NBANDS - 1.0, lane)
    ra[ida] = mine * log_power

    def sum_a(dc, dy):
        return remote(ra.at[ida], ra.at[ida], ra_send, ra_recv, peer_y(dc, dy))

    def sum_b(dh, dx, dz):
        return remote(rb.at[idb], rb.at[idb], rb_send, rb_recv, peer_plane(dh, dx, dz))

    sum_a_all = remote(ra.at[0:15], ra.at[0:15], ra_send, ra_recv, {"shard_2": y})
    sum_b_all = remote(rb.at[0:31], rb.at[0:31], rb_send, rb_recv, {"shard_2": y})

    for member in members_a:
        sum_a(*member).start()

    @pl.when(n >= 0)
    def _():
        bands = lax.broadcasted_iota(jnp.int32, (NCOEF, NBANDS), 1)
        basis = chebyshev_rows(
            (2 * bands + 1).astype(F32) / NBANDS - 1.0,
            lax.broadcasted_iota(jnp.int32, (NCOEF, NBANDS), 0),
        )
        sub = lax.broadcasted_iota(jnp.int32, (NCOEF, Q), 0)
        lane8 = lax.broadcasted_iota(jnp.int32, (NCOEF, Q), 1)
        position = (2 * jnp.full((NCOEF, Q), n, jnp.int32) + 1).astype(F32) / NBANDS - 1.0
        table = jnp.where(lane8 == NCOEF, chebyshev_rows(position, sub), 0.0)
        for k in range(NCOEF):
            column = jnp.sum(basis * basis[k:k + 1, :], axis=1, keepdims=True)
            table = jnp.where(lane8 == k, column, table)
        rows = []
        for k in range(NCOEF):
            root = jnp.sqrt(table[k:k + 1, k:k + 1])
            row = table[k:k + 1, :] / root
            column = table[:, k:k + 1] / root
            rows.append(row)
            table = jnp.where(sub > k, table - column * row, table)
        zrow = jnp.zeros((1, Q), F32)
        for k in reversed(range(NCOEF)):
            row = rows[k]
            known = jnp.sum(jnp.where((lane > k) & (lane < NCOEF), row * zrow, 0.0), axis=1, keepdims=True)
            value = (row[:, NCOEF:NCOEF + 1] - known) / row[:, k:k + 1]
            zrow = jnp.where(lane == k, value, zrow)
        zrow_ref[...] = zrow
        for part in range(2):
            res_out[:, part, :] = new_ref[part]

    p1_all.wait_send()
    remote(
        a.at[0:NXZ - 1, 0], a.at[0:NXZ - 1, 0], p2_send, p2_recv.at[xz], {"shard_2": y}
    ).wait_send()

    @pl.when(has_next)
    def _():
        forward.wait_send()

    @pl.when(has_prev)
    def _():
        backward.wait_send()

    @pl.when(up)
    def _():
        up_copy.wait_send()

    @pl.when(down)
    def _():
        down_copy.wait_send()

    sum_a_all.wait_recv()
    rb[idb] = jnp.sum(ra[...], axis=0)
    for member in members_b:
        sum_b(*member).start()
    sum_a_all.wait_send()
    sum_b_all.wait_recv()
    moment = jnp.sum(rb[...], axis=0)
    fit = jnp.sum(zrow_ref[...] * moment, axis=1, keepdims=True)
    fit_out[...] = jnp.broadcast_to(fit, (1, Q))
    sum_b_all.wait_send()


def write_out(acc_ref, res_ref, fit_ref, acc_out, res_out, fit_out, fit_smem, sems):
    copies = [pltpu.make_async_copy(acc_ref, acc_out, sems.at[4])]
    for i in range(4):
        rows = pl.ds(i * (W // 4), W // 4)
        copies.append(pltpu.make_async_copy(res_ref.at[rows], res_out.at[rows], sems.at[i]))
    for copy in copies:
        copy.start()
    fit_smem[0] = fit_ref[0, 0]
    copies.append(pltpu.make_async_copy(fit_smem, fit_out, sems.at[5]))
    copies[-1].start()
    for copy in copies:
        copy.wait()


def local(data, inv_noise, mbh_amp, mbh_phase, bin_amp, bin_phase, bin_slope, bin_curve, bin_start, bin_count):
    vmem = pl.BlockSpec(memory_space=pltpu.VMEM)
    smem = pl.BlockSpec(memory_space=pltpu.SMEM)
    dma = pltpu.SemaphoreType.DMA
    rows = 3 * HALF
    accept, residual, fit = pl.pallas_call(
        kernel,
        out_shape=(
            jax.ShapeDtypeStruct((W, SLOTS), F32),
            jax.ShapeDtypeStruct((W, 2, BINS), F32),
            jax.ShapeDtypeStruct((1, Q), F32),
        ),
        in_specs=[pl.BlockSpec(memory_space=pltpu.HBM)] * 9 + [smem],
        out_specs=(vmem, vmem, vmem),
        scratch_shapes=[
            pltpu.VMEM((2, BINS), F32),
            pltpu.VMEM((NBLK, Q), BF16),
            pltpu.VMEM((1, SLOTS), F32),
            pltpu.VMEM((1, SLOTS), F32),
            pltpu.VMEM((1, SLOTS), F32),
            pltpu.VMEM((1, SLOTS), F32),
            pltpu.VMEM((1, SLOTS), jnp.int32),
            pltpu.VMEM((40, 1, Q), F32),
            pltpu.VMEM((Q, Q), F32),
            pltpu.VMEM((NY, NXZ, 1, Q), F32),
            pltpu.VMEM((NY, NXZ, 1, Q), F32),
            pltpu.VMEM((NXZ, 2, NY, 1, Q), F32),
            pltpu.VMEM((8, SLOTS), F32),
            pltpu.VMEM((8, SLOTS), F32),
            pltpu.VMEM((8, Q), F32),
            pltpu.VMEM((8, Q), F32),
            pltpu.VMEM((2, (NBLK + 1) * Q, SLOTS), BF16),
            pltpu.VMEM((2, 2 * Q, SLOTS), BF16),
            pltpu.VMEM((Q, SLOTS), F32),
            pltpu.VMEM((1, SLOTS), F32),
            pltpu.VMEM((2, NXZ, 8, EXT * Q), F32),
            pltpu.VMEM((2, W, BINS), F32),
            pltpu.VMEM((16, 1, Q), F32),
            pltpu.VMEM((32, 1, Q), F32),
            pltpu.VMEM((1, Q), F32),
            dma((9,)), dma, dma, dma, dma((NXZ,)), dma((2,)), dma((2,)), dma((2,)),
            dma, dma, dma, dma,
        ],
        compiler_params=pltpu.CompilerParams(
            collective_id=0, has_side_effects=True, vmem_limit_bytes=48 * 1024 * 1024
        ),
        name="gibbs_round",
    )(
        *(
            pltpu.with_memory_space_constraint(v, pltpu.HBM)
            for v in (
                data,
                inv_noise.reshape(NBLK, Q),
                mbh_amp.transpose(1, 2, 0, 3).reshape(rows, 1, Q),
                mbh_phase.transpose(1, 2, 0, 3).reshape(rows, 1, Q),
                bin_amp, bin_phase, bin_slope, bin_curve, bin_start,
            )
        ),
        bin_count,
    )
    accept, residual, fit = pl.pallas_call(
        write_out,
        out_shape=(
            jax.ShapeDtypeStruct((W, SLOTS), F32),
            jax.ShapeDtypeStruct((W, 2, BINS), F32),
            jax.ShapeDtypeStruct((1,), F32),
        ),
        in_specs=[vmem] * 3,
        out_specs=(pl.BlockSpec(memory_space=pltpu.HBM),) * 3,
        scratch_shapes=[pltpu.SMEM((1,), F32), dma((6,))],
        name="write_out",
    )(
        pltpu.with_memory_space_constraint(accept, pltpu.VMEM),
        pltpu.with_memory_space_constraint(residual, pltpu.VMEM),
        pltpu.with_memory_space_constraint(fit, pltpu.VMEM),
    )
    return accept, residual, fit


def solution(mesh):
    split = Mesh(mesh.devices.reshape(2, 2, NX, NZ, NY), GROUP_SHARD)
    return jax.shard_map(
        local,
        mesh=split,
        in_specs=(
            P(None, GROUP_SHARD),
            P(GROUP_SHARD),
            P(SHARD, None, None, GROUP),
            P(SHARD, None, None, GROUP),
            P(GROUP_SHARD, None),
            P(GROUP_SHARD, None),
            P(GROUP_SHARD, None),
            P(GROUP_SHARD, None),
            P(GROUP_SHARD, None),
            P(GROUP_SHARD),
        ),
        out_specs=(P(None, GROUP_SHARD), P(None, None, GROUP_SHARD), P(GROUP_SHARD)),
        check_vma=False,
    )
```

```python
import jax
import jax.numpy as jnp
from jax import lax
from jax.experimental import pallas as pl
from jax.experimental.pallas import tpu as pltpu
from jax.sharding import Mesh
from jax.sharding import PartitionSpec as P

W = 64
HALF = 6
Q = 128
BINS = 1024
SLOTS = 512
NCOEF = 8
NX, NZ, NY = 4, 4, 8
NXZ = NX * NZ
NBANDS = 512
NBLK = BINS // Q
EXT = NBLK + 2
SHARD = ("shard_0", "shard_1", "shard_2")
GROUP_SHARD = ("group_0", "group_1", "shard_0", "shard_1", "shard_2")
GROUP = ("group_0", "group_1")
MESH = pl.DeviceIdType.MESH
F32 = jnp.float32
BF16 = jnp.bfloat16

INV_TURN = 0.15915494309189535
TURN_HI = 6.28125
TURN_LO = 0.0019353071795864769
SIN_C = (4.44288283, -7.30824115, 3.60628896, -0.84576359, 0.10920575)
COS_C = (1.4142135, -6.97885099, 5.73946117, -1.88356298, 0.31069818)
COS6_C = (1.41421356, -6.97886411, 5.73988155, -1.888275, 0.33225188, -0.03450217)
SIN1_C = (3.14159258, -5.16770688, 2.55003138, -0.59804517, 0.0772201264)
COS1_C = (0.999999956, -4.93479286, 4.05841191, -1.33188016, 0.21969679)
SECTION = 36
ROT = 108
TILES = 2
FAR = (4, 3, 5, 2, 6, 1, 7, 0)
PLANE = ((2, 2), (2, 1), (1, 2), (2, 3), (3, 2), (1, 1), (1, 3), (3, 1), (3, 3),
         (0, 2), (2, 0), (0, 1), (0, 3), (1, 0), (3, 0), (0, 0))


def poly(coefs, square):
    total = coefs[-1] * square + coefs[-2]
    for c in coefs[-3::-1]:
        total = total * square + c
    return total


def nearest(t):
    return jnp.round(t)


def sin_cos_halves(f):
    square = f * f
    return f * poly(SIN_C, square), poly(COS_C, square)


def chebyshev_rows(x, index):
    terms = [jnp.ones_like(x), x]
    for _ in range(2, NCOEF):
        terms.append(2.0 * x * terms[-1] - terms[-2])
    out = jnp.zeros_like(x)
    for k in range(NCOEF):
        out = jnp.where(index == k, terms[k], out)
    return out


def wave_tile(amp, phase, slope, curve, start, live):
    low = jnp.bitwise_and(start, Q - 1)
    row = lax.broadcasted_iota(jnp.int32, (Q, SLOTS), 0)
    j = jnp.bitwise_and(row - low, Q - 1)
    block = lax.shift_right_logical(start, 7) + (row < low).astype(jnp.int32)
    jf = j.astype(F32)
    angle = phase + slope * jf + curve * jf * jf
    turns = nearest(angle * INV_TURN)
    rest = (angle - turns * TURN_HI) - turns * TURN_LO
    s, c = sin_cos_halves(rest * INV_TURN)
    y = (jf + (0.5 - Q / 2)) * (1.0 / Q)
    half = poly(COS6_C, y * y)
    size = jnp.where(live, amp, 0.0) * (half * half * 0.5)
    re = size * (1.0 - s * s)
    im = size * (s * c)
    return re.astype(BF16).astype(F32), im.astype(BF16).astype(F32), block


def own_template(tile, base, coef_rows):
    v = (lax.broadcasted_iota(jnp.int32, (8, Q), 1).astype(F32) + (NBLK - 1) * Q / 2) * (1.0 / BINS)
    re, im = [None] * NBLK, [None] * NBLK
    for h in range(HALF):
        ca = base + 3 * h
        cp = ca + coef_rows
        a0, a1, a2, p0, p1, p2, g2r, g2i = (
            jnp.broadcast_to(tile[:, k:k + 1], (8, Q))
            for k in (ca, ca + 1, ca + 2, cp, cp + 1, cp + 2, ROT + h, ROT + 8 + h)
        )
        g4r, g4i = 1.0 - 2.0 * (g2i * g2i), 2.0 * (g2i * g2r)
        g6r, g6i = g4r * g2r - g4i * g2i, g4i * g2r + g4r * g2i
        theta = p1 * 0.125 + v * (p2 * 0.25)
        whole = nearest(theta)
        f = theta - whole
        square = f * f
        yi, yr = f * poly(SIN1_C, square), poly(COS1_C, square)
        twice = 2.0 - 4.0 * (yi * yi)
        y_last = None
        center = (p0 + v * (p1 + v * p2)) + (p2 * (1.0 / 256) + 0.5 * whole)
        s, c = sin_cos_halves(center - nearest(center))
        xr, xi = 1.0 - s * s, s * c
        alpha = a0 + v * (a1 + v * a2)
        beta = a1 * 0.125 + v * (a2 * 0.25)
        curve = a2 * (1.0 / 64)
        for i in range(NBLK // 2):
            m = i + 0.5
            if i == 1:
                y_next = ((twice - 1.0) * yr, (twice + 1.0) * yi)
            elif i > 1:
                y_next = (twice * yr - y_last[0], twice * yi - y_last[1])
            if i > 0:
                y_last, (yr, yi) = (yr, yi), y_next
                rr, ri = ((g2r, g2i), (g4r, g4i), (g6r, g6i))[i - 1]
                xr, xi = xr * rr - xi * ri, xi * rr + xr * ri
            size, tilt = alpha + curve * (m * m), beta * m
            rr_, ii_, ri_, ir_ = xr * yr, xi * yi, xr * yi, xi * yr
            for block, amp, x_re, x_im in (
                (NBLK // 2 + i, size + tilt, rr_ - ii_, ir_ + ri_),
                (NBLK // 2 - 1 - i, size - tilt, rr_ + ii_, ir_ - ri_),
            ):
                if h == 0:
                    re[block], im[block] = amp * x_re, amp * x_im
                else:
                    re[block], im[block] = re[block] + amp * x_re, im[block] + amp * x_im
    return re, im


def wrapped(v, n):
    return jnp.where(v >= n, v - n, v)


def kernel(
    data_hbm, noise_hbm, amp_hbm, phase_hbm, bamp_hbm, bphase_hbm, bslope_hbm, bcurve_hbm,
    bstart_hbm, bcount,
    acc_out, res_out, fit_out,
    data_ref, noise_ref, bamp, bphase, bslope, bcurve, bstart,
    xm, m, s1, r1, a, ex, pk, fw, bk, bw, wt, wp, rim_power, self_ref, res, new_ref, ra, rb,
    zrow_ref,
    in_sem, p1_send, p1_recv, p2_send, p2_recv, ex_send, ex_recv, nb_send, nb_recv,
    ra_send, ra_recv, rb_send, rb_recv,
):
    coef_rows = 3 * HALF
    inputs = [
        (amp_hbm, xm.at[0:coef_rows]), (phase_hbm, xm.at[coef_rows:2 * coef_rows]),
        (data_hbm, data_ref), (noise_hbm, noise_ref), (bamp_hbm, bamp), (bphase_hbm, bphase),
        (bslope_hbm, bslope), (bcurve_hbm, bcurve), (bstart_hbm, bstart),
    ]
    fetches = [
        pltpu.make_async_copy(src, dst, in_sem.at[i]) for i, (src, dst) in enumerate(inputs)
    ]
    for fetch in fetches:
        fetch.start()

    zh, co = lax.axis_index("group_0"), lax.axis_index("group_1")
    x, z, y = lax.axis_index("shard_0"), lax.axis_index("shard_1"), lax.axis_index("shard_2")
    g = zh * 2 + co
    s = x * (NZ * NY) + z * NY + y
    n = g * (NBANDS // 4) + s
    xz = x * NZ + z
    ida = co * NY + y
    idb = zh * NXZ + xz
    has_prev, has_next = n > 0, n < NBANDS - 1
    first, last = s == 0, s == NBANDS // 4 - 1
    up = (y == 0) & (g < 3)
    down = (y == NY - 1) & (g > 0)

    def at(group0, group1, xi, zi, yi):
        return {
            "group_0": group0, "group_1": group1, "shard_0": xi, "shard_1": zi, "shard_2": yi,
        }

    turn_y = y == NY - 1
    turn_z = turn_y & (z == NZ - 1)
    turn_x = turn_z & (x == NX - 1)
    turn_c = turn_x & (co == 1)
    above_id = at(
        jnp.where(turn_c, 1 - zh, zh), jnp.where(turn_x, 1 - co, co),
        jnp.where(turn_z, wrapped(x + 1, NX), x), jnp.where(turn_y, wrapped(z + 1, NZ), z),
        wrapped(y + 1, NY),
    )
    back_y = y == 0
    back_z = back_y & (z == 0)
    back_x = back_z & (x == 0)
    back_c = back_x & (co == 0)
    below_id = at(
        jnp.where(back_c, 1 - zh, zh), jnp.where(back_x, 1 - co, co),
        jnp.where(back_z, wrapped(x + NX - 1, NX), x),
        jnp.where(back_y, wrapped(z + NZ - 1, NZ), z),
        wrapped(y + NY - 1, NY),
    )
    next_zh, next_co = jnp.where(co == 1, 1 - zh, zh), 1 - co
    prev_zh, prev_co = jnp.where(co == 0, 1 - zh, zh), 1 - co

    barrier = pltpu.get_barrier_semaphore()

    def greet(where):
        pl.semaphore_signal(barrier, inc=1, device_id=where, device_id_type=MESH)

    def peer_y(dc, dy):
        return {"group_1": 1 - co if dc else co, "shard_2": wrapped(y + dy, NY)}

    def peer_plane(dh, dx, dz):
        return {
            "group_0": 1 - zh if dh else zh,
            "shard_0": wrapped(x + dx, NX), "shard_1": wrapped(z + dz, NZ),
        }

    members_a = [(dc, dy) for dy in FAR for dc in (1, 0) if (dc, dy) != (0, 0)]
    members_b = [(dh, dx, dz) for dx, dz in PLANE for dh in (1, 0) if (dh, dx, dz) != (0, 0, 0)]

    @pl.when(first & (g > 0))
    def _():
        for k in range(NXZ):
            greet(at(prev_zh, prev_co, k // NZ, k % NZ, 0))

    @pl.when(last & (g < 3))
    def _():
        for k in range(NXZ):
            greet(at(next_zh, next_co, k // NZ, k % NZ, NY - 1))

    for dx, dz in PLANE[:-1]:
        greet(peer_plane(0, dx, dz))
    greet(peer_plane(1, 0, 0))
    for dy in FAR[:-1]:
        greet(peer_y(0, dy))
    greet(peer_y(1, 0))

    @pl.when(has_prev)
    def _():
        greet(below_id)

    @pl.when(has_next)
    def _():
        greet(above_id)

    for fetch in fetches:
        fetch.wait()
    amps, turns = xm[0:coef_rows, 0, :], xm[coef_rows:2 * coef_rows, 0, :] * INV_TURN
    bend = jnp.concatenate([turns[3 * h + 2:3 * h + 3, :] for h in range(HALF)], axis=0)
    bend = bend * (1.0 / 32)
    sn, cs = sin_cos_halves(bend - nearest(bend))
    xm[coef_rows:2 * coef_rows, 0, :] = turns
    own = xm[:, 0, :]
    message = [own, pltpu.roll(own, 1, 1), pltpu.roll(own, Q - 1, 1)]
    xm[0:HALF, 0, :] = 1.0 - sn * sn
    xm[8:8 + HALF, 0, :] = sn * cs
    xm[16:24, 0, :] = jnp.zeros((8, Q), F32)
    m[...] = jnp.concatenate([part[0:2 * coef_rows] for part in message] + [xm[0:Q - 6 * coef_rows, 0, :]], axis=0).T
    for k in range(NY):
        s1[k, :, 0, :] = m[pl.ds(k, NXZ, stride=NY), :]

    noise8 = noise_ref[...].astype(F32)
    noise = jnp.concatenate([noise8[b:b + 1, :] for b in range(NBLK)], axis=1)
    pk[...] = jnp.zeros_like(pk)
    pk[0:1, :] = bamp[...]
    pk[1:2, :] = bphase[...]
    pk[2:3, :] = bslope[...]
    pk[3:4, :] = bcurve[...]
    pk[4:5, :] = bstart[...].astype(F32)
    pk[5:6, :] = jnp.full((1, SLOTS), bcount[0], jnp.int32).astype(F32)
    pk[6:7, 0:Q] = data_ref[0:1, BINS - Q:]
    pk[6:7, Q:2 * Q] = data_ref[1:2, BINS - Q:]
    pk[6:7, 2 * Q:3 * Q] = noise8[NBLK - 1:NBLK, :]
    bk[...] = jnp.zeros_like(bk)
    bk[0:2, :] = data_ref[:, 0:Q]
    bk[2:3, :] = noise8[0:1, :]

    slot = lax.broadcasted_iota(jnp.int32, (1, SLOTS), 1)
    waits = NXZ + NY + has_prev.astype(jnp.int32) + has_next.astype(jnp.int32)
    pl.semaphore_wait(barrier, waits + up.astype(jnp.int32) + down.astype(jnp.int32))

    def remote(src, dst, send, recv, where):
        return pltpu.make_async_remote_copy(
            src_ref=src, dst_ref=dst, send_sem=send, recv_sem=recv, device_id=where,
            device_id_type=MESH,
        )

    slot_y = (y % 2) * (NY // 2) + y // 2

    def p1(dy):
        k = wrapped(y + dy, NY)
        return remote(
            s1.at[k], r1.at[slot_y], p1_send, p1_recv, {"shard_2": k}
        )

    for dy in FAR[:-1]:
        p1(dy).start()

    forward = remote(pk, fw, nb_send.at[0], nb_recv.at[0], above_id)
    backward = remote(bk, bw, nb_send.at[1], nb_recv.at[1], below_id)

    @pl.when(has_next)
    def _():
        forward.start()

    @pl.when(has_prev)
    def _():
        backward.start()

    r1[slot_y] = s1[y]

    @pl.when(n >= 0)
    def _():
        re_own, im_own, block_own = wave_tile(
            bamp[...], bphase[...], bslope[...], bcurve[...], bstart[...], slot < bcount[0]
        )
        noise_columns = jnp.concatenate([noise8, jnp.zeros((8, Q), F32)], axis=0).T
        total = jnp.zeros((Q, SLOTS), F32)
        for b in range(NBLK + 1):
            here = block_own == b
            wt[0, b * Q:(b + 1) * Q, :] = jnp.where(here, re_own, 0.0).astype(BF16)
            wt[1, b * Q:(b + 1) * Q, :] = jnp.where(here, im_own, 0.0).astype(BF16)
            if b < NBLK:
                total = jnp.where(here, noise_columns[:, b:b + 1], total)
        power = re_own * re_own + im_own * im_own
        rim_power[...] = jnp.where(block_own == NBLK, power, 0.0)
        self_ref[...] = jnp.sum(power * total, axis=0, keepdims=True)

    p1_all = remote(r1.at[0:NY - 1], r1.at[0:NY - 1], p1_send, p1_recv, {"shard_2": y})
    p1_all.wait_recv()

    up_copy = remote(
        r1.at[:, 0], ex.at[xz], ex_send.at[0], ex_recv, at(next_zh, next_co, 0, 0, 0)
    )
    down_copy = remote(
        r1.at[:, NXZ - 1], ex.at[xz], ex_send.at[1], ex_recv,
        at(prev_zh, prev_co, NX - 1, NZ - 1, NY - 1),
    )

    @pl.when(up)
    def _():
        up_copy.start()

    @pl.when(down)
    def _():
        down_copy.start()

    def p2(dx, dz):
        xk, zk = wrapped(x + dx, NX), wrapped(z + dz, NZ)
        return remote(
            r1.at[:, xk * NZ + zk], a.at[xz], p2_send, p2_recv.at[xz],
            {"shard_0": xk, "shard_1": zk},
        )

    for dx, dz in PLANE[:-1]:
        p2(dx, dz).start()
    a[xz] = r1[:, xz]

    @pl.when(has_prev)
    def _():
        forward.wait_recv()

    @pl.when(has_next)
    def _():
        backward.wait_recv()

    below = jnp.where(jnp.full((8, SLOTS), n, jnp.int32) > 0, fw[...], 0.0)
    above = jnp.where(jnp.full((8, Q), n, jnp.int32) < NBANDS - 1, bw[...], 0.0)
    re_prev, im_prev, block_prev = wave_tile(
        below[0:1], below[1:2], below[2:3], below[3:4], below[4:5].astype(jnp.int32),
        slot.astype(F32) < below[5:6],
    )
    for b in range(2):
        here = block_prev == NBLK - 1 + b
        wp[0, b * Q:(b + 1) * Q, :] = jnp.where(here, re_prev, 0.0).astype(BF16)
        wp[1, b * Q:(b + 1) * Q, :] = jnp.where(here, im_prev, 0.0).astype(BF16)

    rim_noise = jnp.concatenate(
        [below[6:7, 2 * Q:3 * Q], noise8[0:1, :], above[2:3, :], jnp.zeros((5, Q), F32)], axis=0
    ).T
    self_power = self_ref[...] + jnp.sum(rim_power[...] * rim_noise[:, 2:3], axis=0, keepdims=True)
    power_prev = re_prev * re_prev + im_prev * im_prev
    total_prev = jnp.where(
        block_prev == NBLK - 1, rim_noise[:, 0:1],
        jnp.where(block_prev == NBLK, rim_noise[:, 1:2], 0.0),
    )
    self_prev = jnp.sum(power_prev * total_prev, axis=0, keepdims=True)

    edge_first, edge_last = first & (g > 0), last & (g < 3)
    below_data = (below[6:7, 0:Q], below[6:7, Q:2 * Q])
    above_data = (above[0:1, :], above[1:2, :])
    z_end = jnp.where(z < 2, z, NZ - 1 - z)
    used = lax.broadcasted_iota(jnp.int32, (8, Q), 1) < jnp.full((8, Q), n + Q, jnp.int32)

    def arrived(turn):
        near, xi = turn // NX, turn % NX
        dx = jnp.where(xi >= 2, 5 - xi, xi)
        low = jnp.where((z_end == 1) & (near < 2), 1 - near, near)
        zk = jnp.where(z < 2, low, NZ - 1 - low)
        k = wrapped(x + dx, NX) * NZ + zk
        part = a.at[k]
        remote(part, part, p2_send, p2_recv.at[k], {"shard_2": y}).wait_recv()
        return k

    def edge_template(tile, section, offset):
        u = (lax.broadcasted_iota(jnp.int32, (8, Q), 1).astype(F32) + offset) * (1.0 / BINS)
        base = section * SECTION
        lost = amp_sum = im = None
        for h in range(HALF):
            ca = base + 3 * h
            cp = ca + coef_rows
            a0, a1, a2, p0, p1_, p2_ = (
                jnp.broadcast_to(tile[:, k:k + 1], (8, Q))
                for k in (ca, ca + 1, ca + 2, cp, cp + 1, cp + 2)
            )
            t = p0 + u * (p1_ + u * p2_)
            sn, cs = sin_cos_halves(t - nearest(t))
            amp = a0 + u * (a1 + u * a2)
            asn = amp * sn
            if h == 0:
                amp_sum, lost, im = amp, asn * sn, asn * cs
            else:
                amp_sum, lost, im = amp_sum + amp, lost + asn * sn, im + asn * cs
        return amp_sum - lost, im

    def put(k, block, parts, values):
        for part, half in enumerate(parts):
            half = half.astype(BF16).astype(F32)
            template = half + pltpu.roll(half, 4, 0)
            res[part, k, :, block * Q:(block + 1) * Q] = values[part] - template

    def template_rows(ks):
        for k in ks:
            tile = jnp.where(used, a[k, :, 0, :], 0.0)
            own_re, own_im = own_template(tile, 0, coef_rows)
            for block in range(NBLK):
                columns = slice(block * Q, (block + 1) * Q)
                put(
                    k, block + 1, (own_re[block], own_im[block]),
                    (data_ref[0:1, columns], data_ref[1:2, columns]),
                )
            put(k, 0, edge_template(tile, 1, BINS - Q), below_data)
            put(k, NBLK + 1, edge_template(tile, 2, 0), above_data)

    template_rows([xz])

    @pl.loop(0, (NXZ - 2) // TILES)
    def _(step):
        template_rows([arrived(1 + step * TILES + i) for i in range(TILES)])

    template_rows([arrived(jnp.int32(NXZ - 1))])

    def other_group(section, offset, block, values):
        remote(ex, ex, ex_send.at[0], ex_recv, {"shard_2": y}).wait_recv()

        @pl.loop(0, NXZ // 8)
        def _(step):
            for i in range(8):
                k = step * 8 + i
                tile = jnp.where(used, ex[k, :, 0, :], 0.0)
                put(k, block, edge_template(tile, section, offset), values)

    @pl.when(edge_first)
    def _():
        other_group(1, BINS - Q, 0, below_data)

    @pl.when(edge_last)
    def _():
        other_group(2, 0, NBLK + 1, above_data)

    noise_ext = jnp.concatenate([below[6:7, 2 * Q:3 * Q], noise, above[2:3, :]], axis=1)
    corr = jnp.zeros((W, SLOTS), F32)
    corr_prev = jnp.zeros((W, SLOTS), F32)
    upper = lax.broadcasted_iota(jnp.int32, (NXZ // 2, 8, EXT * Q), 1) < 4

    def residual(part):
        pairs = res[part].reshape(NXZ // 2, 2, 8, EXT * Q)
        return jnp.where(upper, pairs[:, 0], pairs[:, 1]).reshape(W, EXT * Q)

    residuals = [residual(part) for part in range(2)]
    for part in range(2):
        weighted = (residuals[part] * noise_ext).astype(BF16)
        corr += jnp.dot(weighted[:, Q:], wt[part], preferred_element_type=F32)
        corr_prev += jnp.dot(weighted[:, 0:2 * Q], wp[part], preferred_element_type=F32)

    def sigmoid(v):
        return 1.0 / (1.0 + jnp.exp(-v))

    accept = jnp.where(slot < bcount[0], sigmoid(corr - 0.5 * self_power), 0.0)
    acc_out[...] = accept
    accept = accept.astype(BF16)
    accept_prev = sigmoid(corr_prev - 0.5 * self_prev).astype(BF16)
    square = jnp.zeros((1, BINS), F32)
    nt = (((1,), (1,)), ((), ()))
    for part in range(2):
        change = lax.dot_general(accept, wt[part, 0:BINS, :], nt, preferred_element_type=F32)
        rim = lax.dot_general(accept_prev, wp[part, Q:2 * Q, :], nt, preferred_element_type=F32)
        new = residuals[part][:, Q:Q + BINS] - change
        new = jnp.concatenate([new[:, 0:Q] - rim, new[:, Q:]], axis=1)
        new_ref[part] = new
        square += jnp.sum(new * new, axis=0, keepdims=True)
    mean = jnp.sum(square, axis=1, keepdims=True) * (1.0 / (2 * W * BINS))
    log_power = jnp.log(mean + 1e-06)
    lane = lax.broadcasted_iota(jnp.int32, (1, Q), 1)
    mine = chebyshev_rows((2 * jnp.full((1, Q), n, jnp.int32) + 1).astype(F32) / NBANDS - 1.0, lane)
    ra[ida] = mine * log_power

    def sum_a(dc, dy):
        return remote(ra.at[ida], ra.at[ida], ra_send, ra_recv, peer_y(dc, dy))

    def sum_b(dh, dx, dz):
        return remote(rb.at[idb], rb.at[idb], rb_send, rb_recv, peer_plane(dh, dx, dz))

    sum_a_all = remote(ra.at[0:15], ra.at[0:15], ra_send, ra_recv, {"shard_2": y})
    sum_b_all = remote(rb.at[0:31], rb.at[0:31], rb_send, rb_recv, {"shard_2": y})

    for member in members_a:
        sum_a(*member).start()

    @pl.when(n >= 0)
    def _():
        bands = lax.broadcasted_iota(jnp.int32, (NCOEF, NBANDS), 1)
        basis = chebyshev_rows(
            (2 * bands + 1).astype(F32) / NBANDS - 1.0,
            lax.broadcasted_iota(jnp.int32, (NCOEF, NBANDS), 0),
        )
        sub = lax.broadcasted_iota(jnp.int32, (NCOEF, Q), 0)
        lane8 = lax.broadcasted_iota(jnp.int32, (NCOEF, Q), 1)
        position = (2 * jnp.full((NCOEF, Q), n, jnp.int32) + 1).astype(F32) / NBANDS - 1.0
        table = jnp.where(lane8 == NCOEF, chebyshev_rows(position, sub), 0.0)
        for k in range(NCOEF):
            column = jnp.sum(basis * basis[k:k + 1, :], axis=1, keepdims=True)
            table = jnp.where(lane8 == k, column, table)
        rows = []
        for k in range(NCOEF):
            root = jnp.sqrt(table[k:k + 1, k:k + 1])
            row = table[k:k + 1, :] / root
            column = table[:, k:k + 1] / root
            rows.append(row)
            table = jnp.where(sub > k, table - column * row, table)
        zrow = jnp.zeros((1, Q), F32)
        for k in reversed(range(NCOEF)):
            row = rows[k]
            known = jnp.sum(jnp.where((lane > k) & (lane < NCOEF), row * zrow, 0.0), axis=1, keepdims=True)
            value = (row[:, NCOEF:NCOEF + 1] - known) / row[:, k:k + 1]
            zrow = jnp.where(lane == k, value, zrow)
        zrow_ref[...] = zrow
        for part in range(2):
            res_out[:, part, :] = new_ref[part]

    p1_all.wait_send()
    remote(
        a.at[0:NXZ - 1], a.at[0:NXZ - 1], p2_send, p2_recv.at[xz], {"shard_2": y}
    ).wait_send()

    @pl.when(has_next)
    def _():
        forward.wait_send()

    @pl.when(has_prev)
    def _():
        backward.wait_send()

    @pl.when(up)
    def _():
        up_copy.wait_send()

    @pl.when(down)
    def _():
        down_copy.wait_send()

    sum_a_all.wait_recv()
    rb[idb] = jnp.sum(ra[...], axis=0)
    for member in members_b:
        sum_b(*member).start()
    sum_a_all.wait_send()
    sum_b_all.wait_recv()
    moment = jnp.sum(rb[...], axis=0)
    fit = jnp.sum(zrow_ref[...] * moment, axis=1, keepdims=True)
    fit_out[...] = jnp.broadcast_to(fit, (1, Q))
    sum_b_all.wait_send()


def write_out(acc_ref, res_ref, fit_ref, acc_out, res_out, fit_out, fit_smem, sems):
    copies = [pltpu.make_async_copy(acc_ref, acc_out, sems.at[4])]
    for i in range(4):
        rows = pl.ds(i * (W // 4), W // 4)
        copies.append(pltpu.make_async_copy(res_ref.at[rows], res_out.at[rows], sems.at[i]))
    for copy in copies:
        copy.start()
    fit_smem[0] = fit_ref[0, 0]
    copies.append(pltpu.make_async_copy(fit_smem, fit_out, sems.at[5]))
    copies[-1].start()
    for copy in copies:
        copy.wait()


def local(data, inv_noise, mbh_amp, mbh_phase, bin_amp, bin_phase, bin_slope, bin_curve, bin_start, bin_count):
    vmem = pl.BlockSpec(memory_space=pltpu.VMEM)
    smem = pl.BlockSpec(memory_space=pltpu.SMEM)
    dma = pltpu.SemaphoreType.DMA
    rows = 3 * HALF
    accept, residual, fit = pl.pallas_call(
        kernel,
        out_shape=(
            jax.ShapeDtypeStruct((W, SLOTS), F32),
            jax.ShapeDtypeStruct((W, 2, BINS), F32),
            jax.ShapeDtypeStruct((1, Q), F32),
        ),
        in_specs=[pl.BlockSpec(memory_space=pltpu.HBM)] * 9 + [smem],
        out_specs=(vmem, vmem, vmem),
        scratch_shapes=[
            pltpu.VMEM((2, BINS), F32),
            pltpu.VMEM((NBLK, Q), BF16),
            pltpu.VMEM((1, SLOTS), F32),
            pltpu.VMEM((1, SLOTS), F32),
            pltpu.VMEM((1, SLOTS), F32),
            pltpu.VMEM((1, SLOTS), F32),
            pltpu.VMEM((1, SLOTS), jnp.int32),
            pltpu.VMEM((40, 1, Q), F32),
            pltpu.VMEM((Q, Q), F32),
            pltpu.VMEM((NY, NXZ, 1, Q), F32),
            pltpu.VMEM((NY, NXZ, 1, Q), F32),
            pltpu.VMEM((NXZ, NY, 1, Q), F32),
            pltpu.VMEM((NXZ, NY, 1, Q), F32),
            pltpu.VMEM((8, SLOTS), F32),
            pltpu.VMEM((8, SLOTS), F32),
            pltpu.VMEM((8, Q), F32),
            pltpu.VMEM((8, Q), F32),
            pltpu.VMEM((2, (NBLK + 1) * Q, SLOTS), BF16),
            pltpu.VMEM((2, 2 * Q, SLOTS), BF16),
            pltpu.VMEM((Q, SLOTS), F32),
            pltpu.VMEM((1, SLOTS), F32),
            pltpu.VMEM((2, NXZ, 8, EXT * Q), F32),
            pltpu.VMEM((2, W, BINS), F32),
            pltpu.VMEM((16, 1, Q), F32),
            pltpu.VMEM((32, 1, Q), F32),
            pltpu.VMEM((1, Q), F32),
            dma((9,)), dma, dma, dma, dma((NXZ,)), dma((2,)), dma, dma((2,)), dma((2,)),
            dma, dma, dma, dma,
        ],
        compiler_params=pltpu.CompilerParams(
            collective_id=0, has_side_effects=True, vmem_limit_bytes=48 * 1024 * 1024
        ),
        name="gibbs_round",
    )(
        *(
            pltpu.with_memory_space_constraint(v, pltpu.HBM)
            for v in (
                data,
                inv_noise.reshape(NBLK, Q),
                mbh_amp.transpose(1, 2, 0, 3).reshape(rows, 1, Q),
                mbh_phase.transpose(1, 2, 0, 3).reshape(rows, 1, Q),
                bin_amp, bin_phase, bin_slope, bin_curve, bin_start,
            )
        ),
        bin_count,
    )
    accept, residual, fit = pl.pallas_call(
        write_out,
        out_shape=(
            jax.ShapeDtypeStruct((W, SLOTS), F32),
            jax.ShapeDtypeStruct((W, 2, BINS), F32),
            jax.ShapeDtypeStruct((1,), F32),
        ),
        in_specs=[vmem] * 3,
        out_specs=(pl.BlockSpec(memory_space=pltpu.HBM),) * 3,
        scratch_shapes=[pltpu.SMEM((1,), F32), dma((6,))],
        name="write_out",
    )(
        pltpu.with_memory_space_constraint(accept, pltpu.VMEM),
        pltpu.with_memory_space_constraint(residual, pltpu.VMEM),
        pltpu.with_memory_space_constraint(fit, pltpu.VMEM),
    )
    return accept, residual, fit


def solution(mesh):
    split = Mesh(mesh.devices.reshape(2, 2, NX, NZ, NY), GROUP_SHARD)
    return jax.shard_map(
        local,
        mesh=split,
        in_specs=(
            P(None, GROUP_SHARD),
            P(GROUP_SHARD),
            P(SHARD, None, None, GROUP),
            P(SHARD, None, None, GROUP),
            P(GROUP_SHARD, None),
            P(GROUP_SHARD, None),
            P(GROUP_SHARD, None),
            P(GROUP_SHARD, None),
            P(GROUP_SHARD, None),
            P(GROUP_SHARD),
        ),
        out_specs=(P(None, GROUP_SHARD), P(None, None, GROUP_SHARD), P(GROUP_SHARD)),
        check_vma=False,
    )
```

```python
import jax
import jax.numpy as jnp
from jax import lax
from jax.experimental import pallas as pl
from jax.experimental.pallas import tpu as pltpu
from jax.sharding import Mesh
from jax.sharding import PartitionSpec as P

W = 64
HALF = 6
Q = 128
BINS = 1024
SLOTS = 512
NCOEF = 8
NX, NZ, NY = 4, 4, 8
NXZ = NX * NZ
NBANDS = 512
NBLK = BINS // Q
EXT = NBLK + 2
SHARD = ("shard_0", "shard_1", "shard_2")
GROUP_SHARD = ("group_0", "group_1", "shard_0", "shard_1", "shard_2")
GROUP = ("group_0", "group_1")
MESH = pl.DeviceIdType.MESH
F32 = jnp.float32
BF16 = jnp.bfloat16

INV_TURN = 0.15915494309189535
TURN_HI = 6.28125
TURN_LO = 0.0019353071795864769
SIN_C = (4.44288283, -7.30824115, 3.60628896, -0.84576359, 0.10920575)
COS_C = (1.4142135, -6.97885099, 5.73946117, -1.88356298, 0.31069818)
COS6_C = (1.41421356, -6.97886411, 5.73988155, -1.888275, 0.33225188, -0.03450217)
SIN1_C = (3.14159258, -5.16770688, 2.55003138, -0.59804517, 0.0772201264)
COS1_C = (0.999999956, -4.93479286, 4.05841191, -1.33188016, 0.21969679)
SECTION = 36
ROT = 108
TILES = 3
FAR = (4, 3, 5, 2, 6, 1, 7, 0)
PLANE = ((2, 2), (2, 1), (1, 2), (2, 3), (3, 2), (1, 1), (1, 3), (3, 1), (3, 3),
         (0, 2), (2, 0), (0, 1), (0, 3), (1, 0), (3, 0), (0, 0))


def poly(coefs, square):
    total = coefs[-1] * square + coefs[-2]
    for c in coefs[-3::-1]:
        total = total * square + c
    return total


def nearest(t):
    return jnp.round(t)


def sin_cos_halves(f):
    square = f * f
    return f * poly(SIN_C, square), poly(COS_C, square)


def chebyshev_rows(x, index):
    terms = [jnp.ones_like(x), x]
    for _ in range(2, NCOEF):
        terms.append(2.0 * x * terms[-1] - terms[-2])
    out = jnp.zeros_like(x)
    for k in range(NCOEF):
        out = jnp.where(index == k, terms[k], out)
    return out


def wave_tile(amp, phase, slope, curve, start, live):
    low = jnp.bitwise_and(start, Q - 1)
    row = lax.broadcasted_iota(jnp.int32, (Q, SLOTS), 0)
    j = jnp.bitwise_and(row - low, Q - 1)
    block = lax.shift_right_logical(start, 7) + (row < low).astype(jnp.int32)
    jf = j.astype(F32)
    angle = phase + slope * jf + curve * jf * jf
    turns = nearest(angle * INV_TURN)
    rest = (angle - turns * TURN_HI) - turns * TURN_LO
    s, c = sin_cos_halves(rest * INV_TURN)
    y = (jf + (0.5 - Q / 2)) * (1.0 / Q)
    half = poly(COS6_C, y * y)
    size = jnp.where(live, amp, 0.0) * (half * half * 0.5)
    re = size * (1.0 - s * s)
    im = size * (s * c)
    return re.astype(BF16).astype(F32), im.astype(BF16).astype(F32), block


def own_template(tile, base, coef_rows):
    v = (lax.broadcasted_iota(jnp.int32, (8, Q), 1).astype(F32) + (NBLK - 1) * Q / 2) * (1.0 / BINS)
    re, im = [None] * NBLK, [None] * NBLK
    for h in range(HALF):
        ca = base + 3 * h
        cp = ca + coef_rows
        a0, a1, a2, p0, p1, p2, g2r, g2i = (
            jnp.broadcast_to(tile[:, k:k + 1], (8, Q))
            for k in (ca, ca + 1, ca + 2, cp, cp + 1, cp + 2, ROT + h, ROT + 8 + h)
        )
        g4r, g4i = 1.0 - 2.0 * (g2i * g2i), 2.0 * (g2i * g2r)
        g6r, g6i = g4r * g2r - g4i * g2i, g4i * g2r + g4r * g2i
        theta = p1 * 0.125 + v * (p2 * 0.25)
        whole = nearest(theta)
        f = theta - whole
        square = f * f
        yi, yr = f * poly(SIN1_C, square), poly(COS1_C, square)
        twice = 2.0 - 4.0 * (yi * yi)
        y_last = None
        center = (p0 + v * (p1 + v * p2)) + (p2 * (1.0 / 256) + 0.5 * whole)
        s, c = sin_cos_halves(center - nearest(center))
        xr, xi = 1.0 - s * s, s * c
        alpha = a0 + v * (a1 + v * a2)
        beta = a1 * 0.125 + v * (a2 * 0.25)
        curve = a2 * (1.0 / 64)
        for i in range(NBLK // 2):
            m = i + 0.5
            if i == 1:
                y_next = ((twice - 1.0) * yr, (twice + 1.0) * yi)
            elif i > 1:
                y_next = (twice * yr - y_last[0], twice * yi - y_last[1])
            if i > 0:
                y_last, (yr, yi) = (yr, yi), y_next
                rr, ri = ((g2r, g2i), (g4r, g4i), (g6r, g6i))[i - 1]
                xr, xi = xr * rr - xi * ri, xi * rr + xr * ri
            size, tilt = alpha + curve * (m * m), beta * m
            rr_, ii_, ri_, ir_ = xr * yr, xi * yi, xr * yi, xi * yr
            for block, amp, x_re, x_im in (
                (NBLK // 2 + i, size + tilt, rr_ - ii_, ir_ + ri_),
                (NBLK // 2 - 1 - i, size - tilt, rr_ + ii_, ir_ - ri_),
            ):
                if h == 0:
                    re[block], im[block] = amp * x_re, amp * x_im
                else:
                    re[block], im[block] = re[block] + amp * x_re, im[block] + amp * x_im
    return re, im


def wrapped(v, n):
    return jnp.where(v >= n, v - n, v)


def kernel(
    data_hbm, noise_hbm, amp_hbm, phase_hbm, bamp_hbm, bphase_hbm, bslope_hbm, bcurve_hbm,
    bstart_hbm, bcount,
    acc_out, res_out, fit_out,
    data_ref, noise_ref, bamp, bphase, bslope, bcurve, bstart,
    xm, m, s1, r1, a, ex, pk, fw, bk, bw, wt, wp, rim_power, self_ref, res, new_ref, ra, rb,
    zrow_ref,
    in_sem, p1_send, p1_recv, p2_send, p2_recv, ex_send, ex_recv, nb_send, nb_recv,
    ra_send, ra_recv, rb_send, rb_recv,
):
    coef_rows = 3 * HALF
    inputs = [
        (amp_hbm, xm.at[0:coef_rows]), (phase_hbm, xm.at[coef_rows:2 * coef_rows]),
        (data_hbm, data_ref), (noise_hbm, noise_ref), (bamp_hbm, bamp), (bphase_hbm, bphase),
        (bslope_hbm, bslope), (bcurve_hbm, bcurve), (bstart_hbm, bstart),
    ]
    fetches = [
        pltpu.make_async_copy(src, dst, in_sem.at[i]) for i, (src, dst) in enumerate(inputs)
    ]
    for fetch in fetches:
        fetch.start()

    zh, co = lax.axis_index("group_0"), lax.axis_index("group_1")
    x, z, y = lax.axis_index("shard_0"), lax.axis_index("shard_1"), lax.axis_index("shard_2")
    g = zh * 2 + co
    s = x * (NZ * NY) + z * NY + y
    n = g * (NBANDS // 4) + s
    xz = x * NZ + z
    ida = co * NY + y
    idb = zh * NXZ + xz
    has_prev, has_next = n > 0, n < NBANDS - 1
    first, last = s == 0, s == NBANDS // 4 - 1
    up = (y == 0) & (g < 3)
    down = (y == NY - 1) & (g > 0)

    def at(group0, group1, xi, zi, yi):
        return {
            "group_0": group0, "group_1": group1, "shard_0": xi, "shard_1": zi, "shard_2": yi,
        }

    turn_y = y == NY - 1
    turn_z = turn_y & (z == NZ - 1)
    turn_x = turn_z & (x == NX - 1)
    turn_c = turn_x & (co == 1)
    above_id = at(
        jnp.where(turn_c, 1 - zh, zh), jnp.where(turn_x, 1 - co, co),
        jnp.where(turn_z, wrapped(x + 1, NX), x), jnp.where(turn_y, wrapped(z + 1, NZ), z),
        wrapped(y + 1, NY),
    )
    back_y = y == 0
    back_z = back_y & (z == 0)
    back_x = back_z & (x == 0)
    back_c = back_x & (co == 0)
    below_id = at(
        jnp.where(back_c, 1 - zh, zh), jnp.where(back_x, 1 - co, co),
        jnp.where(back_z, wrapped(x + NX - 1, NX), x),
        jnp.where(back_y, wrapped(z + NZ - 1, NZ), z),
        wrapped(y + NY - 1, NY),
    )
    next_zh, next_co = jnp.where(co == 1, 1 - zh, zh), 1 - co
    prev_zh, prev_co = jnp.where(co == 0, 1 - zh, zh), 1 - co

    barrier = pltpu.get_barrier_semaphore()

    def greet(where):
        pl.semaphore_signal(barrier, inc=1, device_id=where, device_id_type=MESH)

    def peer_y(dc, dy):
        return {"group_1": 1 - co if dc else co, "shard_2": wrapped(y + dy, NY)}

    def peer_plane(dh, dx, dz):
        return {
            "group_0": 1 - zh if dh else zh,
            "shard_0": wrapped(x + dx, NX), "shard_1": wrapped(z + dz, NZ),
        }

    members_a = [(dc, dy) for dy in FAR for dc in (1, 0) if (dc, dy) != (0, 0)]
    members_b = [(dh, dx, dz) for dx, dz in PLANE for dh in (1, 0) if (dh, dx, dz) != (0, 0, 0)]

    @pl.when(first & (g > 0))
    def _():
        for k in range(NXZ):
            greet(at(prev_zh, prev_co, k // NZ, k % NZ, 0))

    @pl.when(last & (g < 3))
    def _():
        for k in range(NXZ):
            greet(at(next_zh, next_co, k // NZ, k % NZ, NY - 1))

    for dx, dz in PLANE[:-1]:
        greet(peer_plane(0, dx, dz))
    greet(peer_plane(1, 0, 0))
    for dy in FAR[:-1]:
        greet(peer_y(0, dy))
    greet(peer_y(1, 0))

    @pl.when(has_prev)
    def _():
        greet(below_id)

    @pl.when(has_next)
    def _():
        greet(above_id)

    for fetch in fetches:
        fetch.wait()
    amps, turns = xm[0:coef_rows, 0, :], xm[coef_rows:2 * coef_rows, 0, :] * INV_TURN
    bend = jnp.concatenate([turns[3 * h + 2:3 * h + 3, :] for h in range(HALF)], axis=0)
    bend = bend * (1.0 / 32)
    sn, cs = sin_cos_halves(bend - nearest(bend))
    xm[coef_rows:2 * coef_rows, 0, :] = turns
    own = xm[:, 0, :]
    message = [own, pltpu.roll(own, 1, 1), pltpu.roll(own, Q - 1, 1)]
    xm[0:HALF, 0, :] = 1.0 - sn * sn
    xm[8:8 + HALF, 0, :] = sn * cs
    xm[16:24, 0, :] = jnp.zeros((8, Q), F32)
    m[...] = jnp.concatenate([part[0:2 * coef_rows] for part in message] + [xm[0:Q - 6 * coef_rows, 0, :]], axis=0).T
    for k in range(NY):
        s1[k, :, 0, :] = m[pl.ds(k, NXZ, stride=NY), :]

    noise8 = noise_ref[...].astype(F32)
    noise = jnp.concatenate([noise8[b:b + 1, :] for b in range(NBLK)], axis=1)
    pk[...] = jnp.zeros_like(pk)
    pk[0:1, :] = bamp[...]
    pk[1:2, :] = bphase[...]
    pk[2:3, :] = bslope[...]
    pk[3:4, :] = bcurve[...]
    pk[4:5, :] = bstart[...].astype(F32)
    pk[5:6, :] = jnp.full((1, SLOTS), bcount[0], jnp.int32).astype(F32)
    pk[6:7, 0:Q] = data_ref[0:1, BINS - Q:]
    pk[6:7, Q:2 * Q] = data_ref[1:2, BINS - Q:]
    pk[6:7, 2 * Q:3 * Q] = noise8[NBLK - 1:NBLK, :]
    bk[...] = jnp.zeros_like(bk)
    bk[0:2, :] = data_ref[:, 0:Q]
    bk[2:3, :] = noise8[0:1, :]

    slot = lax.broadcasted_iota(jnp.int32, (1, SLOTS), 1)
    waits = NXZ + NY + has_prev.astype(jnp.int32) + has_next.astype(jnp.int32)
    pl.semaphore_wait(barrier, waits + up.astype(jnp.int32) + down.astype(jnp.int32))

    def remote(src, dst, send, recv, where):
        return pltpu.make_async_remote_copy(
            src_ref=src, dst_ref=dst, send_sem=send, recv_sem=recv, device_id=where,
            device_id_type=MESH,
        )

    slot_y = (y % 2) * (NY // 2) + y // 2

    def p1(dy):
        k = wrapped(y + dy, NY)
        return remote(
            s1.at[k], r1.at[slot_y], p1_send, p1_recv, {"shard_2": k}
        )

    for dy in FAR[:-1]:
        p1(dy).start()

    forward = remote(pk, fw, nb_send.at[0], nb_recv.at[0], above_id)
    backward = remote(bk, bw, nb_send.at[1], nb_recv.at[1], below_id)

    @pl.when(has_next)
    def _():
        forward.start()

    @pl.when(has_prev)
    def _():
        backward.start()

    r1[slot_y] = s1[y]

    @pl.when(n >= 0)
    def _():
        re_own, im_own, block_own = wave_tile(
            bamp[...], bphase[...], bslope[...], bcurve[...], bstart[...], slot < bcount[0]
        )
        noise_columns = jnp.concatenate([noise8, jnp.zeros((8, Q), F32)], axis=0).T
        total = jnp.zeros((Q, SLOTS), F32)
        for b in range(NBLK + 1):
            here = block_own == b
            wt[0, b * Q:(b + 1) * Q, :] = jnp.where(here, re_own, 0.0).astype(BF16)
            wt[1, b * Q:(b + 1) * Q, :] = jnp.where(here, im_own, 0.0).astype(BF16)
            if b < NBLK:
                total = jnp.where(here, noise_columns[:, b:b + 1], total)
        power = re_own * re_own + im_own * im_own
        rim_power[...] = jnp.where(block_own == NBLK, power, 0.0)
        self_ref[...] = jnp.sum(power * total, axis=0, keepdims=True)

    p1_all = remote(r1.at[0:NY - 1], r1.at[0:NY - 1], p1_send, p1_recv, {"shard_2": y})
    p1_all.wait_recv()

    up_copy = remote(
        r1.at[:, 0], ex.at[xz], ex_send.at[0], ex_recv, at(next_zh, next_co, 0, 0, 0)
    )
    down_copy = remote(
        r1.at[:, NXZ - 1], ex.at[xz], ex_send.at[1], ex_recv,
        at(prev_zh, prev_co, NX - 1, NZ - 1, NY - 1),
    )

    @pl.when(up)
    def _():
        up_copy.start()

    @pl.when(down)
    def _():
        down_copy.start()

    def p2(dx, dz):
        xk, zk = wrapped(x + dx, NX), wrapped(z + dz, NZ)
        return remote(
            r1.at[:, xk * NZ + zk], a.at[xz], p2_send, p2_recv.at[xz],
            {"shard_0": xk, "shard_1": zk},
        )

    for dx, dz in PLANE[-2::-1]:
        p2(dx, dz).start()
    a[xz] = r1[:, xz]

    @pl.when(has_prev)
    def _():
        forward.wait_recv()

    @pl.when(has_next)
    def _():
        backward.wait_recv()

    below = jnp.where(jnp.full((8, SLOTS), n, jnp.int32) > 0, fw[...], 0.0)
    above = jnp.where(jnp.full((8, Q), n, jnp.int32) < NBANDS - 1, bw[...], 0.0)
    re_prev, im_prev, block_prev = wave_tile(
        below[0:1], below[1:2], below[2:3], below[3:4], below[4:5].astype(jnp.int32),
        slot.astype(F32) < below[5:6],
    )
    for b in range(2):
        here = block_prev == NBLK - 1 + b
        wp[0, b * Q:(b + 1) * Q, :] = jnp.where(here, re_prev, 0.0).astype(BF16)
        wp[1, b * Q:(b + 1) * Q, :] = jnp.where(here, im_prev, 0.0).astype(BF16)

    rim_noise = jnp.concatenate(
        [below[6:7, 2 * Q:3 * Q], noise8[0:1, :], above[2:3, :], jnp.zeros((5, Q), F32)], axis=0
    ).T
    self_power = self_ref[...] + jnp.sum(rim_power[...] * rim_noise[:, 2:3], axis=0, keepdims=True)
    power_prev = re_prev * re_prev + im_prev * im_prev
    total_prev = jnp.where(
        block_prev == NBLK - 1, rim_noise[:, 0:1],
        jnp.where(block_prev == NBLK, rim_noise[:, 1:2], 0.0),
    )
    self_prev = jnp.sum(power_prev * total_prev, axis=0, keepdims=True)

    edge_first, edge_last = first & (g > 0), last & (g < 3)
    below_data = (below[6:7, 0:Q], below[6:7, Q:2 * Q])
    above_data = (above[0:1, :], above[1:2, :])
    z_end = jnp.where(z < 2, z, NZ - 1 - z)
    used = lax.broadcasted_iota(jnp.int32, (8, Q), 1) < jnp.full((8, Q), n + Q, jnp.int32)

    def arrived(turn):
        near, xi = turn // NX, turn % NX
        dx = jnp.where(xi >= 2, 5 - xi, xi)
        low = jnp.where((z_end == 1) & (near < 2), 1 - near, near)
        zk = jnp.where(z < 2, low, NZ - 1 - low)
        k = wrapped(x + dx, NX) * NZ + zk
        part = a.at[k]
        remote(part, part, p2_send, p2_recv.at[k], {"shard_2": y}).wait_recv()
        return k

    def edge_template(tile, section, offset):
        u = (lax.broadcasted_iota(jnp.int32, (8, Q), 1).astype(F32) + offset) * (1.0 / BINS)
        base = section * SECTION
        lost = amp_sum = im = None
        for h in range(HALF):
            ca = base + 3 * h
            cp = ca + coef_rows
            a0, a1, a2, p0, p1_, p2_ = (
                jnp.broadcast_to(tile[:, k:k + 1], (8, Q))
                for k in (ca, ca + 1, ca + 2, cp, cp + 1, cp + 2)
            )
            t = p0 + u * (p1_ + u * p2_)
            sn, cs = sin_cos_halves(t - nearest(t))
            amp = a0 + u * (a1 + u * a2)
            asn = amp * sn
            if h == 0:
                amp_sum, lost, im = amp, asn * sn, asn * cs
            else:
                amp_sum, lost, im = amp_sum + amp, lost + asn * sn, im + asn * cs
        return amp_sum - lost, im

    def put(k, block, parts, values):
        for part, half in enumerate(parts):
            half = half.astype(BF16).astype(F32)
            template = half + pltpu.roll(half, 4, 0)
            res[part, k, :, block * Q:(block + 1) * Q] = values[part] - template

    def template_rows(ks):
        for k in ks:
            tile = jnp.where(used, a[k, :, 0, :], 0.0)
            own_re, own_im = own_template(tile, 0, coef_rows)
            for block in range(NBLK):
                columns = slice(block * Q, (block + 1) * Q)
                put(
                    k, block + 1, (own_re[block], own_im[block]),
                    (data_ref[0:1, columns], data_ref[1:2, columns]),
                )
            put(k, 0, edge_template(tile, 1, BINS - Q), below_data)
            put(k, NBLK + 1, edge_template(tile, 2, 0), above_data)

    template_rows([xz])

    template_rows([arrived(jnp.int32(turn)) for turn in (1, 2)])

    @pl.loop(0, (NXZ - 4) // TILES)
    def _(step):
        template_rows([arrived(3 + step * TILES + i) for i in range(TILES)])

    template_rows([arrived(jnp.int32(NXZ - 1))])

    def other_group(section, offset, block, values):
        remote(ex, ex, ex_send.at[0], ex_recv, {"shard_2": y}).wait_recv()

        @pl.loop(0, NXZ // 8)
        def _(step):
            for i in range(8):
                k = step * 8 + i
                tile = jnp.where(used, ex[k, :, 0, :], 0.0)
                put(k, block, edge_template(tile, section, offset), values)

    @pl.when(edge_first)
    def _():
        other_group(1, BINS - Q, 0, below_data)

    @pl.when(edge_last)
    def _():
        other_group(2, 0, NBLK + 1, above_data)

    noise_ext = jnp.concatenate([below[6:7, 2 * Q:3 * Q], noise, above[2:3, :]], axis=1)
    corr = jnp.zeros((W, SLOTS), F32)
    corr_prev = jnp.zeros((W, SLOTS), F32)
    upper = lax.broadcasted_iota(jnp.int32, (NXZ // 2, 8, EXT * Q), 1) < 4

    def residual(part):
        pairs = res[part].reshape(NXZ // 2, 2, 8, EXT * Q)
        return jnp.where(upper, pairs[:, 0], pairs[:, 1]).reshape(W, EXT * Q)

    residuals = [residual(part) for part in range(2)]
    for part in range(2):
        weighted = (residuals[part] * noise_ext).astype(BF16)
        corr += jnp.dot(weighted[:, Q:], wt[part], preferred_element_type=F32)
        corr_prev += jnp.dot(weighted[:, 0:2 * Q], wp[part], preferred_element_type=F32)

    def sigmoid(v):
        return 1.0 / (1.0 + jnp.exp(-v))

    accept = jnp.where(slot < bcount[0], sigmoid(corr - 0.5 * self_power), 0.0)
    acc_out[...] = accept
    accept = accept.astype(BF16)
    accept_prev = sigmoid(corr_prev - 0.5 * self_prev).astype(BF16)
    square = jnp.zeros((1, BINS), F32)
    nt = (((1,), (1,)), ((), ()))
    for part in range(2):
        change = lax.dot_general(accept, wt[part, 0:BINS, :], nt, preferred_element_type=F32)
        rim = lax.dot_general(accept_prev, wp[part, Q:2 * Q, :], nt, preferred_element_type=F32)
        new = residuals[part][:, Q:Q + BINS] - change
        new = jnp.concatenate([new[:, 0:Q] - rim, new[:, Q:]], axis=1)
        new_ref[part] = new
        square += jnp.sum(new * new, axis=0, keepdims=True)
    mean = jnp.sum(square, axis=1, keepdims=True) * (1.0 / (2 * W * BINS))
    log_power = jnp.log(mean + 1e-06)
    lane = lax.broadcasted_iota(jnp.int32, (1, Q), 1)
    mine = chebyshev_rows((2 * jnp.full((1, Q), n, jnp.int32) + 1).astype(F32) / NBANDS - 1.0, lane)
    ra[ida] = mine * log_power

    def sum_a(dc, dy):
        return remote(ra.at[ida], ra.at[ida], ra_send, ra_recv, peer_y(dc, dy))

    def sum_b(dh, dx, dz):
        return remote(rb.at[idb], rb.at[idb], rb_send, rb_recv, peer_plane(dh, dx, dz))

    sum_a_all = remote(ra.at[0:15], ra.at[0:15], ra_send, ra_recv, {"shard_2": y})
    sum_b_all = remote(rb.at[0:31], rb.at[0:31], rb_send, rb_recv, {"shard_2": y})

    for member in members_a:
        sum_a(*member).start()

    @pl.when(n >= 0)
    def _():
        bands = lax.broadcasted_iota(jnp.int32, (NCOEF, NBANDS), 1)
        basis = chebyshev_rows(
            (2 * bands + 1).astype(F32) / NBANDS - 1.0,
            lax.broadcasted_iota(jnp.int32, (NCOEF, NBANDS), 0),
        )
        sub = lax.broadcasted_iota(jnp.int32, (NCOEF, Q), 0)
        lane8 = lax.broadcasted_iota(jnp.int32, (NCOEF, Q), 1)
        position = (2 * jnp.full((NCOEF, Q), n, jnp.int32) + 1).astype(F32) / NBANDS - 1.0
        table = jnp.where(lane8 == NCOEF, chebyshev_rows(position, sub), 0.0)
        for k in range(NCOEF):
            column = jnp.sum(basis * basis[k:k + 1, :], axis=1, keepdims=True)
            table = jnp.where(lane8 == k, column, table)
        rows = []
        for k in range(NCOEF):
            root = jnp.sqrt(table[k:k + 1, k:k + 1])
            row = table[k:k + 1, :] / root
            column = table[:, k:k + 1] / root
            rows.append(row)
            table = jnp.where(sub > k, table - column * row, table)
        zrow = jnp.zeros((1, Q), F32)
        for k in reversed(range(NCOEF)):
            row = rows[k]
            known = jnp.sum(jnp.where((lane > k) & (lane < NCOEF), row * zrow, 0.0), axis=1, keepdims=True)
            value = (row[:, NCOEF:NCOEF + 1] - known) / row[:, k:k + 1]
            zrow = jnp.where(lane == k, value, zrow)
        zrow_ref[...] = zrow
        for part in range(2):
            res_out[:, part, :] = new_ref[part]

    p1_all.wait_send()
    remote(
        a.at[0:NXZ - 1], a.at[0:NXZ - 1], p2_send, p2_recv.at[xz], {"shard_2": y}
    ).wait_send()

    @pl.when(has_next)
    def _():
        forward.wait_send()

    @pl.when(has_prev)
    def _():
        backward.wait_send()

    @pl.when(up)
    def _():
        up_copy.wait_send()

    @pl.when(down)
    def _():
        down_copy.wait_send()

    sum_a_all.wait_recv()
    rb[idb] = jnp.sum(ra[...], axis=0)
    for member in members_b:
        sum_b(*member).start()
    sum_a_all.wait_send()
    sum_b_all.wait_recv()
    moment = jnp.sum(rb[...], axis=0)
    fit = jnp.sum(zrow_ref[...] * moment, axis=1, keepdims=True)
    fit_out[...] = jnp.broadcast_to(fit, (1, Q))
    sum_b_all.wait_send()


def write_out(acc_ref, res_ref, fit_ref, acc_out, res_out, fit_out, fit_smem, sems):
    copies = [pltpu.make_async_copy(acc_ref, acc_out, sems.at[4])]
    for i in range(4):
        rows = pl.ds(i * (W // 4), W // 4)
        copies.append(pltpu.make_async_copy(res_ref.at[rows], res_out.at[rows], sems.at[i]))
    for copy in copies:
        copy.start()
    fit_smem[0] = fit_ref[0, 0]
    copies.append(pltpu.make_async_copy(fit_smem, fit_out, sems.at[5]))
    copies[-1].start()
    for copy in copies:
        copy.wait()


def local(data, inv_noise, mbh_amp, mbh_phase, bin_amp, bin_phase, bin_slope, bin_curve, bin_start, bin_count):
    vmem = pl.BlockSpec(memory_space=pltpu.VMEM)
    smem = pl.BlockSpec(memory_space=pltpu.SMEM)
    dma = pltpu.SemaphoreType.DMA
    rows = 3 * HALF
    accept, residual, fit = pl.pallas_call(
        kernel,
        out_shape=(
            jax.ShapeDtypeStruct((W, SLOTS), F32),
            jax.ShapeDtypeStruct((W, 2, BINS), F32),
            jax.ShapeDtypeStruct((1, Q), F32),
        ),
        in_specs=[pl.BlockSpec(memory_space=pltpu.HBM)] * 9 + [smem],
        out_specs=(vmem, vmem, vmem),
        scratch_shapes=[
            pltpu.VMEM((2, BINS), F32),
            pltpu.VMEM((NBLK, Q), BF16),
            pltpu.VMEM((1, SLOTS), F32),
            pltpu.VMEM((1, SLOTS), F32),
            pltpu.VMEM((1, SLOTS), F32),
            pltpu.VMEM((1, SLOTS), F32),
            pltpu.VMEM((1, SLOTS), jnp.int32),
            pltpu.VMEM((40, 1, Q), F32),
            pltpu.VMEM((Q, Q), F32),
            pltpu.VMEM((NY, NXZ, 1, Q), F32),
            pltpu.VMEM((NY, NXZ, 1, Q), F32),
            pltpu.VMEM((NXZ, NY, 1, Q), F32),
            pltpu.VMEM((NXZ, NY, 1, Q), F32),
            pltpu.VMEM((8, SLOTS), F32),
            pltpu.VMEM((8, SLOTS), F32),
            pltpu.VMEM((8, Q), F32),
            pltpu.VMEM((8, Q), F32),
            pltpu.VMEM((2, (NBLK + 1) * Q, SLOTS), BF16),
            pltpu.VMEM((2, 2 * Q, SLOTS), BF16),
            pltpu.VMEM((Q, SLOTS), F32),
            pltpu.VMEM((1, SLOTS), F32),
            pltpu.VMEM((2, NXZ, 8, EXT * Q), F32),
            pltpu.VMEM((2, W, BINS), F32),
            pltpu.VMEM((16, 1, Q), F32),
            pltpu.VMEM((32, 1, Q), F32),
            pltpu.VMEM((1, Q), F32),
            dma((9,)), dma, dma, dma, dma((NXZ,)), dma((2,)), dma, dma((2,)), dma((2,)),
            dma, dma, dma, dma,
        ],
        compiler_params=pltpu.CompilerParams(
            collective_id=0, has_side_effects=True, vmem_limit_bytes=48 * 1024 * 1024
        ),
        name="gibbs_round",
    )(
        *(
            pltpu.with_memory_space_constraint(v, pltpu.HBM)
            for v in (
                data,
                inv_noise.reshape(NBLK, Q),
                mbh_amp.transpose(1, 2, 0, 3).reshape(rows, 1, Q),
                mbh_phase.transpose(1, 2, 0, 3).reshape(rows, 1, Q),
                bin_amp, bin_phase, bin_slope, bin_curve, bin_start,
            )
        ),
        bin_count,
    )
    accept, residual, fit = pl.pallas_call(
        write_out,
        out_shape=(
            jax.ShapeDtypeStruct((W, SLOTS), F32),
            jax.ShapeDtypeStruct((W, 2, BINS), F32),
            jax.ShapeDtypeStruct((1,), F32),
        ),
        in_specs=[vmem] * 3,
        out_specs=(pl.BlockSpec(memory_space=pltpu.HBM),) * 3,
        scratch_shapes=[pltpu.SMEM((1,), F32), dma((6,))],
        name="write_out",
    )(
        pltpu.with_memory_space_constraint(accept, pltpu.VMEM),
        pltpu.with_memory_space_constraint(residual, pltpu.VMEM),
        pltpu.with_memory_space_constraint(fit, pltpu.VMEM),
    )
    return accept, residual, fit


def solution(mesh):
    split = Mesh(mesh.devices.reshape(2, 2, NX, NZ, NY), GROUP_SHARD)
    return jax.shard_map(
        local,
        mesh=split,
        in_specs=(
            P(None, GROUP_SHARD),
            P(GROUP_SHARD),
            P(SHARD, None, None, GROUP),
            P(SHARD, None, None, GROUP),
            P(GROUP_SHARD, None),
            P(GROUP_SHARD, None),
            P(GROUP_SHARD, None),
            P(GROUP_SHARD, None),
            P(GROUP_SHARD, None),
            P(GROUP_SHARD),
        ),
        out_specs=(P(None, GROUP_SHARD), P(None, None, GROUP_SHARD), P(GROUP_SHARD)),
        check_vma=False,
    )
```

```python
import jax
import jax.numpy as jnp
from jax import lax
from jax.experimental import pallas as pl
from jax.experimental.pallas import tpu as pltpu
from jax.sharding import Mesh
from jax.sharding import PartitionSpec as P

W = 64
HALF = 6
Q = 128
BINS = 1024
SLOTS = 512
NCOEF = 8
NX, NZ, NY = 4, 4, 8
NXZ = NX * NZ
NBANDS = 512
NBLK = BINS // Q
EXT = NBLK + 2
SHARD = ("shard_0", "shard_1", "shard_2")
GROUP_SHARD = ("group_0", "group_1", "shard_0", "shard_1", "shard_2")
GROUP = ("group_0", "group_1")
MESH = pl.DeviceIdType.MESH
F32 = jnp.float32
BF16 = jnp.bfloat16

INV_TURN = 0.15915494309189535
TURN_HI = 6.28125
TURN_LO = 0.0019353071795864769
SIN_C = (4.44288283, -7.30824115, 3.60628896, -0.84576359, 0.10920575)
COS_C = (1.4142135, -6.97885099, 5.73946117, -1.88356298, 0.31069818)
COS6_C = (1.41421356, -6.97886411, 5.73988155, -1.888275, 0.33225188, -0.03450217)
SIN1_C = (3.14159258, -5.16770688, 2.55003138, -0.59804517, 0.0772201264)
COS1_C = (0.999999956, -4.93479286, 4.05841191, -1.33188016, 0.21969679)
SECTION = 36
ROT = 108
TILES = 3
FAR = (4, 3, 5, 2, 6, 1, 7, 0)
PLANE = ((2, 2), (2, 1), (1, 2), (2, 3), (3, 2), (1, 1), (1, 3), (3, 1), (3, 3),
         (0, 2), (2, 0), (0, 1), (0, 3), (1, 0), (3, 0), (0, 0))


def poly(coefs, square):
    total = coefs[-1] * square + coefs[-2]
    for c in coefs[-3::-1]:
        total = total * square + c
    return total


def nearest(t):
    return jnp.round(t)


def sin_cos_halves(f):
    square = f * f
    return f * poly(SIN_C, square), poly(COS_C, square)


def chebyshev_rows(x, index):
    terms = [jnp.ones_like(x), x]
    for _ in range(2, NCOEF):
        terms.append(2.0 * x * terms[-1] - terms[-2])
    out = jnp.zeros_like(x)
    for k in range(NCOEF):
        out = jnp.where(index == k, terms[k], out)
    return out


def wave_tile(amp, phase, slope, curve, start, live):
    low = jnp.bitwise_and(start, Q - 1)
    row = lax.broadcasted_iota(jnp.int32, (Q, SLOTS), 0)
    j = jnp.bitwise_and(row - low, Q - 1)
    block = lax.shift_right_logical(start, 7) + (row < low).astype(jnp.int32)
    jf = j.astype(F32)
    angle = phase + slope * jf + curve * jf * jf
    turns = nearest(angle * INV_TURN)
    rest = (angle - turns * TURN_HI) - turns * TURN_LO
    s, c = sin_cos_halves(rest * INV_TURN)
    y = (jf + (0.5 - Q / 2)) * (1.0 / Q)
    half = poly(COS6_C, y * y)
    size = jnp.where(live, amp, 0.0) * (half * half * 0.5)
    re = size * (1.0 - s * s)
    im = size * (s * c)
    return re.astype(BF16).astype(F32), im.astype(BF16).astype(F32), block


def own_template(tile, base, coef_rows):
    v = (lax.broadcasted_iota(jnp.int32, (8, Q), 1).astype(F32) + (NBLK - 1) * Q / 2) * (1.0 / BINS)
    re, im = [None] * NBLK, [None] * NBLK
    for h in range(HALF):
        ca = base + 3 * h
        cp = ca + coef_rows
        a0, a1, a2, p0, p1, p2, g2r, g2i = (
            jnp.broadcast_to(tile[:, k:k + 1], (8, Q))
            for k in (ca, ca + 1, ca + 2, cp, cp + 1, cp + 2, ROT + h, ROT + 8 + h)
        )
        g4r, g4i = 1.0 - 2.0 * (g2i * g2i), 2.0 * (g2i * g2r)
        g6r, g6i = g4r * g2r - g4i * g2i, g4i * g2r + g4r * g2i
        theta = p1 * 0.125 + v * (p2 * 0.25)
        whole = nearest(theta)
        f = theta - whole
        square = f * f
        yi, yr = f * poly(SIN1_C, square), poly(COS1_C, square)
        twice = 2.0 - 4.0 * (yi * yi)
        y_last = None
        center = (p0 + v * (p1 + v * p2)) + (p2 * (1.0 / 256) + 0.5 * whole)
        s, c = sin_cos_halves(center - nearest(center))
        xr, xi = 1.0 - s * s, s * c
        alpha = a0 + v * (a1 + v * a2)
        beta = a1 * 0.125 + v * (a2 * 0.25)
        curve = a2 * (1.0 / 64)
        for i in range(NBLK // 2):
            m = i + 0.5
            if i == 1:
                y_next = ((twice - 1.0) * yr, (twice + 1.0) * yi)
            elif i > 1:
                y_next = (twice * yr - y_last[0], twice * yi - y_last[1])
            if i > 0:
                y_last, (yr, yi) = (yr, yi), y_next
                rr, ri = ((g2r, g2i), (g4r, g4i), (g6r, g6i))[i - 1]
                xr, xi = xr * rr - xi * ri, xi * rr + xr * ri
            size, tilt = alpha + curve * (m * m), beta * m
            rr_, ii_, ri_, ir_ = xr * yr, xi * yi, xr * yi, xi * yr
            for block, amp, x_re, x_im in (
                (NBLK // 2 + i, size + tilt, rr_ - ii_, ir_ + ri_),
                (NBLK // 2 - 1 - i, size - tilt, rr_ + ii_, ir_ - ri_),
            ):
                if h == 0:
                    re[block], im[block] = amp * x_re, amp * x_im
                else:
                    re[block], im[block] = re[block] + amp * x_re, im[block] + amp * x_im
    return re, im


def wrapped(v, n):
    return jnp.where(v >= n, v - n, v)


def kernel(
    data_hbm, noise_hbm, amp_hbm, phase_hbm, bamp_hbm, bphase_hbm, bslope_hbm, bcurve_hbm,
    bstart_hbm, bcount,
    acc_out, res_out, fit_out,
    data_ref, noise_ref, bamp, bphase, bslope, bcurve, bstart,
    xm, m, s1, r1, a, ex, pk, fw, bk, bw, wt, wp, rim_power, self_ref, res, new_ref, ra, rb,
    zrow_ref,
    in_sem, p1_send, p1_recv, p2_send, p2_recv, ex_send, ex_recv, nb_send, nb_recv,
    ra_send, ra_recv, rb_send, rb_recv,
):
    coef_rows = 3 * HALF
    inputs = [
        (amp_hbm, xm.at[0:coef_rows]), (phase_hbm, xm.at[coef_rows:2 * coef_rows]),
        (data_hbm, data_ref), (noise_hbm, noise_ref), (bamp_hbm, bamp), (bphase_hbm, bphase),
        (bslope_hbm, bslope), (bcurve_hbm, bcurve), (bstart_hbm, bstart),
    ]
    fetches = [
        pltpu.make_async_copy(src, dst, in_sem.at[i]) for i, (src, dst) in enumerate(inputs)
    ]
    for fetch in fetches:
        fetch.start()

    zh, co = lax.axis_index("group_0"), lax.axis_index("group_1")
    x, z, y = lax.axis_index("shard_0"), lax.axis_index("shard_1"), lax.axis_index("shard_2")
    g = zh * 2 + co
    s = x * (NZ * NY) + z * NY + y
    n = g * (NBANDS // 4) + s
    xz = x * NZ + z
    ida = co * NY + y
    idb = zh * NXZ + xz
    has_prev, has_next = n > 0, n < NBANDS - 1
    first, last = s == 0, s == NBANDS // 4 - 1
    up = (y == 0) & (g < 3)
    down = (y == NY - 1) & (g > 0)

    def at(group0, group1, xi, zi, yi):
        return {
            "group_0": group0, "group_1": group1, "shard_0": xi, "shard_1": zi, "shard_2": yi,
        }

    turn_y = y == NY - 1
    turn_z = turn_y & (z == NZ - 1)
    turn_x = turn_z & (x == NX - 1)
    turn_c = turn_x & (co == 1)
    above_id = at(
        jnp.where(turn_c, 1 - zh, zh), jnp.where(turn_x, 1 - co, co),
        jnp.where(turn_z, wrapped(x + 1, NX), x), jnp.where(turn_y, wrapped(z + 1, NZ), z),
        wrapped(y + 1, NY),
    )
    back_y = y == 0
    back_z = back_y & (z == 0)
    back_x = back_z & (x == 0)
    back_c = back_x & (co == 0)
    below_id = at(
        jnp.where(back_c, 1 - zh, zh), jnp.where(back_x, 1 - co, co),
        jnp.where(back_z, wrapped(x + NX - 1, NX), x),
        jnp.where(back_y, wrapped(z + NZ - 1, NZ), z),
        wrapped(y + NY - 1, NY),
    )
    next_zh, next_co = jnp.where(co == 1, 1 - zh, zh), 1 - co
    prev_zh, prev_co = jnp.where(co == 0, 1 - zh, zh), 1 - co

    barrier = pltpu.get_barrier_semaphore()

    def greet(where):
        pl.semaphore_signal(barrier, inc=1, device_id=where, device_id_type=MESH)

    def peer_y(dc, dy):
        return {"group_1": 1 - co if dc else co, "shard_2": wrapped(y + dy, NY)}

    def peer_plane(dh, dx, dz):
        return {
            "group_0": 1 - zh if dh else zh,
            "shard_0": wrapped(x + dx, NX), "shard_1": wrapped(z + dz, NZ),
        }

    members_a = [(dc, dy) for dy in FAR for dc in (1, 0) if (dc, dy) != (0, 0)]
    members_b = [(dh, dx, dz) for dx, dz in PLANE for dh in (1, 0) if (dh, dx, dz) != (0, 0, 0)]

    @pl.when(first & (g > 0))
    def _():
        for k in range(NXZ):
            greet(at(prev_zh, prev_co, k // NZ, k % NZ, 0))

    @pl.when(last & (g < 3))
    def _():
        for k in range(NXZ):
            greet(at(next_zh, next_co, k // NZ, k % NZ, NY - 1))

    for dx, dz in PLANE[:-1]:
        greet(peer_plane(0, dx, dz))
    greet(peer_plane(1, 0, 0))
    for dy in FAR[:-1]:
        greet(peer_y(0, dy))
    greet(peer_y(1, 0))

    @pl.when(has_prev)
    def _():
        greet(below_id)

    @pl.when(has_next)
    def _():
        greet(above_id)

    for fetch in fetches:
        fetch.wait()
    amps, turns = xm[0:coef_rows, 0, :], xm[coef_rows:2 * coef_rows, 0, :] * INV_TURN
    bend = jnp.concatenate([turns[3 * h + 2:3 * h + 3, :] for h in range(HALF)], axis=0)
    bend = bend * (1.0 / 32)
    sn, cs = sin_cos_halves(bend - nearest(bend))
    xm[coef_rows:2 * coef_rows, 0, :] = turns
    own = xm[:, 0, :]
    message = [own, pltpu.roll(own, 1, 1), pltpu.roll(own, Q - 1, 1)]
    xm[0:HALF, 0, :] = 1.0 - sn * sn
    xm[8:8 + HALF, 0, :] = sn * cs
    xm[16:24, 0, :] = jnp.zeros((8, Q), F32)
    m[...] = jnp.concatenate([part[0:2 * coef_rows] for part in message] + [xm[0:Q - 6 * coef_rows, 0, :]], axis=0).T
    for k in range(NY):
        s1[k, :, 0, :] = m[pl.ds(k, NXZ, stride=NY), :]

    noise8 = noise_ref[...].astype(F32)
    noise = jnp.concatenate([noise8[b:b + 1, :] for b in range(NBLK)], axis=1)
    pk[...] = jnp.zeros_like(pk)
    pk[0:1, :] = bamp[...]
    pk[1:2, :] = bphase[...]
    pk[2:3, :] = bslope[...]
    pk[3:4, :] = bcurve[...]
    pk[4:5, :] = bstart[...].astype(F32)
    pk[5:6, :] = jnp.full((1, SLOTS), bcount[0], jnp.int32).astype(F32)
    pk[6:7, 0:Q] = data_ref[0:1, BINS - Q:]
    pk[6:7, Q:2 * Q] = data_ref[1:2, BINS - Q:]
    pk[6:7, 2 * Q:3 * Q] = noise8[NBLK - 1:NBLK, :]
    bk[...] = jnp.zeros_like(bk)
    bk[0:2, :] = data_ref[:, 0:Q]
    bk[2:3, :] = noise8[0:1, :]

    slot = lax.broadcasted_iota(jnp.int32, (1, SLOTS), 1)
    waits = NXZ + NY + has_prev.astype(jnp.int32) + has_next.astype(jnp.int32)
    pl.semaphore_wait(barrier, waits + up.astype(jnp.int32) + down.astype(jnp.int32))

    def remote(src, dst, send, recv, where):
        return pltpu.make_async_remote_copy(
            src_ref=src, dst_ref=dst, send_sem=send, recv_sem=recv, device_id=where,
            device_id_type=MESH,
        )

    slot_y = (y % 2) * (NY // 2) + y // 2

    def p1(dy):
        k = wrapped(y + dy, NY)
        return remote(
            s1.at[k], r1.at[slot_y], p1_send, p1_recv, {"shard_2": k}
        )

    for dy in FAR[:-1]:
        p1(dy).start()

    forward = remote(pk, fw, nb_send.at[0], nb_recv.at[0], above_id)
    backward = remote(bk, bw, nb_send.at[1], nb_recv.at[1], below_id)

    @pl.when(has_next)
    def _():
        forward.start()

    @pl.when(has_prev)
    def _():
        backward.start()

    r1[slot_y] = s1[y]

    @pl.when(n >= 0)
    def _():
        re_own, im_own, block_own = wave_tile(
            bamp[...], bphase[...], bslope[...], bcurve[...], bstart[...], slot < bcount[0]
        )
        noise_columns = jnp.concatenate([noise8, jnp.zeros((8, Q), F32)], axis=0).T
        total = jnp.zeros((Q, SLOTS), F32)
        for b in range(NBLK + 1):
            here = block_own == b
            wt[0, b * Q:(b + 1) * Q, :] = jnp.where(here, re_own, 0.0).astype(BF16)
            wt[1, b * Q:(b + 1) * Q, :] = jnp.where(here, im_own, 0.0).astype(BF16)
            if b < NBLK:
                total = jnp.where(here, noise_columns[:, b:b + 1], total)
        power = re_own * re_own + im_own * im_own
        rim_power[...] = jnp.where(block_own == NBLK, power, 0.0)
        self_ref[...] = jnp.sum(power * total, axis=0, keepdims=True)

    p1_all = remote(r1.at[0:NY - 1], r1.at[0:NY - 1], p1_send, p1_recv, {"shard_2": y})
    p1_all.wait_recv()

    up_copy = remote(
        r1.at[:, 0], ex.at[xz], ex_send.at[0], ex_recv, at(next_zh, next_co, 0, 0, 0)
    )
    down_copy = remote(
        r1.at[:, NXZ - 1], ex.at[xz], ex_send.at[1], ex_recv,
        at(prev_zh, prev_co, NX - 1, NZ - 1, NY - 1),
    )

    @pl.when(up)
    def _():
        up_copy.start()

    @pl.when(down)
    def _():
        down_copy.start()

    def p2(dx, dz):
        xk, zk = wrapped(x + dx, NX), wrapped(z + dz, NZ)
        return remote(
            r1.at[:, xk * NZ + zk], a.at[xz], p2_send, p2_recv.at[xz],
            {"shard_0": xk, "shard_1": zk},
        )

    for dx, dz in PLANE[-2::-1]:
        p2(dx, dz).start()
    a[xz] = r1[:, xz]

    @pl.when(has_prev)
    def _():
        forward.wait_recv()

    @pl.when(has_next)
    def _():
        backward.wait_recv()

    below = jnp.where(jnp.full((8, SLOTS), n, jnp.int32) > 0, fw[...], 0.0)
    above = jnp.where(jnp.full((8, Q), n, jnp.int32) < NBANDS - 1, bw[...], 0.0)
    re_prev, im_prev, block_prev = wave_tile(
        below[0:1], below[1:2], below[2:3], below[3:4], below[4:5].astype(jnp.int32),
        slot.astype(F32) < below[5:6],
    )
    for b in range(2):
        here = block_prev == NBLK - 1 + b
        wp[0, b * Q:(b + 1) * Q, :] = jnp.where(here, re_prev, 0.0).astype(BF16)
        wp[1, b * Q:(b + 1) * Q, :] = jnp.where(here, im_prev, 0.0).astype(BF16)

    rim_noise = jnp.concatenate(
        [below[6:7, 2 * Q:3 * Q], noise8[0:1, :], above[2:3, :], jnp.zeros((5, Q), F32)], axis=0
    ).T
    self_power = self_ref[...] + jnp.sum(rim_power[...] * rim_noise[:, 2:3], axis=0, keepdims=True)
    power_prev = re_prev * re_prev + im_prev * im_prev
    total_prev = jnp.where(
        block_prev == NBLK - 1, rim_noise[:, 0:1],
        jnp.where(block_prev == NBLK, rim_noise[:, 1:2], 0.0),
    )
    self_prev = jnp.sum(power_prev * total_prev, axis=0, keepdims=True)

    edge_first, edge_last = first & (g > 0), last & (g < 3)
    below_data = (below[6:7, 0:Q], below[6:7, Q:2 * Q])
    above_data = (above[0:1, :], above[1:2, :])
    z_end = jnp.where(z < 2, z, NZ - 1 - z)
    used = lax.broadcasted_iota(jnp.int32, (8, Q), 1) < jnp.full((8, Q), n + Q, jnp.int32)

    def arrived(turn):
        near, xi = turn // NX, turn % NX
        dx = jnp.where(xi >= 2, 5 - xi, xi)
        low = jnp.where((z_end == 1) & (near < 2), 1 - near, near)
        zk = jnp.where(z < 2, low, NZ - 1 - low)
        k = wrapped(x + dx, NX) * NZ + zk
        part = a.at[k]
        remote(part, part, p2_send, p2_recv.at[k], {"shard_2": y}).wait_recv()
        return k

    def edge_template(tile, section, offset):
        u = (lax.broadcasted_iota(jnp.int32, (8, Q), 1).astype(F32) + offset) * (1.0 / BINS)
        base = section * SECTION
        lost = amp_sum = im = None
        for h in range(HALF):
            ca = base + 3 * h
            cp = ca + coef_rows
            a0, a1, a2, p0, p1_, p2_ = (
                jnp.broadcast_to(tile[:, k:k + 1], (8, Q))
                for k in (ca, ca + 1, ca + 2, cp, cp + 1, cp + 2)
            )
            t = p0 + u * (p1_ + u * p2_)
            sn, cs = sin_cos_halves(t - nearest(t))
            amp = a0 + u * (a1 + u * a2)
            asn = amp * sn
            if h == 0:
                amp_sum, lost, im = amp, asn * sn, asn * cs
            else:
                amp_sum, lost, im = amp_sum + amp, lost + asn * sn, im + asn * cs
        return amp_sum - lost, im

    def put(k, block, parts, values):
        for part, half in enumerate(parts):
            half = half.astype(BF16).astype(F32)
            template = half + pltpu.roll(half, 4, 0)
            res[part, k, :, block * Q:(block + 1) * Q] = values[part] - template

    def template_rows(ks):
        for k in ks:
            tile = jnp.where(used, a[k, :, 0, :], 0.0)
            own_re, own_im = own_template(tile, 0, coef_rows)
            for block in range(NBLK):
                columns = slice(block * Q, (block + 1) * Q)
                put(
                    k, block + 1, (own_re[block], own_im[block]),
                    (data_ref[0:1, columns], data_ref[1:2, columns]),
                )
            put(k, 0, edge_template(tile, 1, BINS - Q), below_data)
            put(k, NBLK + 1, edge_template(tile, 2, 0), above_data)

    template_rows([xz])

    template_rows([arrived(jnp.int32(turn)) for turn in (1, 2)])

    @pl.loop(0, (NXZ - 4) // TILES)
    def _(step):
        template_rows([arrived(3 + step * TILES + i) for i in range(TILES)])

    template_rows([arrived(jnp.int32(NXZ - 1))])

    def other_group(section, offset, block, values):
        remote(ex, ex, ex_send.at[0], ex_recv, {"shard_2": y}).wait_recv()

        for k in range(NXZ):
            tile = jnp.where(used, ex[k, :, 0, :], 0.0)
            put(k, block, edge_template(tile, section, offset), values)

    @pl.when(edge_first)
    def _():
        other_group(1, BINS - Q, 0, below_data)

    @pl.when(edge_last)
    def _():
        other_group(2, 0, NBLK + 1, above_data)

    noise_ext = jnp.concatenate([below[6:7, 2 * Q:3 * Q], noise, above[2:3, :]], axis=1)
    corr = jnp.zeros((W, SLOTS), F32)
    corr_prev = jnp.zeros((W, SLOTS), F32)
    upper = lax.broadcasted_iota(jnp.int32, (NXZ // 2, 8, EXT * Q), 1) < 4

    def residual(part):
        pairs = res[part].reshape(NXZ // 2, 2, 8, EXT * Q)
        return jnp.where(upper, pairs[:, 0], pairs[:, 1]).reshape(W, EXT * Q)

    residuals = [residual(part) for part in range(2)]
    for part in range(2):
        weighted = (residuals[part] * noise_ext).astype(BF16)
        corr += jnp.dot(weighted[:, Q:], wt[part], preferred_element_type=F32)
        corr_prev += jnp.dot(weighted[:, 0:2 * Q], wp[part], preferred_element_type=F32)

    def sigmoid(v):
        return 1.0 / (1.0 + jnp.exp(-v))

    accept = jnp.where(slot < bcount[0], sigmoid(corr - 0.5 * self_power), 0.0)
    acc_out[...] = accept
    accept = accept.astype(BF16)
    accept_prev = sigmoid(corr_prev - 0.5 * self_prev).astype(BF16)
    square = jnp.zeros((1, BINS), F32)
    nt = (((1,), (1,)), ((), ()))
    for part in range(2):
        change = lax.dot_general(accept, wt[part, 0:BINS, :], nt, preferred_element_type=F32)
        rim = lax.dot_general(accept_prev, wp[part, Q:2 * Q, :], nt, preferred_element_type=F32)
        new = residuals[part][:, Q:Q + BINS] - change
        new = jnp.concatenate([new[:, 0:Q] - rim, new[:, Q:]], axis=1)
        new_ref[part] = new
        square += jnp.sum(new * new, axis=0, keepdims=True)
    mean = jnp.sum(square, axis=1, keepdims=True) * (1.0 / (2 * W * BINS))
    log_power = jnp.log(mean + 1e-06)
    lane = lax.broadcasted_iota(jnp.int32, (1, Q), 1)
    mine = chebyshev_rows((2 * jnp.full((1, Q), n, jnp.int32) + 1).astype(F32) / NBANDS - 1.0, lane)
    ra[ida] = mine * log_power

    def sum_a(dc, dy):
        return remote(ra.at[ida], ra.at[ida], ra_send, ra_recv, peer_y(dc, dy))

    def sum_b(dh, dx, dz):
        return remote(rb.at[idb], rb.at[idb], rb_send, rb_recv, peer_plane(dh, dx, dz))

    sum_a_all = remote(ra.at[0:15], ra.at[0:15], ra_send, ra_recv, {"shard_2": y})
    sum_b_all = remote(rb.at[0:31], rb.at[0:31], rb_send, rb_recv, {"shard_2": y})

    for member in members_a:
        sum_a(*member).start()

    @pl.when(n >= 0)
    def _():
        bands = lax.broadcasted_iota(jnp.int32, (NCOEF, NBANDS), 1)
        basis = chebyshev_rows(
            (2 * bands + 1).astype(F32) / NBANDS - 1.0,
            lax.broadcasted_iota(jnp.int32, (NCOEF, NBANDS), 0),
        )
        sub = lax.broadcasted_iota(jnp.int32, (NCOEF, Q), 0)
        lane8 = lax.broadcasted_iota(jnp.int32, (NCOEF, Q), 1)
        position = (2 * jnp.full((NCOEF, Q), n, jnp.int32) + 1).astype(F32) / NBANDS - 1.0
        table = jnp.where(lane8 == NCOEF, chebyshev_rows(position, sub), 0.0)
        for k in range(NCOEF):
            column = jnp.sum(basis * basis[k:k + 1, :], axis=1, keepdims=True)
            table = jnp.where(lane8 == k, column, table)
        rows = []
        for k in range(NCOEF):
            root = jnp.sqrt(table[k:k + 1, k:k + 1])
            row = table[k:k + 1, :] / root
            column = table[:, k:k + 1] / root
            rows.append(row)
            table = jnp.where(sub > k, table - column * row, table)
        zrow = jnp.zeros((1, Q), F32)
        for k in reversed(range(NCOEF)):
            row = rows[k]
            known = jnp.sum(jnp.where((lane > k) & (lane < NCOEF), row * zrow, 0.0), axis=1, keepdims=True)
            value = (row[:, NCOEF:NCOEF + 1] - known) / row[:, k:k + 1]
            zrow = jnp.where(lane == k, value, zrow)
        zrow_ref[...] = zrow
        for part in range(2):
            res_out[:, part, :] = new_ref[part]

    p1_all.wait_send()
    remote(
        a.at[0:NXZ - 1], a.at[0:NXZ - 1], p2_send, p2_recv.at[xz], {"shard_2": y}
    ).wait_send()

    @pl.when(has_next)
    def _():
        forward.wait_send()

    @pl.when(has_prev)
    def _():
        backward.wait_send()

    @pl.when(up)
    def _():
        up_copy.wait_send()

    @pl.when(down)
    def _():
        down_copy.wait_send()

    sum_a_all.wait_recv()
    rb[idb] = jnp.sum(ra[...], axis=0)
    for member in members_b:
        sum_b(*member).start()
    sum_a_all.wait_send()
    sum_b_all.wait_recv()
    moment = jnp.sum(rb[...], axis=0)
    fit = jnp.sum(zrow_ref[...] * moment, axis=1, keepdims=True)
    fit_out[...] = jnp.broadcast_to(fit, (1, Q))
    sum_b_all.wait_send()


def write_out(acc_ref, res_ref, fit_ref, acc_out, res_out, fit_out, fit_smem, sems):
    copies = [pltpu.make_async_copy(acc_ref, acc_out, sems.at[4])]
    for i in range(4):
        rows = pl.ds(i * (W // 4), W // 4)
        copies.append(pltpu.make_async_copy(res_ref.at[rows], res_out.at[rows], sems.at[i]))
    for copy in copies:
        copy.start()
    fit_smem[0] = fit_ref[0, 0]
    copies.append(pltpu.make_async_copy(fit_smem, fit_out, sems.at[5]))
    copies[-1].start()
    for copy in copies:
        copy.wait()


def local(data, inv_noise, mbh_amp, mbh_phase, bin_amp, bin_phase, bin_slope, bin_curve, bin_start, bin_count):
    vmem = pl.BlockSpec(memory_space=pltpu.VMEM)
    smem = pl.BlockSpec(memory_space=pltpu.SMEM)
    dma = pltpu.SemaphoreType.DMA
    rows = 3 * HALF
    accept, residual, fit = pl.pallas_call(
        kernel,
        out_shape=(
            jax.ShapeDtypeStruct((W, SLOTS), F32),
            jax.ShapeDtypeStruct((W, 2, BINS), F32),
            jax.ShapeDtypeStruct((1, Q), F32),
        ),
        in_specs=[pl.BlockSpec(memory_space=pltpu.HBM)] * 9 + [smem],
        out_specs=(vmem, vmem, vmem),
        scratch_shapes=[
            pltpu.VMEM((2, BINS), F32),
            pltpu.VMEM((NBLK, Q), BF16),
            pltpu.VMEM((1, SLOTS), F32),
            pltpu.VMEM((1, SLOTS), F32),
            pltpu.VMEM((1, SLOTS), F32),
            pltpu.VMEM((1, SLOTS), F32),
            pltpu.VMEM((1, SLOTS), jnp.int32),
            pltpu.VMEM((40, 1, Q), F32),
            pltpu.VMEM((Q, Q), F32),
            pltpu.VMEM((NY, NXZ, 1, Q), F32),
            pltpu.VMEM((NY, NXZ, 1, Q), F32),
            pltpu.VMEM((NXZ, NY, 1, Q), F32),
            pltpu.VMEM((NXZ, NY, 1, Q), F32),
            pltpu.VMEM((8, SLOTS), F32),
            pltpu.VMEM((8, SLOTS), F32),
            pltpu.VMEM((8, Q), F32),
            pltpu.VMEM((8, Q), F32),
            pltpu.VMEM((2, (NBLK + 1) * Q, SLOTS), BF16),
            pltpu.VMEM((2, 2 * Q, SLOTS), BF16),
            pltpu.VMEM((Q, SLOTS), F32),
            pltpu.VMEM((1, SLOTS), F32),
            pltpu.VMEM((2, NXZ, 8, EXT * Q), F32),
            pltpu.VMEM((2, W, BINS), F32),
            pltpu.VMEM((16, 1, Q), F32),
            pltpu.VMEM((32, 1, Q), F32),
            pltpu.VMEM((1, Q), F32),
            dma((9,)), dma, dma, dma, dma((NXZ,)), dma((2,)), dma, dma((2,)), dma((2,)),
            dma, dma, dma, dma,
        ],
        compiler_params=pltpu.CompilerParams(
            collective_id=0, has_side_effects=True, vmem_limit_bytes=48 * 1024 * 1024
        ),
        name="gibbs_round",
    )(
        *(
            pltpu.with_memory_space_constraint(v, pltpu.HBM)
            for v in (
                data,
                inv_noise.reshape(NBLK, Q),
                mbh_amp.transpose(1, 2, 0, 3).reshape(rows, 1, Q),
                mbh_phase.transpose(1, 2, 0, 3).reshape(rows, 1, Q),
                bin_amp, bin_phase, bin_slope, bin_curve, bin_start,
            )
        ),
        bin_count,
    )
    accept, residual, fit = pl.pallas_call(
        write_out,
        out_shape=(
            jax.ShapeDtypeStruct((W, SLOTS), F32),
            jax.ShapeDtypeStruct((W, 2, BINS), F32),
            jax.ShapeDtypeStruct((1,), F32),
        ),
        in_specs=[vmem] * 3,
        out_specs=(pl.BlockSpec(memory_space=pltpu.HBM),) * 3,
        scratch_shapes=[pltpu.SMEM((1,), F32), dma((6,))],
        name="write_out",
    )(
        pltpu.with_memory_space_constraint(accept, pltpu.VMEM),
        pltpu.with_memory_space_constraint(residual, pltpu.VMEM),
        pltpu.with_memory_space_constraint(fit, pltpu.VMEM),
    )
    return accept, residual, fit


def solution(mesh):
    split = Mesh(mesh.devices.reshape(2, 2, NX, NZ, NY), GROUP_SHARD)
    return jax.shard_map(
        local,
        mesh=split,
        in_specs=(
            P(None, GROUP_SHARD),
            P(GROUP_SHARD),
            P(SHARD, None, None, GROUP),
            P(SHARD, None, None, GROUP),
            P(GROUP_SHARD, None),
            P(GROUP_SHARD, None),
            P(GROUP_SHARD, None),
            P(GROUP_SHARD, None),
            P(GROUP_SHARD, None),
            P(GROUP_SHARD),
        ),
        out_specs=(P(None, GROUP_SHARD), P(None, None, GROUP_SHARD), P(GROUP_SHARD)),
        check_vma=False,
    )
```
